32 devices in a mesh: tm: 8 (over z, y), sta: 4 (over x, core).
Axes of the slice: x: 2, y: 2, z: 4, core: 2. Of those that a mesh axis runs over, the one named last changes fastest.
Arguments:
- traces: bfloat16 [8, 270336], P('sta', 'tm'), may hold values from -64 to 64
- station_flags: int32 [8], P('sta'), may hold values 0 or 1
- tile_mask: int32 [4, 4], replicated, may hold values 0 or 1
- band_block: int32 [1], replicated, may hold values from 1 to 137
- stacks: float32 [8, 8, 2, 3072], P('sta', None, None, 'tm'), may hold values from -6 to 6
Outputs:
- stacked: float32 [8, 8, 2, 3072], P('sta', None, None, 'tm')
The draws below stay inside these ranges and needn't reach their ends.
All inputs are finite; a program needn't handle non-finite values. No bound on the sum of `station_flags` on one device may be relied on, other than what follows from the above.
Results may differ from the reference program's by a relative error of at most 0.0003.
Values may be sent and summed in bfloat16 or wider, within the bound.
No kernel may reach another device: no remote copies, remote signals or barrier semaphores. Data moves between devices by JAX's collectives and lax.ppermute only.
A program may use at most 128 MiB of HBM per device.

```python
import math
import jax
import jax.numpy as jnp
from jax import lax

STA_DEV = 2
TIME_DEV = 33792
BINS_DEV = 384
HALF_WIN = 512
SMOOTH = 32
STATIONS = 8
BLOCKS = 4
SAMPLES = 270336
BINS = 3072
N_TM = 8


def draw_traces(key, part):
    noise_key, level_key = jax.random.split(key, 2)
    segment = 64
    noise_part = jax.random.normal(noise_key, (STATIONS, SAMPLES), jnp.float32)
    levels = jax.random.uniform(level_key, (STATIONS, SAMPLES // segment), jnp.float32, math.log(0.1), math.log(10.0))
    envelope = jnp.repeat(jnp.exp(levels), segment, axis=1)
    return jnp.clip(noise_part * envelope, -64.0, 64.0).astype(jnp.bfloat16)


def set_ends(result, stream_key, least, high):
    place = [jax.random.randint(jax.random.fold_in(stream_key, axis), (), 0, length) for axis, length in enumerate(result.shape)]
    widest = result.shape.index(max(result.shape))
    beside = place[:widest] + [(place[widest] + 1) % result.shape[widest]] + place[widest + 1:]
    return result.at[tuple(place)].set(least).at[tuple(beside)].set(high)


def shard_levels(stream_key, dims, cuts, smallest, high):
    def one(position, blocks):
        heights = jax.random.uniform(jax.random.fold_in(jax.random.fold_in(stream_key, 6), position), (blocks,), jnp.float32, smallest / len(cuts), high / len(cuts))
        return jnp.repeat(jnp.exp(heights), dims[position] // blocks).reshape((-1,) + (1,) * (len(dims) - position - 1))

    factor_of = one(*cuts[0])
    for cut in cuts[1:]:
        factor_of = factor_of * one(*cut)
    return factor_of


def bell_draw(rng, dims, width, bound, pieces=(), kind=jnp.bfloat16):
    gain = shard_levels(rng, dims, pieces, -0.22, 0.18) if pieces else 1.0
    values = jax.random.normal(rng, dims, jnp.float32) * width * gain
    return jnp.minimum(jnp.maximum(values, -bound), bound).astype(kind)


def setup_inputs(seed: int = 0) -> dict:
    streams_of = jax.random.split(jax.random.key(seed), 6)
    traces = draw_traces(jax.random.fold_in(streams_of[5], 71), 0)
    station_flags = set_ends((jax.random.randint(streams_of[1], (STATIONS,), 0, 8) < 7).astype(jnp.int32), jax.random.fold_in(streams_of[1], 1), 0, 1)
    tile_mask = set_ends((jax.random.randint(streams_of[2], (BLOCKS, BLOCKS), 0, 4) < 3).astype(jnp.int32), jax.random.fold_in(streams_of[2], 1), 0, 1)
    band_block = jax.random.randint(streams_of[3], (1,), 1, TIME_DEV // 250 + 3).astype(jnp.int32)
    stacks = bell_draw(streams_of[4], (STATIONS, STATIONS, 2, BINS), 1.0, 6.0, ((0, 4), (3, 8)), jnp.float32)
    return dict(traces=traces, station_flags=station_flags, tile_mask=tile_mask, band_block=band_block, stacks=stacks)


EPS_MEAN = 1e-06
EPS_POWER = 1e-06
HIGH = lax.Precision.HIGHEST

def window_mean(padded, length, half_width):
    row_count = padded.shape[0]
    window_span = 2 * half_width
    block_count = length // window_span
    blocked = padded.reshape(row_count, block_count + 1, window_span)
    joined = jnp.concatenate([blocked[:, :-1], blocked[:, 1:]], axis=2)
    summed = jnp.cumsum(joined, axis=2)
    summed = jnp.concatenate([jnp.zeros((row_count, block_count, 1), jnp.float32), summed], axis=2)
    window = summed[:, :, window_span + 1:2 * window_span + 1] - summed[:, :, 0:window_span]
    return window.reshape(row_count, length) / (2 * half_width + 1)

def reference(traces, station_flags, tile_mask, band_block, stacks):
    offsets = jnp.arange(BINS_DEV, dtype=jnp.int32)
    residue_ids = jnp.arange(N_TM, dtype=jnp.int32)
    chosen = (residue_ids[:, None] + N_TM * (band_block[0] + offsets[None, :])).reshape(-1).astype(jnp.int32)

    def one_station(packed):
        trace_row, flag_value = packed
        signal = trace_row.astype(jnp.float32)
        widened = jnp.pad(jnp.abs(signal), (HALF_WIN, HALF_WIN))[None, :]
        running = window_mean(widened, SAMPLES, HALF_WIN)[0]
        normalized = flag_value.astype(jnp.float32) * signal / (running + EPS_MEAN)
        spectrum = jnp.fft.rfft(normalized)
        picked = jnp.take(spectrum, chosen)
        return (jnp.real(picked).astype(jnp.float32), jnp.imag(picked).astype(jnp.float32))
    spec_real, spec_imag = lax.map(one_station, (traces, station_flags))
    power_sum = spec_real * spec_real + spec_imag * spec_imag
    grouped = power_sum.reshape(STATIONS, N_TM, BINS_DEV)
    nearby = (jnp.abs(offsets[:, None] - offsets[None, :]) <= SMOOTH).astype(jnp.float32)
    smoothed = jnp.einsum('srj,jk->srk', grouped, nearby, precision=HIGH) / (2 * SMOOTH + 1)
    amplitude = jnp.sqrt(smoothed.reshape(STATIONS, BINS) + EPS_POWER)
    white_real = spec_real / amplitude
    white_imag = spec_imag / amplitude
    block_of = jnp.arange(STATIONS, dtype=jnp.int32) // STA_DEV
    member = (block_of[:, None] == jnp.arange(tile_mask.shape[0], dtype=jnp.int32)[None, :]).astype(jnp.float32)
    pair_mask = jnp.dot(jnp.dot(member, tile_mask.astype(jnp.float32), precision=HIGH), member.T, precision=HIGH)

    def one_row(packed):
        row_real, row_imag, mask_row, stack_row = packed
        cross_real = row_real[None, :] * white_real + row_imag[None, :] * white_imag
        cross_imag = row_imag[None, :] * white_real - row_real[None, :] * white_imag
        return stack_row + mask_row[:, None, None] * jnp.stack([cross_real, cross_imag], axis=1)
    return lax.map(one_row, (white_real, white_imag, pair_mask, stacks))
```

```python
import functools
import math

import jax
import jax.numpy as jnp
import numpy as np
from jax import lax
from jax.experimental import pallas as pl
from jax.experimental.pallas import tpu as pltpu
from jax.sharding import PartitionSpec as P

HALF_WIN = 512
SMOOTH = 32
EPS_MEAN = 1e-06
EPS_POWER = 1e-06
LANES = 128
SPAN = 2 * HALF_WIN
TILES = SPAN // LANES
HALF_TILES = HALF_WIN // LANES
PAD = 16
HIGH = lax.Precision.HIGHEST
BF = jnp.bfloat16
F32 = jnp.float32


def up_to(value, step):
    return -(-value // step) * step


def sincos(turns):
    quarter = jnp.round(turns * 4.0)
    rest = turns - quarter * 0.25
    y = rest * (2.0 * math.pi)
    y2 = y * y
    s = y + y * y2 * (-1.0 / 6 + y2 * (1.0 / 120 + y2 * (-1.0 / 5040 + y2 * (1.0 / 362880))))
    c = 1.0 + y2 * (-0.5 + y2 * (1.0 / 24 + y2 * (-1.0 / 720 + y2 * (1.0 / 40320))))
    q = quarter - 4.0 * jnp.floor(quarter * 0.25)
    swap = (q == 1.0) | (q == 3.0)
    sine = jnp.where(swap, c, s)
    cosine = jnp.where(swap, s, c)
    sine = jnp.where(q >= 2.0, -sine, sine)
    cosine = jnp.where((q == 1.0) | (q == 2.0), -cosine, cosine)
    return sine, cosine


def turns_of(product, period):
    whole = jnp.floor(product * (1.0 / period))
    return (product - whole * period) * (1.0 / period)


def split2(value):
    high = value.astype(BF)
    return high, (value - high.astype(F32)).astype(BF)


def iota(shape, axis):
    return lax.broadcasted_iota(jnp.int32, shape, axis)


def iota_f(shape, axis):
    return iota(shape, axis).astype(F32)


def window_table():
    low = np.arange(LANES)
    upto = (low[:, None] <= low[None, :]).astype(np.float32)
    onward = (low[:, None] >= low[None, :]).astype(np.float32)
    return np.concatenate([upto, onward, np.ones((LANES, LANES), np.float32)], axis=1)


def np_split(value):
    high = value.astype(jnp.bfloat16).astype(np.float64)
    return high, (value - high).astype(jnp.bfloat16).astype(np.float64)


class Sizes:
    def __init__(self, stations, length, tm_count, bins):
        self.stations, self.length, self.tm, self.bins = stations, length, tm_count, bins
        self.rows = length // SPAN
        self.rows_pad = up_to(self.rows, PAD)
        self.block = min(tm_count, 16)
        self.blocks = tm_count // self.block
        self.folds = -(-(bins + self.rows - 1) // self.rows)
        self.spec_lanes = self.rows * LANES
        self.edge_lanes = 2 * stations * SPAN
        self.payload = self.spec_lanes + self.edge_lanes
        assert length % SPAN == 0 and tm_count % self.block == 0
        assert 2 * stations * PAD * 2 <= LANES and self.folds <= PAD
        assert self.rows >= 2 and 5 * self.rows_pad <= 256

    def first_table(self):
        j2 = np.arange(self.tm)[:, None] + self.tm * np.arange(self.rows)[None, :]
        j2 = j2.reshape(self.blocks, self.block, self.rows).transpose(0, 2, 1).reshape(self.blocks, -1)
        period = self.tm * self.rows
        angle = 2.0 * np.pi / period * (j2[:, :, None] * np.arange(self.rows) % period)
        parts = np.concatenate([np.cos(angle), -np.sin(angle)], axis=1)
        parts = np.pad(parts, ((0, 0), (0, 0), (0, self.rows_pad - self.rows)))
        high, low = np_split(parts)
        return np.concatenate([high, high, high, low, low], axis=2).astype(jnp.bfloat16)

    def shift_table(self):
        angle = 2.0 * np.pi / self.length * (
            np.arange(self.rows)[:, None] * np.arange(SPAN)[None, :] % self.length
        )
        return np.stack([np.cos(angle), -np.sin(angle)]).astype(np.float32)


def transform_kernel(z, band, place, flags, x, first, shift, window, out, xs, sums, stack, weight, acc):
    rows, pad, block = z.rows, z.rows_pad, z.block
    top = 8
    for s in range(z.stations):
        xs[s, 0:top, :] = jnp.zeros((top, SPAN), F32)
        xs[s, top + (rows // 8) * 8 : top + pad, :] = jnp.zeros((pad - (rows // 8) * 8, SPAN), F32)
    for a in range(rows):
        piece = x[:, a * SPAN : (a + 1) * SPAN].astype(F32)
        xs[:, top + a, :] = piece
    for s in range(z.stations):
        for c in range(TILES):
            magnitude = jnp.abs(xs[s, top : top + pad, c * LANES : (c + 1) * LANES]).astype(BF)
            sums[s, c, 0:top, :] = jnp.zeros((top, 3 * LANES), F32)
            sums[s, c, top : top + pad, :] = jnp.dot(magnitude, window[...], preferred_element_type=F32)
            sums[s, c, top + pad : top + pad + 8, :] = jnp.zeros((8, 3 * LANES), F32)

        def tile(kind, c):
            turn, cc = divmod(c, TILES)
            return sums[s, cc, top + turn : top + turn + pad, kind * LANES : (kind + 1) * LANES]

        whole = [tile(2, c) for c in range(1 - HALF_TILES, TILES + HALF_TILES - 1)]
        flag = flags[s].astype(F32)
        row = iota((pad, LANES), 0)
        for c in range(TILES):
            total = tile(1, c - HALF_TILES) + tile(0, c + HALF_TILES)
            for d in range(2 * HALF_TILES - 1):
                total = total + whole[c + d]
            here = xs[s, top : top + pad, c * LANES : (c + 1) * LANES]
            value = flag * here / (total * (1.0 / (2 * HALF_WIN + 1)) + EPS_MEAN)
            edge = 0 if c < HALF_TILES else rows - 1
            value = jnp.where(row == edge, 0.0, value)
            high = value.astype(BF)
            left = value - high.astype(F32)
            mid = left.astype(BF)
            low = (left - mid.astype(F32)).astype(BF)
            for k, part in enumerate((high, mid, low, high, mid)):
                stack[s, k * pad : (k + 1) * pad, c * LANES : (c + 1) * LANES] = part
    fold0 = band[0] // rows
    order = iota((PAD, SPAN), 0) + fold0
    lane = iota((PAD, SPAN), 1)
    turns = jnp.bitwise_and(order * lane, SPAN - 1).astype(F32) * (1.0 / SPAN)
    sine, cosine = sincos(turns)
    (sin_h, sin_l), (cos_h, cos_l) = split2(sine), split2(cosine)
    nothing = jnp.zeros((PAD, SPAN), BF)
    for h, (cc, ss) in enumerate(((cos_h, sin_h), (cos_l, sin_l))):
        at = h * 4 * PAD
        weight[at : at + PAD, 0:SPAN] = cc
        weight[at + PAD : at + 2 * PAD, 0:SPAN] = -ss
        weight[at : at + PAD, SPAN : 2 * SPAN] = ss
        weight[at + PAD : at + 2 * PAD, SPAN : 2 * SPAN] = cc
        for k in (2, 3):
            for part in range(2):
                weight[at + k * PAD : at + (k + 1) * PAD, part * SPAN : (part + 1) * SPAN] = nothing
    acc[...] = jnp.zeros_like(acc)
    here = place[0]
    residue = pl.program_id(0) * block + iota((block, 256), 0)
    start = turns_of((here * residue).astype(F32), z.tm)

    def step(c, carry):
        lanes = pl.ds(pl.multiple_of(c * 256, 256), 256)
        lanes_im = pl.ds(pl.multiple_of(SPAN + c * 256, 256), 256)
        offset = c * 256 + iota((block, 256), 1)
        turn = start + (residue * offset).astype(F32) * (1.0 / (z.tm * z.length))
        sn, cs = sincos(turn)
        r_re, r_im = cs[None], -sn[None]
        m_re = shift[0, :, lanes][:, None, :]
        m_im = shift[1, :, lanes][:, None, :]
        t_re = (m_re * r_re - m_im * r_im).reshape(rows * block, 256)
        t_im = (m_re * r_im + m_im * r_re).reshape(rows * block, 256)
        for s in range(z.stations):
            f = jnp.dot(first[0], stack[s, :, lanes], preferred_element_type=F32)
            f_re, f_im = f[: rows * block], f[rows * block :]
            z_re = f_re * t_re - f_im * t_im
            z_im = f_re * t_im + f_im * t_re
            part = jnp.zeros((rows * block, LANES), F32)
            for value, w in ((z_re, weight[:, lanes]), (z_im, weight[:, lanes_im])):
                for piece in split2(value):
                    part = part + lax.dot_general(
                        piece, w, (((1,), (1,)), ((), ())), preferred_element_type=F32
                    )
            acc[s] = acc[s] + part
        return carry

    lax.fori_loop(0, SPAN // 256, step, 0)
    total = acc[0]
    for s in range(1, z.stations):
        total = total + pltpu.roll(acc[s], s * 2 * PAD, 1)
    total = total + pltpu.roll(total, LANES // 2, 1)
    high = total.astype(BF).astype(F32)
    low = total - high
    both = jnp.where(iota(total.shape, 1) < LANES // 2, high, low)
    for m in range(rows):
        out[:, m * LANES : (m + 1) * LANES] = both[m * block : (m + 1) * block].astype(BF)
    at = z.spec_lanes
    for begin in (0, z.length - SPAN):
        for s in range(z.stations):
            line = x[s : s + 1, begin : begin + SPAN].astype(F32)
            out[:, at : at + SPAN] = jnp.broadcast_to(line, (block, SPAN)).astype(BF)
            at += SPAN


def transform(z, band, place, flags, x):
    smem = pl.BlockSpec(memory_space=pltpu.SMEM)
    vmem = pl.BlockSpec(memory_space=pltpu.VMEM)
    width = 5 * z.rows_pad
    height = 2 * z.rows * z.block
    return pl.pallas_call(
        functools.partial(transform_kernel, z),
        grid=(z.blocks,),
        in_specs=[
            smem,
            smem,
            smem,
            vmem,
            pl.BlockSpec((1, height, width), lambda i: (i, 0, 0)),
            vmem,
            vmem,
        ],
        out_specs=pl.BlockSpec((z.block, z.payload), lambda i: (i, 0)),
        out_shape=jax.ShapeDtypeStruct((z.tm, z.payload), BF),
        scratch_shapes=[
            pltpu.VMEM((z.stations, 8 + z.rows_pad, SPAN), F32),
            pltpu.VMEM((z.stations, TILES, 16 + z.rows_pad, 3 * LANES), F32),
            pltpu.VMEM((z.stations, width, SPAN), BF),
            pltpu.VMEM((LANES, 2 * SPAN), BF),
            pltpu.VMEM((z.stations, z.rows * z.block, LANES), F32),
        ],
        name="transform",
    )(band, place, flags, x, jnp.asarray(z.first_table()), jnp.asarray(z.shift_table()),
      jnp.asarray(window_table(), BF))


def spectrum_kernel(z, band, place, flags, got, window, out):
    rows, tm, bins = z.rows, z.tm, z.bins
    base = band[0]
    residue = place[0]
    first = base % rows
    spot = iota_f((1, bins), 1) + first.astype(F32)
    fold = jnp.floor((spot + 0.5) * (1.0 / rows))
    rest = spot - fold * rows
    which = iota_f((rows, tm, bins), 0).reshape(rows * tm, bins)
    choose = (which == rest).astype(F32).astype(BF)
    parts = jnp.concatenate(
        [got[:, m * LANES : (m + 1) * LANES].astype(F32) for m in range(rows)], axis=0
    ).astype(BF)
    placed = lax.dot_general(parts, choose, (((0,), (0,)), ((), ())), preferred_element_type=F32)
    keep = (iota_f((PAD, bins), 0) == fold).astype(F32)
    folded = [
        jnp.sum(placed[k * PAD : (k + 1) * PAD] * keep, axis=0, keepdims=True)
        for k in range(2 * 2 * z.stations)
    ]
    spec = [folded[k] + folded[k + 2 * z.stations] for k in range(2 * z.stations)]
    count = 2 * TILES
    pieces = []
    for s in range(z.stations):
        for i in range(count):
            side = 1 if i < TILES else 0
            at = z.spec_lanes + (side * z.stations + s) * SPAN + (i % TILES) * LANES
            value = got[:, at : at + LANES].astype(F32)
            pieces.append(pltpu.roll(value, 1, 0) if side else value)
    magnitude = jnp.abs(jnp.concatenate(pieces, axis=0)).astype(BF)
    sums = jnp.dot(magnitude, window[...], preferred_element_type=F32)
    inner = iota((tm, LANES), 0) != 0
    p_turns = turns_of((residue * iota((tm, LANES), 0)).astype(F32), tm)
    p_sin, p_cos = sincos(p_turns)

    freq = (residue + tm * (base + iota((1, bins), 1))).astype(F32)
    step = iota_f((PAD, bins), 0)
    step = step - jnp.where(step >= TILES, float(TILES), 0.0) - HALF_TILES
    a_sin, a_cos = sincos(turns_of(step * freq, tm * (z.length // LANES)))
    real_row = iota((PAD, bins), 0) < TILES
    table = jnp.concatenate(
        [jnp.where(real_row, a_cos, a_sin), jnp.where(real_row, -a_sin, a_cos)], axis=1
    )
    l_sin, l_cos = sincos(turns_of(iota_f((LANES, bins), 0) * freq, tm * z.length))
    near = jnp.abs(iota((bins, bins), 0) - iota((bins, bins), 1)) <= SMOOTH
    near = near.astype(F32).astype(BF)

    for s in range(z.stations):
        def get(kind, i):
            at = (s * count + i) * tm
            return sums[at : at + tm, kind * LANES : (kind + 1) * LANES]

        reals, imags = [], []
        flag = flags[s].astype(F32)
        for i in range(HALF_TILES, HALF_TILES + TILES):
            terms = [(i - HALF_TILES, 1), (i + HALF_TILES, 0)]
            terms += [(i + d, 2) for d in range(1 - HALF_TILES, HALF_TILES)]
            own, other = jnp.zeros((tm, LANES), F32), jnp.zeros((tm, LANES), F32)
            for j, kind in terms:
                if (j < TILES) == (i < TILES):
                    own = own + get(kind, j)
                else:
                    other = other + get(kind, j)
            total = own + jnp.where(inner, other, 0.0)
            value = flag * pieces[s * count + i] / (total * (1.0 / (2 * HALF_WIN + 1)) + EPS_MEAN)
            reals.append(jnp.sum(value * p_cos, axis=0, keepdims=True))
            imags.append(-jnp.sum(value * p_sin, axis=0, keepdims=True))
        mixed = jnp.concatenate(reals + imags, axis=0)
        spread = lax.dot_general(
            mixed, table, (((0,), (0,)), ((), ())), precision=HIGH, preferred_element_type=F32
        )
        g_re, g_im = spread[:, :bins], spread[:, bins:]
        re = spec[2 * s] + jnp.sum(g_re * l_cos + g_im * l_sin, axis=0, keepdims=True)
        im = spec[2 * s + 1] + jnp.sum(g_im * l_cos - g_re * l_sin, axis=0, keepdims=True)
        power = re * re + im * im
        high = power.astype(BF)
        left = power - high.astype(F32)
        mid = left.astype(BF)
        low = (left - mid.astype(F32)).astype(BF)
        stacked = jnp.concatenate(
            [high.astype(F32), mid.astype(F32), low.astype(F32), jnp.zeros((5, bins), F32)], axis=0
        ).astype(BF)
        smooth = jnp.dot(stacked, near, preferred_element_type=F32)
        smooth = (smooth[0:1] + smooth[1:2] + smooth[2:3]) * (1.0 / (2 * SMOOTH + 1))
        scale = 1.0 / jnp.sqrt(smooth + EPS_POWER)
        out[2 * s : 2 * s + 1, :] = re * scale
        out[2 * s + 1 : 2 * s + 2, :] = im * scale


def spectrum(z, band, place, flags, got):
    smem = pl.BlockSpec(memory_space=pltpu.SMEM)
    vmem = pl.BlockSpec(memory_space=pltpu.VMEM)
    return pl.pallas_call(
        functools.partial(spectrum_kernel, z),
        in_specs=[smem, smem, smem, vmem, vmem],
        out_specs=vmem,
        out_shape=jax.ShapeDtypeStruct((2 * z.stations, z.bins), F32),
        name="spectrum",
    )(band, place, flags, got, jnp.asarray(window_table(), BF))


def shards(traces, station_flags, tile_mask, band_block, stacks):
    tm_count = lax.axis_size("tm")
    sta_here = lax.axis_index("sta")
    stations, length = traces.shape
    z = Sizes(stations, length, tm_count, stacks.shape[-1])
    place = lax.axis_index("tm").astype(jnp.int32).reshape(1)
    sent = transform(z, band_block, place, station_flags, traces)
    got = lax.all_to_all(sent, "tm", split_axis=0, concat_axis=0, tiled=True)
    white = spectrum(z, band_block, place, station_flags, got)
    every = lax.all_gather(white, "sta", axis=0, tiled=True).reshape(-1, 2, z.bins)
    mine = white.reshape(stations, 2, z.bins)
    other_real, other_imag = every[:, 0], every[:, 1]
    real, imag = mine[:, 0], mine[:, 1]
    mask_row = lax.dynamic_index_in_dim(tile_mask, sta_here, 0, keepdims=False).astype(F32)
    column_mask = jnp.repeat(mask_row, stations)
    cross_real = real[:, None, :] * other_real[None] + imag[:, None, :] * other_imag[None]
    cross_imag = imag[:, None, :] * other_real[None] - real[:, None, :] * other_imag[None]
    return stacks + jnp.stack([cross_real, cross_imag], axis=2) * column_mask[None, :, None, None]


def solution(mesh):
    return jax.shard_map(
        shards,
        mesh=mesh,
        in_specs=(P("sta", "tm"), P("sta"), P(), P(), P("sta", None, None, "tm")),
        out_specs=P("sta", None, None, "tm"),
        check_vma=False,
    )
```

```python
import functools
import math

import jax
import jax.numpy as jnp
import numpy as np
from jax import lax
from jax.experimental import pallas as pl
from jax.experimental.pallas import tpu as pltpu
from jax.sharding import PartitionSpec as P

HALF_WIN = 512
SMOOTH = 32
EPS_MEAN = 1e-06
EPS_POWER = 1e-06
LANES = 128
SPAN = 2 * HALF_WIN
TILES = SPAN // LANES
HALF_TILES = HALF_WIN // LANES
PAD = 16
VMEM_LIMIT = 16 * 1024 * 1024
BF = jnp.bfloat16
F32 = jnp.float32


def up_to(value, step):
    return -(-value // step) * step


def sincos(turns):
    quarter = jnp.round(turns * 4.0)
    rest = turns - quarter * 0.25
    y = rest * (2.0 * math.pi)
    y2 = y * y
    s = y + y * y2 * (-1.0 / 6 + y2 * (1.0 / 120 + y2 * (-1.0 / 5040 + y2 * (1.0 / 362880))))
    c = 1.0 + y2 * (-0.5 + y2 * (1.0 / 24 + y2 * (-1.0 / 720 + y2 * (1.0 / 40320))))
    q = quarter - 4.0 * jnp.floor(quarter * 0.25)
    swap = (q == 1.0) | (q == 3.0)
    sine = jnp.where(swap, c, s)
    cosine = jnp.where(swap, s, c)
    sine = jnp.where(q >= 2.0, -sine, sine)
    cosine = jnp.where((q == 1.0) | (q == 2.0), -cosine, cosine)
    return sine, cosine


def turns_of(product, period):
    whole = jnp.floor(product * (1.0 / period))
    return (product - whole * period) * (1.0 / period)


def split2(value):
    high = value.astype(BF)
    return high, (value - high.astype(F32)).astype(BF)


def iota(shape, axis):
    return lax.broadcasted_iota(jnp.int32, shape, axis)


def iota_f(shape, axis):
    return iota(shape, axis).astype(F32)


def window_tables():
    row, lane = iota((LANES, LANES), 0), iota((LANES, LANES), 1)
    upto = (row <= lane).astype(F32).astype(BF)
    onward = (row >= lane).astype(F32).astype(BF)
    return upto, onward, jnp.ones((LANES, LANES), BF)


def np_split(value):
    high = value.astype(jnp.bfloat16).astype(np.float64)
    return high, (value - high).astype(jnp.bfloat16).astype(np.float64)


class Sizes:
    def __init__(self, stations, length, tm_count, bins):
        self.stations, self.length, self.tm, self.bins = stations, length, tm_count, bins
        self.rows = length // SPAN
        self.half = self.rows // 2 + 1
        self.pad = up_to(self.rows, PAD)
        self.block = min(tm_count, 16)
        self.blocks = tm_count // self.block
        self.folds = -(-(bins + self.rows - 1) // self.rows)
        self.spec_rows = up_to(2 * self.half, 8)
        self.edge_rows = 2 * stations * TILES
        self.sent_rows = self.spec_rows + self.edge_rows
        assert length % SPAN == 0 and tm_count % self.block == 0
        assert stations == 2 and self.folds <= PAD
        assert self.rows >= 2 and 4 * self.pad <= 256

    def first_table(self):
        j2 = np.arange(self.tm)[:, None] + self.tm * np.arange(self.half)[None, :]
        j2 = j2.reshape(self.blocks, self.block, self.half).transpose(0, 2, 1).reshape(self.blocks, -1)
        period = self.tm * self.rows
        angle = 2.0 * np.pi / period * (j2[:, :, None] * np.arange(self.rows) % period)
        parts = np.concatenate([np.cos(angle), -np.sin(angle)], axis=1)
        parts = np.pad(parts, ((0, 0), (0, 0), (0, self.pad - self.rows)))
        high, low = np_split(parts)
        return np.concatenate([high, high, low, low], axis=2).astype(jnp.bfloat16)

    def shift_table(self):
        angle = 2.0 * np.pi / self.length * (
            np.arange(self.half)[:, None] * np.arange(SPAN)[None, :] % self.length
        )
        return np.stack([np.cos(angle), -np.sin(angle)]).astype(np.float32)


def normalize(z, flags, x, xs, wide, stack, edges):
    rows, pad, top = z.rows, z.pad, 8
    full = rows // 8 * 8
    for s in range(z.stations):
        xs[s, 0:top, :] = jnp.zeros((top, SPAN), F32)
        xs[s, top + full : top + pad + 8, :] = jnp.zeros((pad + 8 - full, SPAN), F32)
    for a in range(rows):
        xs[:, top + a, :] = x[:, a * SPAN : (a + 1) * SPAN].astype(F32)
    for s in range(z.stations):
        for side, a in ((0, 0), (1, rows - 1)):
            for c in range(TILES):
                at = (side * z.stations + s) * TILES + c
                edges[at : at + 1, :] = xs[s, top + a : top + a + 1, c * LANES : (c + 1) * LANES]
    upto, onward, ones = window_tables()
    kernel = jnp.concatenate([onward] + [ones] * (2 * HALF_TILES - 1) + [upto], axis=0)
    row = iota((pad, LANES), 0)
    for s in range(z.stations):
        for turn, (lo, hi) in ((-1, (HALF_WIN, SPAN)), (0, (0, SPAN)), (1, (0, HALF_WIN))):
            at = HALF_WIN + turn * SPAN + lo
            wide[s, :, at : at + hi - lo] = jnp.abs(
                xs[s, top + turn : top + turn + pad, lo:hi]
            ).astype(BF)
        for c in range(TILES):
            here = wide[s, :, c * LANES : c * LANES + SPAN + LANES]
            total = jnp.dot(here, kernel, preferred_element_type=F32)
            value = xs[s, top : top + pad, c * LANES : (c + 1) * LANES] * flags[s].astype(F32)
            value = value / (total * (1.0 / (2 * HALF_WIN + 1)) + EPS_MEAN)
            edge = 0 if c < HALF_TILES else rows - 1
            high, low = split2(jnp.where(row == edge, 0.0, value))
            for k, part in enumerate((high, low, high, low)):
                stack[s, k * pad : (k + 1) * pad, c * LANES : (c + 1) * LANES] = part


def fold_weights(z, band, weight):
    for kind in range(2):
        order = iota((PAD, SPAN), 0) + (band[0] // z.rows + kind)
        turns = jnp.bitwise_and(order * iota((PAD, SPAN), 1), SPAN - 1).astype(F32) * (1.0 / SPAN)
        sine, cosine = sincos(turns)
        for h, (s, c) in enumerate(zip(split2(sine), split2(cosine))):
            table = ((c, s), (-s, c)) if kind == 0 else ((c, -s), (-s, -c))
            for part in range(2):
                at = h * 4 * PAD + kind * 2 * PAD + part * PAD
                weight[at : at + PAD, 0:SPAN] = table[part][0]
                weight[at : at + PAD, SPAN : 2 * SPAN] = table[part][1]


def transform_kernel(
    z, band, place, flags, x, first, shift, out, xs, wide, stack, edges, weight, acc, both, spec
):
    half, block, tm = z.half, z.block, z.tm
    height = half * block
    index = pl.program_id(0)

    def prologue():
        normalize(z, flags, x, xs, wide, stack, edges)
        fold_weights(z, band, weight)
        spec[:, z.spec_rows - 8 : z.spec_rows, :] = jnp.zeros((tm, 8, LANES), F32)

    if z.blocks == 1:
        prologue()
    else:
        pl.when(index == 0)(prologue)
    acc[...] = jnp.zeros_like(acc)
    width = 256
    residue = index * block + iota((block, width), 0)
    start = turns_of((place[0] * residue).astype(F32), tm)

    def step(c, carry):
        lanes = pl.ds(pl.multiple_of(c * width, width), width)
        lanes_im = pl.ds(pl.multiple_of(SPAN + c * width, width), width)
        offset = c * width + iota((block, width), 1)
        turn = start + (residue * offset).astype(F32) * (1.0 / (tm * z.length))
        sn, cs = sincos(turn)
        r_re, r_im = cs[None], -sn[None]
        m_re = shift[0, :, lanes][:, None, :]
        m_im = shift[1, :, lanes][:, None, :]
        t_re = (m_re * r_re - m_im * r_im).reshape(height, width)
        t_im = (m_re * r_im + m_im * r_re).reshape(height, width)
        w = jnp.concatenate([weight[:, lanes], weight[:, lanes_im]] * 2, axis=1)
        for s in range(z.stations):
            f = jnp.dot(first[0], stack[s, :, lanes], preferred_element_type=F32)
            f_re, f_im = f[:height], f[height:]
            re_h, re_l = split2(f_re * t_re - f_im * t_im)
            im_h, im_l = split2(f_re * t_im + f_im * t_re)
            value = jnp.concatenate([re_h, im_h, re_l, im_l], axis=1)
            acc[s] += lax.dot_general(
                value, w, (((1,), (1,)), ((), ())), preferred_element_type=F32
            )
        return carry

    lax.fori_loop(0, SPAN // width, step, 0)
    zero, one = (acc[s] + pltpu.roll(acc[s], LANES // 2, 1) for s in range(2))
    lane = iota((height, LANES), 1)
    early = jnp.bitwise_and(lane, LANES // 2 - 1) < LANES // 4
    direct = jnp.where(early, zero, pltpu.roll(one, LANES // 4, 1))
    mirror = jnp.where(early, pltpu.roll(zero, LANES // 4, 1), one)
    for kind, value in enumerate((direct, mirror)):
        high = value.astype(BF).astype(F32)
        both[kind] = jnp.where(lane < LANES // 2, high, value - high)
    for k in range(block):
        here = index * block + k
        there = jnp.where(here == 0, 0, tm - here) if z.blocks > 1 else (tm - k) % tm
        here = here if z.blocks > 1 else k
        rows = pl.ds(k, half, stride=block)
        spec[here, 0:half, :] = both[0, rows, :]
        spec[there, half : 2 * half, :] = both[1, rows, :]

    def finish():
        ends = edges[...].astype(BF)

        def one_row(k, carry):
            out[k, 0 : z.spec_rows, :] = spec[k].astype(BF)
            out[k, z.spec_rows : z.sent_rows, :] = ends
            return carry

        if z.blocks == 1:
            for k in range(tm):
                one_row(k, 0)
        else:
            lax.fori_loop(0, tm, one_row, 0)

    if z.blocks == 1:
        finish()
    else:
        pl.when(index == z.blocks - 1)(finish)


SMEM_SPEC = pl.BlockSpec(memory_space=pltpu.SMEM)
VMEM_SPEC = pl.BlockSpec(memory_space=pltpu.VMEM)


def params():
    return pltpu.CompilerParams(vmem_limit_bytes=VMEM_LIMIT)


def transform(z, band, place, flags, x):
    width = 4 * z.pad
    height = z.half * z.block
    return pl.pallas_call(
        functools.partial(transform_kernel, z),
        grid=(z.blocks,),
        in_specs=[
            SMEM_SPEC,
            SMEM_SPEC,
            SMEM_SPEC,
            VMEM_SPEC,
            pl.BlockSpec((1, 2 * height, width), lambda i: (i, 0, 0)),
            VMEM_SPEC,
        ],
        out_specs=VMEM_SPEC,
        out_shape=jax.ShapeDtypeStruct((z.tm, z.sent_rows, LANES), BF),
        scratch_shapes=[
            pltpu.VMEM((z.stations, 16 + z.pad, SPAN), F32),
            pltpu.VMEM((z.stations, z.pad, 2 * SPAN), BF),
            pltpu.VMEM((z.stations, width, SPAN), BF),
            pltpu.VMEM((z.edge_rows, LANES), F32),
            pltpu.VMEM((LANES, 2 * SPAN), BF),
            pltpu.VMEM((z.stations, height, LANES), F32),
            pltpu.VMEM((2, height, LANES), F32),
            pltpu.VMEM((z.tm, z.spec_rows, LANES), F32),
        ],
        compiler_params=params(),
        name="transform",
    )(band, place, flags, x, jnp.asarray(z.first_table()), jnp.asarray(z.shift_table()))


def table_kernel(z, band, place, choose, keep, steps, turns, near, phase):
    rows, tm, bins, half = z.rows, z.tm, z.bins, z.half
    base, residue = band[0], place[0]
    spot = iota_f((1, bins), 1) + (base % rows).astype(F32)
    fold = jnp.floor((spot + 0.5) * (1.0 / rows))
    rest = spot - fold * rows
    row = iota_f((z.spec_rows, bins), 0)
    last = (rows - 1 + half + (residue == 0).astype(jnp.int32)).astype(F32)
    mirror = last - row
    target = jnp.where(row < half, row, jnp.where(mirror >= half, mirror, -1.0))
    one = (target == rest).astype(F32).astype(BF)
    for p in range(tm):
        choose[p] = one
    keep[...] = (iota_f((PAD, bins), 0) == fold).astype(F32)
    freq = (residue + tm * (base + iota((1, bins), 1))).astype(F32)
    step = iota_f((TILES, bins), 0) - HALF_TILES
    sine, cosine = sincos(turns_of(step * freq, tm * (z.length // LANES)))
    table = jnp.concatenate(
        [jnp.concatenate([cosine, -sine], axis=1), jnp.concatenate([sine, cosine], axis=1)], axis=0
    )
    high, low = split2(table)
    for k, part in enumerate((high, high, low, low)):
        steps[k * 2 * TILES : (k + 1) * 2 * TILES, :] = part
    sine, cosine = sincos(turns_of(iota_f((LANES, bins), 0) * freq, tm * z.length))
    turns[0] = cosine
    turns[1] = sine
    gap = jnp.abs(iota((bins, bins), 0) - iota((bins, bins), 1))
    near[...] = (gap <= SMOOTH).astype(F32).astype(BF)
    p_sin, p_cos = sincos(turns_of((residue * iota((tm, LANES), 0)).astype(F32), tm))
    phase[0] = p_cos
    phase[1] = -p_sin


def tables(z, band, place):
    return pl.pallas_call(
        functools.partial(table_kernel, z),
        in_specs=[SMEM_SPEC, SMEM_SPEC],
        out_specs=[VMEM_SPEC] * 6,
        out_shape=[
            jax.ShapeDtypeStruct((z.tm, z.spec_rows, z.bins), BF),
            jax.ShapeDtypeStruct((PAD, z.bins), F32),
            jax.ShapeDtypeStruct((8 * TILES, 2 * z.bins), BF),
            jax.ShapeDtypeStruct((2, LANES, z.bins), F32),
            jax.ShapeDtypeStruct((z.bins, z.bins), BF),
            jax.ShapeDtypeStruct((2, z.tm, LANES), F32),
        ],
        compiler_params=params(),
        cost_estimate=pl.CostEstimate(flops=4000000, bytes_accessed=2000000, transcendentals=0),
        name="tables",
    )(band, place)


def sublane_sums(value, row):
    total = value
    for shift in (1, 2, 4):
        total = total + jnp.where(row >= shift, pltpu.roll(total, shift, 0), 0.0)
    return total - value, total


def spectrum_kernel(z, flags, got, choose, keep, steps, turns, near, phase, out):
    tm, bins, at = z.tm, z.bins, z.spec_rows
    parts = got[:, 0:at, :].astype(F32).reshape(tm * at, LANES).astype(BF)
    weights = choose[...].astype(F32).reshape(tm * at, bins).astype(BF)
    placed = lax.dot_general(parts, weights, (((0,), (0,)), ((), ())), preferred_element_type=F32)
    mask = keep[...]
    folded = [
        jnp.sum(placed[k * PAD : (k + 1) * PAD] * mask, axis=0, keepdims=True)
        for k in range(4 * z.stations)
    ]
    spec = [folded[k] + folded[k + 2 * z.stations] for k in range(2 * z.stations)]
    upto, onward, ones = window_tables()
    row = iota((TILES, LANES), 0)
    late = row >= HALF_TILES
    sides = []
    side_rows = z.stations * TILES
    for side, table in ((0, upto), (1, onward)):
        rows = slice(at + side * side_rows, at + (side + 1) * side_rows)
        value = got[:, rows, :].astype(F32).reshape(tm * side_rows, LANES)
        sums = jnp.dot(
            jnp.abs(value).astype(BF),
            jnp.concatenate([table, ones], axis=1),
            preferred_element_type=F32,
        )
        sides.append((value, sums))
    mixed = []
    for s in range(z.stations):
        real = jnp.zeros((TILES, LANES), F32)
        imag = jnp.zeros((TILES, LANES), F32)
        flag = flags[s].astype(F32)
        for p in range(tm):
            begin = (p * z.stations + s) * TILES
            before = ((p - 1) % tm * z.stations + s) * TILES
            value_r, sums_r = (v[begin : begin + TILES] for v in sides[0])
            value_l, sums_l = (v[before : before + TILES] for v in sides[1])
            earlier, _ = sublane_sums(sums_r[:, LANES:], row)
            right = sums_r[:, :LANES] + earlier
            tail = sums_l[:, LANES:]
            for shift in (1, 2, 4):
                tail = tail + jnp.where(row < TILES - shift, pltpu.roll(tail, TILES - shift, 0), 0.0)
            left = sums_l[:, :LANES] + jnp.where(
                row < TILES - 1, pltpu.roll(tail, TILES - 1, 0), 0.0
            )
            total = left + right if p else jnp.where(late, right, left)
            sample = pltpu.roll(jnp.where(late, value_l, value_r), HALF_TILES, 0)
            value = flag * sample / (total * (1.0 / (2 * HALF_WIN + 1)) + EPS_MEAN)
            real = real + value * phase[0, p : p + 1, :]
            imag = imag + value * phase[1, p : p + 1, :]
        mixed.append(jnp.concatenate([real, imag], axis=0))
    high, low = split2(jnp.concatenate(mixed, axis=1))
    spread = lax.dot_general(
        jnp.concatenate([high, low, high, low], axis=0),
        steps[...],
        (((0,), (0,)), ((), ())),
        preferred_element_type=F32,
    )
    cosine, sine = turns[0], turns[1]
    pieces = []
    for s in range(z.stations):
        g_re = spread[s * LANES : (s + 1) * LANES, :bins]
        g_im = spread[s * LANES : (s + 1) * LANES, bins:]
        spec[2 * s] += jnp.sum(g_re * cosine + g_im * sine, axis=0, keepdims=True)
        spec[2 * s + 1] += jnp.sum(g_im * cosine - g_re * sine, axis=0, keepdims=True)
        power = spec[2 * s] * spec[2 * s] + spec[2 * s + 1] * spec[2 * s + 1]
        for _ in range(3):
            part = power.astype(BF).astype(F32)
            pieces.append(part)
            power = power - part
    pieces.append(jnp.zeros((8 - len(pieces), bins), F32))
    smooth = jnp.dot(
        jnp.concatenate(pieces, axis=0).astype(BF), near[...], preferred_element_type=F32
    )
    for s in range(z.stations):
        mean = smooth[3 * s : 3 * s + 1] + smooth[3 * s + 1 : 3 * s + 2] + smooth[3 * s + 2 : 3 * s + 3]
        scale = 1.0 / jnp.sqrt(mean * (1.0 / (2 * SMOOTH + 1)) + EPS_POWER)
        out[2 * s : 2 * s + 1, :] = spec[2 * s] * scale
        out[2 * s + 1 : 2 * s + 2, :] = spec[2 * s + 1] * scale


def spectrum(z, flags, got, made):
    return pl.pallas_call(
        functools.partial(spectrum_kernel, z),
        in_specs=[SMEM_SPEC] + [VMEM_SPEC] * 7,
        out_specs=VMEM_SPEC,
        out_shape=jax.ShapeDtypeStruct((2 * z.stations, z.bins), F32),
        compiler_params=params(),
        name="spectrum",
    )(flags, got, *made)


def cross_kernel(z, offsets, mask, where, stacks, *refs):
    pieces, out = refs[:-1], refs[-1]
    here = where[0]
    mine = pieces[0][...]
    bins = z.bins
    sides = []
    for i in range(z.stations):
        re, im = mine[2 * i : 2 * i + 1], mine[2 * i + 1 : 2 * i + 2]
        sides.append((jnp.concatenate([re, im], axis=0), jnp.concatenate([im, -re], axis=0)))
    for offset, piece in zip(offsets, pieces):
        source = here ^ offset
        on = mask[here, source].astype(F32)
        for j in range(z.stations):
            re = jnp.broadcast_to(piece[2 * j : 2 * j + 1, :] * on, (2, bins))
            im = jnp.broadcast_to(piece[2 * j + 1 : 2 * j + 2, :] * on, (2, bins))
            column = source * z.stations + j
            for i, (p, q) in enumerate(sides):
                out[i, column] = stacks[i, column] + (re * p + im * q)


def cross(z, offsets, mask, where, stacks, pieces):
    return pl.pallas_call(
        functools.partial(cross_kernel, z, offsets),
        in_specs=[SMEM_SPEC, SMEM_SPEC] + [VMEM_SPEC] * (1 + len(pieces)),
        out_specs=VMEM_SPEC,
        out_shape=jax.ShapeDtypeStruct(stacks.shape, F32),
        compiler_params=params(),
        name="cross",
    )(mask, where, stacks, *pieces)


def shards(traces, station_flags, tile_mask, band_block, stacks):
    tm_count, sta_count = lax.axis_size("tm"), lax.axis_size("sta")
    stations, length = traces.shape
    z = Sizes(stations, length, tm_count, stacks.shape[-1])
    assert sta_count & (sta_count - 1) == 0
    place = lax.axis_index("tm").astype(jnp.int32).reshape(1)
    where = lax.axis_index("sta").astype(jnp.int32).reshape(1)
    sent = transform(z, band_block, place, station_flags, traces)
    got = lax.all_to_all(sent, "tm", split_axis=0, concat_axis=0, tiled=True)
    made = tables(z, band_block, place)
    white = spectrum(z, station_flags, got, made)
    offsets, pieces = [0], [white]
    bit = sta_count // 2
    while bit:
        pairs = [(i, i ^ bit) for i in range(sta_count)]
        pieces += [lax.ppermute(piece, "sta", pairs) for piece in pieces]
        offsets += [offset ^ bit for offset in offsets]
        bit //= 2
    return cross(z, offsets, tile_mask, where, stacks, pieces)


def solution(mesh):
    return jax.shard_map(
        shards,
        mesh=mesh,
        in_specs=(P("sta", "tm"), P("sta"), P(), P(), P("sta", None, None, "tm")),
        out_specs=P("sta", None, None, "tm"),
        check_vma=False,
    )
```

```python
import functools
import math

import jax
import jax.numpy as jnp
import numpy as np
from jax import lax
from jax.experimental import pallas as pl
from jax.experimental.pallas import tpu as pltpu
from jax.sharding import PartitionSpec as P

HALF_WIN = 512
SMOOTH = 32
EPS_MEAN = 1e-06
EPS_POWER = 1e-06
LANES = 128
SPAN = 2 * HALF_WIN
TILES = SPAN // LANES
HALF_TILES = HALF_WIN // LANES
PAD = 16
GROUP = 1
position = lax.axis_index
VMEM_LIMIT = 16 * 1024 * 1024
BF = jnp.bfloat16
F32 = jnp.float32


def up_to(value, step):
    return -(-value // step) * step


def sincos(turns):
    quarter = jnp.round(turns * 4.0)
    rest = turns - quarter * 0.25
    y = rest * (2.0 * math.pi)
    y2 = y * y
    s = y + y * y2 * (-1.0 / 6 + y2 * (1.0 / 120 + y2 * (-1.0 / 5040 + y2 * (1.0 / 362880))))
    c = 1.0 + y2 * (-0.5 + y2 * (1.0 / 24 + y2 * (-1.0 / 720 + y2 * (1.0 / 40320))))
    q = quarter - 4.0 * jnp.floor(quarter * 0.25)
    swap = (q == 1.0) | (q == 3.0)
    sine = jnp.where(swap, c, s)
    cosine = jnp.where(swap, s, c)
    sine = jnp.where(q >= 2.0, -sine, sine)
    cosine = jnp.where((q == 1.0) | (q == 2.0), -cosine, cosine)
    return sine, cosine


def turns_of(product, period):
    whole = jnp.floor(product * (1.0 / period))
    return (product - whole * period) * (1.0 / period)


def split2(value):
    high = value.astype(BF)
    return high, (value - high.astype(F32)).astype(BF)


def iota(shape, axis):
    return lax.broadcasted_iota(jnp.int32, shape, axis)


def iota_f(shape, axis):
    return iota(shape, axis).astype(F32)


def window_tables():
    row, lane = iota((LANES, LANES), 0), iota((LANES, LANES), 1)
    upto = (row <= lane).astype(F32).astype(BF)
    onward = (row >= lane).astype(F32).astype(BF)
    return upto, onward, jnp.ones((LANES, LANES), BF)


def np_split(value):
    high = value.astype(jnp.bfloat16).astype(np.float64)
    return high, (value - high).astype(jnp.bfloat16).astype(np.float64)


class Sizes:
    def __init__(self, stations, length, tm_count, bins):
        self.stations, self.length, self.tm, self.bins = stations, length, tm_count, bins
        self.rows = length // SPAN
        self.half = self.rows // 2 + 1
        self.pad = up_to(self.rows, PAD)
        self.full = self.rows // PAD * PAD
        self.tail = self.rows - self.full
        self.depth = 3 * self.full + PAD
        self.block = min(tm_count, 16)
        self.blocks = tm_count // self.block
        self.folds = -(-(bins + self.rows - 1) // self.rows)
        self.spec_rows = up_to(2 * self.half, 8)
        self.edge_rows = 2 * stations * TILES
        self.sent_rows = self.spec_rows + self.edge_rows
        assert length % SPAN == 0 and tm_count % self.block == 0
        assert stations == 2 and self.folds <= PAD
        assert self.rows >= 2 and 0 < 3 * self.tail <= 8

    def row_order(self):
        j2 = np.arange(self.tm)[:, None] + self.tm * np.arange(self.half)[None, :]
        return j2.reshape(self.blocks, self.block, self.half).transpose(0, 2, 1).reshape(self.blocks, -1)

    def first_table(self):
        j2 = self.row_order()[:, None, :, None]
        tile = np.arange(TILES)[None, :, None, None]
        total = self.tm * self.length
        time = np.arange(self.rows) * SPAN + tile * LANES
        angle = 2.0 * np.pi / total * (j2 * time % total)
        parts = np.concatenate([np.cos(angle), -np.sin(angle)], axis=2)
        high, low = np_split(parts)
        full = self.full
        pieces = [piece[..., :full] for piece in (high, high, low)]
        for piece in (high, high, low):
            rest = piece[..., full:]
            pieces.append(np.pad(rest, ((0, 0), (0, 0), (0, 0), (0, self.tail - rest.shape[-1]))))
        table = np.concatenate(pieces, axis=3)
        gap = ((0, 0), (0, 0), (0, 0), (0, self.depth - table.shape[-1]))
        return np.pad(table, gap).astype(jnp.bfloat16)

    def lane_table(self):
        angle = 2.0 * np.pi / (self.tm * self.length) * (
            self.row_order()[:, :, None] * np.arange(LANES)
        )
        return np.stack([np.cos(angle), -np.sin(angle)], axis=1).astype(np.float32)


def normalize(z, x, xs, sums, stack, edges):
    rows, pad, top = z.rows, z.pad, 8
    short = up_to(rows, 8)
    for a in range(rows):
        xs[:, top + a, :] = x[:, a * SPAN : (a + 1) * SPAN].astype(F32)
    for s in range(z.stations):
        for side, a in ((0, 0), (1, rows - 1)):
            for c in range(TILES):
                at = (side * z.stations + s) * TILES + c
                edges[at : at + 1, :] = xs[s, top + a : top + a + 1, c * LANES : (c + 1) * LANES]
    upto, onward, ones = window_tables()
    kernel = jnp.concatenate([upto, onward, ones], axis=1)
    group = 4
    for s in range(z.stations):
        for c0 in range(0, TILES, group):
            part = jnp.concatenate(
                [
                    jnp.abs(xs[s, top : top + pad, c * LANES : (c + 1) * LANES]).astype(BF)
                    for c in range(c0, c0 + group)
                ],
                axis=0,
            )
            got = jnp.dot(part, kernel, preferred_element_type=F32)
            for k in range(group):
                sums[s, c0 + k, top : top + short, :] = got[k * pad : k * pad + short]
    blank = jnp.zeros((1, HALF_WIN), F32)
    for s in range(z.stations):
        xs[s, top : top + 1, 0:HALF_WIN] = blank
        xs[s, top + rows - 1 : top + rows, HALF_WIN:SPAN] = blank
    for s in range(z.stations):

        def tile(kind, c):
            turn, cc = divmod(c, TILES)
            lines = slice(top + turn, top + turn + short)
            return sums[s, cc, lines, kind * LANES : (kind + 1) * LANES]

        ones_ = [tile(2, c) for c in range(1 - HALF_TILES, TILES + HALF_TILES - 1)]
        twos = [ones_[c] + ones_[c + 1] for c in range(len(ones_) - 1)]
        for c in range(TILES):
            inner = (twos[c] + twos[c + 2]) + (twos[c + 4] + ones_[c + 6])
            total = inner + (tile(1, c - HALF_TILES) + tile(0, c + HALF_TILES))
            value = xs[s, top : top + short, c * LANES : (c + 1) * LANES]
            value = value / (total * (1.0 / (2 * HALF_WIN + 1)) + EPS_MEAN)
            high, low = split2(value[: z.full])
            lanes = slice((c * z.stations + s) * LANES, (c * z.stations + s + 1) * LANES)
            for k, part in enumerate((high, low, high)):
                stack[k * z.full : (k + 1) * z.full, lanes] = part
            rest = value[z.full :]
            high = rest.astype(BF).astype(F32)
            rest = high + pltpu.roll(rest - high, z.tail, 0) + pltpu.roll(high, 2 * z.tail, 0)
            rest = jnp.concatenate([rest, jnp.zeros((PAD - rest.shape[0], LANES), F32)], axis=0)
            stack[3 * z.full :, lanes] = rest.astype(BF)


def fold_waves(fold):
    lane = iota((PAD, SPAN), 1)
    for kind in range(2):
        turns = jnp.bitwise_and((iota((PAD, SPAN), 0) + kind) * lane, SPAN - 1).astype(F32)
        sine, cosine = sincos(turns * (1.0 / SPAN))
        fold[kind, 0] = cosine
        fold[kind, 1] = sine


def fold_weights(z, base, fold, weight):
    spot = iota((TILES, LANES), 0) * LANES + iota((TILES, LANES), 1)
    turns = jnp.bitwise_and((base // z.rows) * spot, SPAN - 1).astype(F32)
    sine, cosine = sincos(turns * (1.0 / SPAN))
    b_cos = jnp.concatenate([cosine[c : c + 1] for c in range(TILES)], axis=1)
    b_sin = jnp.concatenate([sine[c : c + 1] for c in range(TILES)], axis=1)
    for kind in range(2):
        w_cos, w_sin = fold[kind, 0], fold[kind, 1]
        sine = w_sin * b_cos + w_cos * b_sin
        cosine = w_cos * b_cos - w_sin * b_sin
        for h, (s, c) in enumerate(zip(split2(sine), split2(cosine))):
            table = ((c, s), (-s, c)) if kind == 0 else ((c, -s), (-s, -c))
            for part in range(2):
                at = h * 4 * PAD + kind * 2 * PAD + part * PAD
                for tile in range(TILES):
                    for side in range(2):
                        to = (2 * tile + side) * LANES
                        weight[at : at + PAD, to : to + LANES] = table[part][side][
                            :, tile * LANES : (tile + 1) * LANES
                        ]


def transform_kernel(
    z, band, flags, x, first, lanes_table, out,
    band_s, flags_s, x_v, first_v, lanes_v, xs, sums, stack, edges, fold, weight, acc, both, spec, sems,
):
    half, block, tm = z.half, z.block, z.tm
    height = half * block
    index = pl.program_id(0)
    top, rows, pad = 8, z.rows, z.pad

    get_first = pltpu.make_async_copy(first.at[index], first_v, sems.at[3])
    get_lanes = pltpu.make_async_copy(lanes_table.at[index], lanes_v, sems.at[4])

    def prologue():
        copies = [
            pltpu.make_async_copy(band, band_s, sems.at[0]),
            pltpu.make_async_copy(flags, flags_s, sems.at[1]),
            pltpu.make_async_copy(x, x_v, sems.at[2]),
        ]
        for copy in copies:
            copy.start()
        get_lanes.start()
        get_first.start()
        full = rows // 8 * 8
        for s in range(z.stations):
            xs[s, top + full : top + pad, :] = jnp.zeros((pad - full, SPAN), F32)
            for c in range(TILES):
                sums[s, c, 0:top, :] = jnp.zeros((top, 3 * LANES), F32)
                sums[s, c, top + up_to(rows, 8) :, :] = jnp.zeros((8, 3 * LANES), F32)
        spec[:, z.spec_rows - 8 : z.spec_rows, :] = jnp.zeros((tm, 8, LANES), F32)
        fold_waves(fold)
        for copy in copies:
            copy.wait()
        fold_weights(z, band_s[0, 0], fold, weight)
        normalize(z, x_v, xs, sums, stack, edges)

    if z.blocks == 1:
        prologue()
    else:
        pl.when(index == 0)(prologue)

        @pl.when(index > 0)
        def _():
            get_lanes.start()
            get_first.start()

    get_lanes.wait()
    residue = index * block + iota((block, LANES), 0)
    sine, cosine = sincos(turns_of((position("tm") * residue).astype(F32), tm))
    l_re = lanes_v[0].reshape(half, block, LANES)
    l_im = lanes_v[1].reshape(half, block, LANES)
    t_re = (l_re * cosine[None] + l_im * sine[None]).reshape(height, LANES)
    t_im = (l_im * cosine[None] - l_re * sine[None]).reshape(height, LANES)
    get_first.wait()
    wide_lanes = z.stations * LANES

    def first_stage(c):
        return jnp.dot(
            first_v[c],
            stack[:, c * wide_lanes : (c + 1) * wide_lanes],
            preferred_element_type=F32,
        )

    def second_stage(c0, parts):
        w = weight[:, 2 * c0 * LANES : 2 * (c0 + GROUP) * LANES]
        for s in range(z.stations):
            left = jnp.concatenate([jnp.concatenate(piece, axis=1) for piece in parts[s]], axis=0)
            got = lax.dot_general(left, w, (((1,), (1,)), ((), ())), preferred_element_type=F32)
            value = got[:height] + got[height:]
            acc[s] = value if c0 == 0 else acc[s] + value

    waiting = None
    coming = [first_stage(c) for c in range(GROUP)]
    for c0 in range(0, TILES, GROUP):
        current = coming
        parts = [[[], []] for _ in range(z.stations)]
        for f in current:
            for s in range(z.stations):
                f_re = f[:height, s * LANES : (s + 1) * LANES]
                f_im = f[height:, s * LANES : (s + 1) * LANES]
                for value in (f_re * t_re - f_im * t_im, f_re * t_im + f_im * t_re):
                    high, low = split2(value)
                    parts[s][0].append(high)
                    parts[s][1].append(low)
        if c0 + GROUP < TILES:
            coming = [first_stage(c) for c in range(c0 + GROUP, c0 + 2 * GROUP)]
        if waiting is not None:
            second_stage(c0 - GROUP, waiting)
        waiting = parts
    second_stage(TILES - GROUP, waiting)
    zero, one = (
        (acc[s] + pltpu.roll(acc[s], LANES // 2, 1)) * flags_s[s].astype(F32) for s in range(2)
    )
    lane = iota((height, LANES), 1)
    early = jnp.bitwise_and(lane, LANES // 2 - 1) < LANES // 4
    direct = jnp.where(early, zero, pltpu.roll(one, LANES // 4, 1))
    mirror = jnp.where(early, pltpu.roll(zero, LANES // 4, 1), one)
    for kind, value in enumerate((direct, mirror)):
        high = value.astype(BF).astype(F32)
        both[kind] = jnp.where(lane < LANES // 2, high, value - high)
    for k in range(block):
        here = index * block + k
        there = jnp.where(here == 0, 0, tm - here) if z.blocks > 1 else (tm - k) % tm
        here = here if z.blocks > 1 else k
        lines = pl.ds(k, half, stride=block)
        spec[here, 0:half, :] = both[0, lines, :]
        spec[there, half : 2 * half, :] = both[1, lines, :]

    def finish():
        ends = edges[...].astype(BF)

        def one_row(k, carry):
            out[k, 0 : z.spec_rows, :] = spec[k].astype(BF)
            out[k, z.spec_rows : z.sent_rows, :] = ends
            return carry

        if z.blocks == 1:
            for k in range(tm):
                one_row(k, 0)
        else:
            lax.fori_loop(0, tm, one_row, 0)

    if z.blocks == 1:
        finish()
    else:
        pl.when(index == z.blocks - 1)(finish)


SMEM_SPEC = pl.BlockSpec(memory_space=pltpu.SMEM)
VMEM_SPEC = pl.BlockSpec(memory_space=pltpu.VMEM)
HBM_SPEC = pl.BlockSpec(memory_space=pltpu.HBM)


def params():
    return pltpu.CompilerParams(vmem_limit_bytes=VMEM_LIMIT)


def transform(z, band, flags, x):
    band = band.reshape(1, 1)
    height = z.half * z.block
    first, lanes = z.first_table(), z.lane_table()
    return pl.pallas_call(
        functools.partial(transform_kernel, z),
        grid=(z.blocks,),
        in_specs=[HBM_SPEC] * 5,
        out_specs=VMEM_SPEC,
        out_shape=jax.ShapeDtypeStruct((z.tm, z.sent_rows, LANES), BF),
        scratch_shapes=[
            pltpu.SMEM((1, 1), jnp.int32),
            pltpu.SMEM((z.stations,), jnp.int32),
            pltpu.VMEM(x.shape, BF),
            pltpu.VMEM(first.shape[1:], BF),
            pltpu.VMEM(lanes.shape[1:], F32),
            pltpu.VMEM((z.stations, 8 + z.pad, SPAN), F32),
            pltpu.VMEM((z.stations, TILES, 16 + up_to(z.rows, 8), 3 * LANES), F32),
            pltpu.VMEM((z.depth, z.stations * SPAN), BF),
            pltpu.VMEM((z.edge_rows, LANES), F32),
            pltpu.VMEM((2, 2, PAD, SPAN), F32),
            pltpu.VMEM((LANES, 2 * SPAN), BF),
            pltpu.VMEM((z.stations, height, LANES), F32),
            pltpu.VMEM((2, height, LANES), F32),
            pltpu.VMEM((z.tm, z.spec_rows, LANES), F32),
            pltpu.SemaphoreType.DMA((5,)),
        ],
        name="transform",
    )(band, flags, x, jnp.asarray(first), jnp.asarray(lanes))


def table_kernel(
    z, band, flags, choose, keep, steps, turns, near, phase, switch, band_s, flags_s, sems
):
    rows, tm, bins, half = z.rows, z.tm, z.bins, z.half
    copies = [
        pltpu.make_async_copy(band, band_s, sems.at[0]),
        pltpu.make_async_copy(flags, flags_s, sems.at[1]),
    ]
    for copy in copies:
        copy.start()
    for copy in copies:
        copy.wait()
    base, residue = band_s[0, 0], position("tm")
    for s in range(z.stations):
        switch[s] = jnp.full((TILES, LANES), flags_s[s].astype(F32))
    spot = iota_f((1, bins), 1) + (base % rows).astype(F32)
    fold = jnp.floor((spot + 0.5) * (1.0 / rows))
    rest = spot - fold * rows
    row = iota_f((z.spec_rows, bins), 0)
    last = (rows - 1 + half + (residue == 0).astype(jnp.int32)).astype(F32)
    mirror = last - row
    target = jnp.where(row < half, row, jnp.where(mirror >= half, mirror, -1.0))
    one = (target == rest).astype(F32).astype(BF)
    for p in range(tm):
        choose[p] = one
    keep[...] = (iota_f((PAD, bins), 0) == fold).astype(F32)
    freq = (residue + tm * (base + iota((1, bins), 1))).astype(F32)
    step = iota_f((TILES, bins), 0) - HALF_TILES
    sine, cosine = sincos(turns_of(step * freq, tm * (z.length // LANES)))
    table = jnp.concatenate(
        [jnp.concatenate([cosine, -sine], axis=1), jnp.concatenate([sine, cosine], axis=1)], axis=0
    )
    high, low = split2(table)
    for k, part in enumerate((high, high, low, low)):
        steps[k * 2 * TILES : (k + 1) * 2 * TILES, :] = part
    sine, cosine = sincos(turns_of(iota_f((LANES, bins), 0) * freq, tm * z.length))
    turns[0] = cosine
    turns[1] = sine
    gap = jnp.abs(iota((bins, bins), 0) - iota((bins, bins), 1))
    near[...] = (gap <= SMOOTH).astype(F32).astype(BF)
    p_sin, p_cos = sincos(turns_of((residue * iota((tm, LANES), 0)).astype(F32), tm))
    phase[0] = p_cos
    phase[1] = -p_sin


def tables(z, band, flags):
    return pl.pallas_call(
        functools.partial(table_kernel, z),
        in_specs=[HBM_SPEC, HBM_SPEC],
        out_specs=[VMEM_SPEC] * 7,
        scratch_shapes=[
            pltpu.SMEM((1, 1), jnp.int32),
            pltpu.SMEM((z.stations,), jnp.int32),
            pltpu.SemaphoreType.DMA((2,)),
        ],
        out_shape=[
            jax.ShapeDtypeStruct((z.tm, z.spec_rows, z.bins), BF),
            jax.ShapeDtypeStruct((PAD, z.bins), F32),
            jax.ShapeDtypeStruct((8 * TILES, 2 * z.bins), BF),
            jax.ShapeDtypeStruct((2, LANES, z.bins), F32),
            jax.ShapeDtypeStruct((z.bins, z.bins), BF),
            jax.ShapeDtypeStruct((2, z.tm, LANES), F32),
            jax.ShapeDtypeStruct((z.stations, TILES, LANES), F32),
        ],
        compiler_params=params(),
        cost_estimate=pl.CostEstimate(flops=4000000, bytes_accessed=2000000, transcendentals=0),
        name="tables",
    )(band.reshape(1, 1), flags)


def sublane_sums(value, row):
    total = value
    for shift in (1, 2, 4):
        total = total + jnp.where(row >= shift, pltpu.roll(total, shift, 0), 0.0)
    return total - value, total


def spectrum_kernel(z, got, choose, keep, steps, turns, near, phase, switch, out):
    tm, bins, at = z.tm, z.bins, z.spec_rows
    parts = got[:, 0:at, :].astype(F32).reshape(tm * at, LANES).astype(BF)
    weights = choose[...].astype(F32).reshape(tm * at, bins).astype(BF)
    placed = lax.dot_general(parts, weights, (((0,), (0,)), ((), ())), preferred_element_type=F32)
    mask = keep[...]
    folded = [
        jnp.sum(placed[k * PAD : (k + 1) * PAD] * mask, axis=0, keepdims=True)
        for k in range(4 * z.stations)
    ]
    spec = [folded[k] + folded[k + 2 * z.stations] for k in range(2 * z.stations)]
    upto, onward, ones = window_tables()
    row = iota((TILES, LANES), 0)
    late = row >= HALF_TILES
    sides = []
    side_rows = z.stations * TILES
    for side, table in ((0, upto), (1, onward)):
        rows = slice(at + side * side_rows, at + (side + 1) * side_rows)
        value = got[:, rows, :].astype(F32).reshape(tm * side_rows, LANES)
        sums = jnp.dot(
            jnp.abs(value).astype(BF),
            jnp.concatenate([table, ones], axis=1),
            preferred_element_type=F32,
        )
        sides.append((value, sums))
    mixed = []
    for s in range(z.stations):
        real = jnp.zeros((TILES, LANES), F32)
        imag = jnp.zeros((TILES, LANES), F32)
        flag = switch[s]
        for p in range(tm):
            begin = (p * z.stations + s) * TILES
            before = ((p - 1) % tm * z.stations + s) * TILES
            value_r, sums_r = (v[begin : begin + TILES] for v in sides[0])
            value_l, sums_l = (v[before : before + TILES] for v in sides[1])
            earlier, _ = sublane_sums(sums_r[:, LANES:], row)
            right = sums_r[:, :LANES] + earlier
            tail = sums_l[:, LANES:]
            for shift in (1, 2, 4):
                tail = tail + jnp.where(row < TILES - shift, pltpu.roll(tail, TILES - shift, 0), 0.0)
            left = sums_l[:, :LANES] + jnp.where(
                row < TILES - 1, pltpu.roll(tail, TILES - 1, 0), 0.0
            )
            total = left + right if p else jnp.where(late, right, left)
            sample = pltpu.roll(jnp.where(late, value_l, value_r), HALF_TILES, 0)
            value = flag * sample / (total * (1.0 / (2 * HALF_WIN + 1)) + EPS_MEAN)
            real = real + value * phase[0, p : p + 1, :]
            imag = imag + value * phase[1, p : p + 1, :]
        mixed.append(jnp.concatenate([real, imag], axis=0))
    high, low = split2(jnp.concatenate(mixed, axis=1))
    spread = lax.dot_general(
        jnp.concatenate([high, low, high, low], axis=0),
        steps[...],
        (((0,), (0,)), ((), ())),
        preferred_element_type=F32,
    )
    cosine, sine = turns[0], turns[1]
    pieces = []
    for s in range(z.stations):
        g_re = spread[s * LANES : (s + 1) * LANES, :bins]
        g_im = spread[s * LANES : (s + 1) * LANES, bins:]
        spec[2 * s] += jnp.sum(g_re * cosine + g_im * sine, axis=0, keepdims=True)
        spec[2 * s + 1] += jnp.sum(g_im * cosine - g_re * sine, axis=0, keepdims=True)
        power = spec[2 * s] * spec[2 * s] + spec[2 * s + 1] * spec[2 * s + 1]
        for _ in range(3):
            part = power.astype(BF).astype(F32)
            pieces.append(part)
            power = power - part
    pieces.append(jnp.zeros((8 - len(pieces), bins), F32))
    smooth = jnp.dot(
        jnp.concatenate(pieces, axis=0).astype(BF), near[...], preferred_element_type=F32
    )
    for s in range(z.stations):
        mean = smooth[3 * s : 3 * s + 1] + smooth[3 * s + 1 : 3 * s + 2] + smooth[3 * s + 2 : 3 * s + 3]
        scale = 1.0 / jnp.sqrt(mean * (1.0 / (2 * SMOOTH + 1)) + EPS_POWER)
        out[2 * s : 2 * s + 1, :] = spec[2 * s] * scale
        out[2 * s + 1 : 2 * s + 2, :] = spec[2 * s + 1] * scale


def spectrum(z, got, made):
    return pl.pallas_call(
        functools.partial(spectrum_kernel, z),
        in_specs=[VMEM_SPEC] * 8,
        out_specs=VMEM_SPEC,
        out_shape=jax.ShapeDtypeStruct((2 * z.stations, z.bins), F32),
        compiler_params=params(),
        name="spectrum",
    )(got, *made)


def cross_kernel(z, offsets, mask, stacks, *refs):
    pieces, out = refs[:-1], refs[-1]
    here = position("sta")
    mine = pieces[0][...]
    bins = z.bins
    sides = []
    for i in range(z.stations):
        re, im = mine[2 * i : 2 * i + 1], mine[2 * i + 1 : 2 * i + 2]
        sides.append((jnp.concatenate([re, im], axis=0), jnp.concatenate([im, -re], axis=0)))
    for offset, piece in zip(offsets, pieces):
        source = here ^ offset
        on = mask[here, source].astype(F32)
        for j in range(z.stations):
            re = jnp.broadcast_to(piece[2 * j : 2 * j + 1, :] * on, (2, bins))
            im = jnp.broadcast_to(piece[2 * j + 1 : 2 * j + 2, :] * on, (2, bins))
            column = source * z.stations + j
            for i, (p, q) in enumerate(sides):
                out[i, column] = stacks[i, column] + (re * p + im * q)


def cross(z, offsets, mask, stacks, pieces):
    return pl.pallas_call(
        functools.partial(cross_kernel, z, offsets),
        in_specs=[SMEM_SPEC] + [VMEM_SPEC] * (1 + len(pieces)),
        out_specs=VMEM_SPEC,
        out_shape=jax.ShapeDtypeStruct(stacks.shape, F32),
        compiler_params=params(),
        name="cross",
    )(mask, stacks, *pieces)


def shards(traces, station_flags, tile_mask, band_block, stacks):
    tm_count, sta_count = lax.axis_size("tm"), lax.axis_size("sta")
    stations, length = traces.shape
    z = Sizes(stations, length, tm_count, stacks.shape[-1])
    assert sta_count & (sta_count - 1) == 0
    sent = transform(z, band_block, station_flags, traces)
    got = lax.all_to_all(sent, "tm", split_axis=0, concat_axis=0, tiled=True)
    made = tables(z, band_block, station_flags)
    white = spectrum(z, got, made)
    offsets, pieces = [0], [white]
    bit = sta_count // 2
    while bit:
        pairs = [(i, i ^ bit) for i in range(sta_count)]
        pieces += [lax.ppermute(piece, "sta", pairs) for piece in pieces]
        offsets += [offset ^ bit for offset in offsets]
        bit //= 2
    return cross(z, offsets, tile_mask, stacks, pieces)


def solution(mesh):
    return jax.shard_map(
        shards,
        mesh=mesh,
        in_specs=(P("sta", "tm"), P("sta"), P(), P(), P("sta", None, None, "tm")),
        out_specs=P("sta", None, None, "tm"),
        check_vma=False,
    )
```

```python
import functools
import math

import jax
import jax.numpy as jnp
import numpy as np
from jax import lax
from jax.experimental import pallas as pl
from jax.experimental.pallas import tpu as pltpu
from jax.sharding import PartitionSpec as P

HALF_WIN = 512
SMOOTH = 32
EPS_MEAN = 1e-06
EPS_POWER = 1e-06
LANES = 128
SPAN = 2 * HALF_WIN
TILES = SPAN // LANES
HALF_TILES = HALF_WIN // LANES
PAD = 16
BAND_TOP = 137
WIDTH = 2 * LANES
CHUNKS = SPAN // WIDTH
position = lax.axis_index
VMEM_LIMIT = 16 * 1024 * 1024
BF = jnp.bfloat16
F32 = jnp.float32


def up_to(value, step):
    return -(-value // step) * step


def sincos(turns):
    quarter = jnp.round(turns * 4.0)
    rest = turns - quarter * 0.25
    y = rest * (2.0 * math.pi)
    y2 = y * y
    s = y + y * y2 * (-1.0 / 6 + y2 * (1.0 / 120 + y2 * (-1.0 / 5040 + y2 * (1.0 / 362880))))
    c = 1.0 + y2 * (-0.5 + y2 * (1.0 / 24 + y2 * (-1.0 / 720 + y2 * (1.0 / 40320))))
    q = quarter - 4.0 * jnp.floor(quarter * 0.25)
    swap = (q == 1.0) | (q == 3.0)
    sine = jnp.where(swap, c, s)
    cosine = jnp.where(swap, s, c)
    sine = jnp.where(q >= 2.0, -sine, sine)
    cosine = jnp.where((q == 1.0) | (q == 2.0), -cosine, cosine)
    return sine, cosine


def turns_of(product, period):
    whole = jnp.floor(product * (1.0 / period))
    return (product - whole * period) * (1.0 / period)


def split2(value):
    high = value.astype(BF)
    return high, (value - high.astype(F32)).astype(BF)


def iota(shape, axis):
    return lax.broadcasted_iota(jnp.int32, shape, axis)


def iota_f(shape, axis):
    return iota(shape, axis).astype(F32)


def window_tables():
    row, lane = iota((LANES, LANES), 0), iota((LANES, LANES), 1)
    upto = (row <= lane).astype(F32).astype(BF)
    onward = (row >= lane).astype(F32).astype(BF)
    return upto, onward, jnp.ones((LANES, LANES), BF)


def np_split(value):
    high = value.astype(jnp.bfloat16).astype(np.float64)
    return high, (value - high).astype(jnp.bfloat16).astype(np.float64)


class Sizes:
    def __init__(self, stations, length, tm_count, bins):
        self.stations, self.length, self.tm, self.bins = stations, length, tm_count, bins
        self.rows = length // SPAN
        self.half = self.rows // 2 + 1
        self.pad = up_to(self.rows, PAD)
        self.full = self.rows // PAD * PAD
        self.tail = self.rows - self.full
        self.depth = 3 * self.full + PAD
        self.block = min(tm_count, 16)
        self.blocks = tm_count // self.block
        self.folds = (BAND_TOP + bins - 1) // self.rows + 1
        self.spec_rows = up_to(2 * self.half, 8)
        self.edge_rows = 2 * stations * TILES
        self.sent_rows = self.spec_rows + self.edge_rows
        assert length % SPAN == 0 and tm_count % self.block == 0
        assert stations == 2 and self.folds <= PAD
        assert self.rows >= 2 and 0 < 3 * self.tail <= 8 and self.depth <= LANES

    def row_order(self):
        j2 = np.arange(self.tm)[:, None] + self.tm * np.arange(self.half)[None, :]
        return j2.reshape(self.blocks, self.block, self.half).transpose(0, 2, 1).reshape(self.blocks, -1)

    def first_table(self):
        period = self.tm * self.rows
        angle = 2.0 * np.pi / period * (self.row_order()[:, :, None] * np.arange(self.rows) % period)
        parts = np.concatenate([np.cos(angle), -np.sin(angle)], axis=1)
        full, rest = parts[..., : self.full], parts[..., self.full :]
        table = np.concatenate([full, full, full, rest, rest, rest], axis=2)
        return np.pad(table, ((0, 0), (0, 0), (0, LANES - table.shape[2]))).astype(np.float32)

    def low_lanes(self, lane):
        at = 3 * self.full
        third = (lane >= 2 * self.full) & (lane < at)
        return third | ((lane >= at + 2 * self.tail) & (lane < at + 3 * self.tail))

    def turn_table(self):
        order = self.row_order().reshape(self.blocks, 1, -1, 1)
        time = np.arange(SPAN).reshape(CHUNKS, 1, WIDTH)
        angle = 2.0 * np.pi / (self.tm * self.length) * (order * time)
        return np.stack([np.cos(angle), -np.sin(angle)], axis=2).astype(np.float32)


def unpack(z, x, xs, edges):
    rows, top = z.rows, 8
    for a in range(rows):
        xs[:, top + a, :] = x[:, a * SPAN : (a + 1) * SPAN].astype(F32)
    for s in range(z.stations):
        for side, a in ((0, 0), (1, rows - 1)):
            for c in range(TILES):
                at = (side * z.stations + s) * TILES + c
                edges[at : at + 1, :] = xs[s, top + a : top + a + 1, c * LANES : (c + 1) * LANES]


def window(z, s, xs, sums):
    rows, pad, top = z.rows, z.pad, 8
    short = up_to(rows, 8)
    kernel = jnp.concatenate(window_tables()[:2], axis=1)
    group = 4
    for c0 in range(0, TILES, group):
        parts = [
            jnp.abs(xs[s, top : top + pad, c * LANES : (c + 1) * LANES])
            for c in range(c0, c0 + group)
        ]
        part = jnp.concatenate([part.astype(BF) for part in parts], axis=0)
        got = jnp.dot(part, kernel, preferred_element_type=F32)
        for k in range(group):
            value = got[k * pad : k * pad + short]
            upto, onward = value[:, :LANES], value[:, LANES:]
            sums[s, c0 + k, top : top + short, 0 : 2 * LANES] = value
            sums[s, c0 + k, top : top + short, 2 * LANES :] = upto + (onward - parts[k][:short])
    blank = jnp.zeros((1, HALF_WIN), F32)
    xs[s, top : top + 1, 0:HALF_WIN] = blank
    xs[s, top + rows - 1 : top + rows, HALF_WIN:SPAN] = blank


def level(z, s, tiles, xs, sums, stack):
    rows, top = z.rows, 8
    short = up_to(rows, 8)

    def tile(kind, c):
        turn, cc = divmod(c, TILES)
        lines = slice(top + turn, top + turn + short)
        return sums[s, cc, lines, kind * LANES : (kind + 1) * LANES]

    first = tiles[0] + 1 - HALF_TILES
    single = [tile(2, c) for c in range(first, tiles[-1] + HALF_TILES)]
    twos = [single[c] + single[c + 1] for c in range(len(single) - 1)]
    for k, c in enumerate(tiles):
        inner = (twos[k] + twos[k + 2]) + (twos[k + 4] + single[k + 6])
        total = inner + (tile(1, c - HALF_TILES) + tile(0, c + HALF_TILES))
        value = xs[s, top : top + short, c * LANES : (c + 1) * LANES]
        value = value / (total * (1.0 / (2 * HALF_WIN + 1)) + EPS_MEAN)
        high, low = split2(value[: z.full])
        lanes = slice(c * LANES, (c + 1) * LANES)
        for k2, part in enumerate((high, low, high)):
            stack[s, k2 * z.full : (k2 + 1) * z.full, lanes] = part
        rest = value[z.full :]
        high = rest.astype(BF).astype(F32)
        rest = high + pltpu.roll(rest - high, z.tail, 0) + pltpu.roll(high, 2 * z.tail, 0)
        rest = jnp.concatenate([rest, jnp.zeros((PAD - rest.shape[0], LANES), F32)], axis=0)
        stack[s, 3 * z.full :, lanes] = rest.astype(BF)


def fold_weights(weight):
    lane = iota((PAD, SPAN), 1)
    for kind in range(2):
        turns = jnp.bitwise_and((iota((PAD, SPAN), 0) + kind) * lane, SPAN - 1).astype(F32)
        sine, cosine = sincos(turns * (1.0 / SPAN))
        for h, (s, c) in enumerate(zip(split2(sine), split2(cosine))):
            table = ((c, s), (-s, c)) if kind == 0 else ((c, -s), (-s, -c))
            for part in range(2):
                at = h * 4 * PAD + kind * 2 * PAD + part * PAD
                for side in range(2):
                    for g in range(CHUNKS):
                        to = (2 * g + side) * WIDTH
                        weight[at : at + PAD, to : to + WIDTH] = table[part][side][
                            :, g * WIDTH : (g + 1) * WIDTH
                        ]


def transform_kernel(
    z, flags, x, first, turn, out,
    flags_s, x_v, first_v, turn_v, table, xs, sums, stack, edges, weight, acc, both, spec, sems,
):
    half, block, tm = z.half, z.block, z.tm
    height = half * block
    index = pl.program_id(0)
    top, rows, pad = 8, z.rows, z.pad
    get_first = pltpu.make_async_copy(first.at[index], first_v, sems.at[2])
    get_turn = [
        pltpu.make_async_copy(turn.at[index, g], turn_v.at[g], sems.at[3 + g]) for g in range(CHUNKS)
    ]

    def prologue():
        copies = [
            pltpu.make_async_copy(x, x_v, sems.at[0]),
            pltpu.make_async_copy(flags, flags_s, sems.at[1]),
        ]
        for copy in copies + [get_first] + get_turn:
            copy.start()
        full = rows // 8 * 8
        for s in range(z.stations):
            xs[s, top + full : top + pad, :] = jnp.zeros((pad - full, SPAN), F32)
            for c in range(TILES):
                sums[s, c, 0:top, :] = jnp.zeros((top, 3 * LANES), F32)
                sums[s, c, top + up_to(rows, 8) :, :] = jnp.zeros((8, 3 * LANES), F32)
        spec[:, z.spec_rows - 8 : z.spec_rows, :] = jnp.zeros((tm, 8, LANES), F32)
        fold_weights(weight)
        for copy in copies:
            copy.wait()
        unpack(z, x_v, xs, edges)
        for s in range(z.stations):
            window(z, s, xs, sums)
            if s == 0 or z.blocks > 1:
                level(z, s, range(TILES), xs, sums, stack)

    if z.blocks == 1:
        prologue()
    else:
        pl.when(index == 0)(prologue)

        @pl.when(index > 0)
        def _():
            for copy in [get_first] + get_turn:
                copy.start()

    for copy in [get_first] + get_turn:
        copy.wait()
    residue = index * block + iota((block, LANES), 0)
    sine, cosine = sincos(turns_of((position("tm") * residue).astype(F32), tm))
    f_re = first_v[:height].reshape(half, block, LANES)
    f_im = first_v[height:].reshape(half, block, LANES)
    low = z.low_lanes(iota((height, LANES), 1))
    for k, value in enumerate(
        (f_re * cosine[None] + f_im * sine[None], f_im * cosine[None] - f_re * sine[None])
    ):
        value = value.reshape(height, LANES)
        high = value.astype(BF).astype(F32)
        table[k * height : (k + 1) * height, :] = jnp.where(low, value - high, high).astype(BF)

    def first_stage(s, g):
        return jnp.dot(
            table[:, : z.depth],
            stack[s, :, g * WIDTH : (g + 1) * WIDTH],
            preferred_element_type=F32,
        )

    def second_stage(s, g, parts):
        w = weight[:, 2 * g * WIDTH : 2 * (g + 1) * WIDTH]
        got = lax.dot_general(parts, w, (((1,), (1,)), ((), ())), preferred_element_type=F32)
        value = got[:height] + got[height:]
        acc[s] = value if g == 0 else acc[s] + value

    def settle(s):
        value = acc[s] + pltpu.roll(acc[s], LANES // 2, 1)
        return value * flags_s[s].astype(F32)

    steps = [(s, g) for s in range(z.stations) for g in range(CHUNKS)]
    coming = first_stage(*steps[0])
    waiting = None
    for k, (s, g) in enumerate(steps):
        f_re, f_im = coming[:height], coming[height:]
        t_re, t_im = turn_v[g, 0], turn_v[g, 1]
        re_h, re_l = split2(f_re * t_re - f_im * t_im)
        im_h, im_l = split2(f_re * t_im + f_im * t_re)
        parts = jnp.concatenate(
            [jnp.concatenate([re_h, im_h], axis=1), jnp.concatenate([re_l, im_l], axis=1)], axis=0
        )
        if s == 0 and z.blocks == 1:
            level(z, 1, range(2 * g, 2 * g + 2), xs, sums, stack)
        if k + 1 < len(steps):
            coming = first_stage(*steps[k + 1])
        if waiting is not None:
            second_stage(*steps[k - 1], waiting)
        waiting = parts
    second_stage(*steps[-1], waiting)
    zero, one = settle(0), settle(1)
    lane = iota((height, LANES), 1)
    early = jnp.bitwise_and(lane, LANES // 2 - 1) < LANES // 4
    direct = jnp.where(early, zero, pltpu.roll(one, LANES // 4, 1))
    mirror = jnp.where(early, pltpu.roll(zero, LANES // 4, 1), one)
    for kind, value in enumerate((direct, mirror)):
        high = value.astype(BF).astype(F32)
        both[kind] = jnp.where(lane < LANES // 2, high, value - high)
    for k in range(block):
        here = index * block + k
        there = jnp.where(here == 0, 0, tm - here) if z.blocks > 1 else (tm - k) % tm
        here = here if z.blocks > 1 else k
        lines = pl.ds(k, half, stride=block)
        spec[here, 0:half, :] = both[0, lines, :]
        spec[there, half : 2 * half, :] = both[1, lines, :]

    def finish():
        ends = edges[...].astype(BF)

        def one_row(k, carry):
            out[k, 0 : z.spec_rows, :] = spec[k].astype(BF)
            out[k, z.spec_rows : z.sent_rows, :] = ends
            return carry

        if z.blocks == 1:
            for k in range(tm):
                one_row(k, 0)
        else:
            lax.fori_loop(0, tm, one_row, 0)

    if z.blocks == 1:
        finish()
    else:
        pl.when(index == z.blocks - 1)(finish)


SMEM_SPEC = pl.BlockSpec(memory_space=pltpu.SMEM)
VMEM_SPEC = pl.BlockSpec(memory_space=pltpu.VMEM)
HBM_SPEC = pl.BlockSpec(memory_space=pltpu.HBM)


def params():
    return pltpu.CompilerParams(vmem_limit_bytes=VMEM_LIMIT)


def transform(z, flags, x):
    height = z.half * z.block
    first, turn = z.first_table(), z.turn_table()
    return pl.pallas_call(
        functools.partial(transform_kernel, z),
        grid=(z.blocks,),
        in_specs=[HBM_SPEC] * 4,
        out_specs=VMEM_SPEC,
        out_shape=jax.ShapeDtypeStruct((z.tm, z.sent_rows, LANES), BF),
        scratch_shapes=[
            pltpu.SMEM((z.stations,), jnp.int32),
            pltpu.VMEM(x.shape, BF),
            pltpu.VMEM(first.shape[1:], F32),
            pltpu.VMEM(turn.shape[1:], F32),
            pltpu.VMEM(first.shape[1:], BF),
            pltpu.VMEM((z.stations, 8 + z.pad, SPAN), F32),
            pltpu.VMEM((z.stations, TILES, 16 + up_to(z.rows, 8), 3 * LANES), F32),
            pltpu.VMEM((z.stations, z.depth, SPAN), BF),
            pltpu.VMEM((z.edge_rows, LANES), F32),
            pltpu.VMEM((LANES, 2 * SPAN), BF),
            pltpu.VMEM((z.stations, height, LANES), F32),
            pltpu.VMEM((2, height, LANES), F32),
            pltpu.VMEM((z.tm, z.spec_rows, LANES), F32),
            pltpu.SemaphoreType.DMA((3 + CHUNKS,)),
        ],
        name="transform",
    )(flags, x, jnp.asarray(first), jnp.asarray(turn))


def table_kernel(
    z, offsets, band, flags, mask, choose, keep, steps, turns, near, phase, switch, pairs,
    band_s, flags_s, mask_s, sems,
):
    rows, tm, bins, half = z.rows, z.tm, z.bins, z.half
    copies = [
        pltpu.make_async_copy(band, band_s, sems.at[0]),
        pltpu.make_async_copy(flags, flags_s, sems.at[1]),
        pltpu.make_async_copy(mask, mask_s, sems.at[2]),
    ]
    for copy in copies:
        copy.start()
    for copy in copies:
        copy.wait()
    here = position("sta")
    for k, offset in enumerate(offsets):
        pairs[k] = jnp.full((2, LANES), mask_s[here, here ^ offset].astype(F32))
    base, residue = band_s[0, 0], position("tm")
    for s in range(z.stations):
        switch[s] = jnp.full((TILES, LANES), flags_s[s].astype(F32))
    spot = iota_f((1, bins), 1) + base.astype(F32)
    fold = jnp.floor((spot + 0.5) * (1.0 / rows))
    rest = spot - fold * rows
    row = iota_f((z.spec_rows, bins), 0)
    last = (rows - 1 + half + (residue == 0).astype(jnp.int32)).astype(F32)
    mirror = last - row
    target = jnp.where(row < half, row, jnp.where(mirror >= half, mirror, -1.0))
    one = (target == rest).astype(F32).astype(BF)
    for p in range(tm):
        choose[p] = one
    keep[...] = (iota_f((PAD, bins), 0) == fold).astype(F32)
    freq = (residue + tm * (base + iota((1, bins), 1))).astype(F32)
    step = iota_f((TILES, bins), 0) - HALF_TILES
    sine, cosine = sincos(turns_of(step * freq, tm * (z.length // LANES)))
    table = jnp.concatenate(
        [jnp.concatenate([cosine, -sine], axis=1), jnp.concatenate([sine, cosine], axis=1)], axis=0
    )
    high, low = split2(table)
    for k, part in enumerate((high, high, low, low)):
        steps[k * 2 * TILES : (k + 1) * 2 * TILES, :] = part
    sine, cosine = sincos(turns_of(iota_f((LANES, bins), 0) * freq, tm * z.length))
    turns[0] = cosine
    turns[1] = sine
    gap = jnp.abs(iota((bins, bins), 0) - iota((bins, bins), 1))
    near[...] = (gap <= SMOOTH).astype(F32).astype(BF)
    p_sin, p_cos = sincos(turns_of((residue * iota((tm, LANES), 0)).astype(F32), tm))
    phase[0] = p_cos
    phase[1] = -p_sin


def tables(z, offsets, band, flags, mask):
    return pl.pallas_call(
        functools.partial(table_kernel, z, offsets),
        in_specs=[HBM_SPEC] * 3,
        out_specs=[VMEM_SPEC] * 8,
        scratch_shapes=[
            pltpu.SMEM((1, 1), jnp.int32),
            pltpu.SMEM((z.stations,), jnp.int32),
            pltpu.SMEM(mask.shape, jnp.int32),
            pltpu.SemaphoreType.DMA((3,)),
        ],
        out_shape=[
            jax.ShapeDtypeStruct((z.tm, z.spec_rows, z.bins), BF),
            jax.ShapeDtypeStruct((PAD, z.bins), F32),
            jax.ShapeDtypeStruct((8 * TILES, 2 * z.bins), BF),
            jax.ShapeDtypeStruct((2, LANES, z.bins), F32),
            jax.ShapeDtypeStruct((z.bins, z.bins), BF),
            jax.ShapeDtypeStruct((2, z.tm, LANES), F32),
            jax.ShapeDtypeStruct((z.stations, TILES, LANES), F32),
            jax.ShapeDtypeStruct((len(offsets), 2, LANES), F32),
        ],
        compiler_params=params(),
        cost_estimate=pl.CostEstimate(flops=4000000, bytes_accessed=2000000, transcendentals=0),
        name="tables",
    )(band.reshape(1, 1), flags, mask)


def sublane_sums(value, row):
    total = value
    for shift in (1, 2, 4):
        total = total + jnp.where(row >= shift, pltpu.roll(total, shift, 0), 0.0)
    return total - value, total


def spectrum_kernel(z, got, choose, keep, steps, turns, near, phase, switch, out):
    tm, bins, at = z.tm, z.bins, z.spec_rows
    parts = got[:, 0:at, :].astype(F32).reshape(tm * at, LANES).astype(BF)
    weights = choose[...].astype(F32).reshape(tm * at, bins).astype(BF)
    placed = lax.dot_general(parts, weights, (((0,), (0,)), ((), ())), preferred_element_type=F32)
    mask = keep[...]
    folded = [
        jnp.sum(placed[k * PAD : (k + 1) * PAD] * mask, axis=0, keepdims=True)
        for k in range(4 * z.stations)
    ]
    spec = [folded[k] + folded[k + 2 * z.stations] for k in range(2 * z.stations)]
    upto, onward, ones = window_tables()
    row = iota((TILES, LANES), 0)
    late = row >= HALF_TILES
    sides = []
    side_rows = z.stations * TILES
    for side, table in ((0, upto), (1, onward)):
        rows = slice(at + side * side_rows, at + (side + 1) * side_rows)
        value = got[:, rows, :].astype(F32).reshape(tm * side_rows, LANES)
        sums = jnp.dot(
            jnp.abs(value).astype(BF),
            jnp.concatenate([table, ones], axis=1),
            preferred_element_type=F32,
        )
        sides.append((value, sums))
    mixed = []
    for s in range(z.stations):
        real = jnp.zeros((TILES, LANES), F32)
        imag = jnp.zeros((TILES, LANES), F32)
        flag = switch[s]
        for p in range(tm):
            begin = (p * z.stations + s) * TILES
            before = ((p - 1) % tm * z.stations + s) * TILES
            value_r, sums_r = (v[begin : begin + TILES] for v in sides[0])
            value_l, sums_l = (v[before : before + TILES] for v in sides[1])
            earlier, _ = sublane_sums(sums_r[:, LANES:], row)
            right = sums_r[:, :LANES] + earlier
            tail = sums_l[:, LANES:]
            for shift in (1, 2, 4):
                tail = tail + jnp.where(row < TILES - shift, pltpu.roll(tail, TILES - shift, 0), 0.0)
            left = sums_l[:, :LANES] + jnp.where(
                row < TILES - 1, pltpu.roll(tail, TILES - 1, 0), 0.0
            )
            total = left + right if p else jnp.where(late, right, left)
            sample = pltpu.roll(jnp.where(late, value_l, value_r), HALF_TILES, 0)
            value = flag * sample / (total * (1.0 / (2 * HALF_WIN + 1)) + EPS_MEAN)
            real = real + value * phase[0, p : p + 1, :]
            imag = imag + value * phase[1, p : p + 1, :]
        mixed.append(jnp.concatenate([real, imag], axis=0))
    high, low = split2(jnp.concatenate(mixed, axis=1))
    spread = lax.dot_general(
        jnp.concatenate([high, low, high, low], axis=0),
        steps[...],
        (((0,), (0,)), ((), ())),
        preferred_element_type=F32,
    )
    cosine, sine = turns[0], turns[1]
    pieces = []
    for s in range(z.stations):
        g_re = spread[s * LANES : (s + 1) * LANES, :bins]
        g_im = spread[s * LANES : (s + 1) * LANES, bins:]
        spec[2 * s] += jnp.sum(g_re * cosine + g_im * sine, axis=0, keepdims=True)
        spec[2 * s + 1] += jnp.sum(g_im * cosine - g_re * sine, axis=0, keepdims=True)
        power = spec[2 * s] * spec[2 * s] + spec[2 * s + 1] * spec[2 * s + 1]
        for _ in range(3):
            part = power.astype(BF).astype(F32)
            pieces.append(part)
            power = power - part
    pieces.append(jnp.zeros((8 - len(pieces), bins), F32))
    smooth = jnp.dot(
        jnp.concatenate(pieces, axis=0).astype(BF), near[...], preferred_element_type=F32
    )
    for s in range(z.stations):
        mean = smooth[3 * s : 3 * s + 1] + smooth[3 * s + 1 : 3 * s + 2] + smooth[3 * s + 2 : 3 * s + 3]
        scale = 1.0 / jnp.sqrt(mean * (1.0 / (2 * SMOOTH + 1)) + EPS_POWER)
        out[2 * s : 2 * s + 1, :] = spec[2 * s] * scale
        out[2 * s + 1 : 2 * s + 2, :] = spec[2 * s + 1] * scale


def spectrum(z, got, made):
    return pl.pallas_call(
        functools.partial(spectrum_kernel, z),
        in_specs=[VMEM_SPEC] * 8,
        out_specs=VMEM_SPEC,
        out_shape=jax.ShapeDtypeStruct((2 * z.stations, z.bins), F32),
        compiler_params=params(),
        name="spectrum",
    )(got, *made)


def cross_kernel(z, offsets, pairs, stacks, *refs):
    pieces, out = refs[:-1], refs[-1]
    here = position("sta")
    mine = pieces[0][...]
    bins = z.bins
    sides = []
    for i in range(z.stations):
        re, im = mine[2 * i : 2 * i + 1], mine[2 * i + 1 : 2 * i + 2]
        sides.append((jnp.concatenate([re, im], axis=0), jnp.concatenate([im, -re], axis=0)))
    for k, (offset, piece) in enumerate(zip(offsets, pieces)):
        on = jnp.concatenate([pairs[k]] * (bins // LANES), axis=1)
        for j in range(z.stations):
            re = jnp.broadcast_to(piece[2 * j : 2 * j + 1, :], (2, bins)) * on
            im = jnp.broadcast_to(piece[2 * j + 1 : 2 * j + 2, :], (2, bins)) * on
            column = (here ^ offset) * z.stations + j
            for i, (p, q) in enumerate(sides):
                out[i, column] = stacks[i, column] + (re * p + im * q)


def cross(z, offsets, pairs, stacks, pieces):
    return pl.pallas_call(
        functools.partial(cross_kernel, z, offsets),
        in_specs=[VMEM_SPEC] * (2 + len(pieces)),
        out_specs=VMEM_SPEC,
        out_shape=jax.ShapeDtypeStruct(stacks.shape, F32),
        compiler_params=params(),
        name="cross",
    )(pairs, stacks, *pieces)


def shards(traces, station_flags, tile_mask, band_block, stacks):
    tm_count, sta_count = lax.axis_size("tm"), lax.axis_size("sta")
    stations, length = traces.shape
    z = Sizes(stations, length, tm_count, stacks.shape[-1])
    assert sta_count & (sta_count - 1) == 0
    sent = transform(z, station_flags, traces)
    got = lax.all_to_all(sent, "tm", split_axis=0, concat_axis=0, tiled=True)
    offsets = [0]
    bits = [1 << k for k in reversed(range(sta_count.bit_length() - 1))]
    for bit in bits:
        offsets += [offset ^ bit for offset in offsets]
    *made, pairs = tables(z, offsets, band_block, station_flags, tile_mask)
    pieces = [spectrum(z, got, made)]
    for bit in bits:
        swap = [(i, i ^ bit) for i in range(sta_count)]
        pieces += [lax.ppermute(piece, "sta", swap) for piece in pieces]
    return cross(z, offsets, pairs, stacks, pieces)


def solution(mesh):
    return jax.shard_map(
        shards,
        mesh=mesh,
        in_specs=(P("sta", "tm"), P("sta"), P(), P(), P("sta", None, None, "tm")),
        out_specs=P("sta", None, None, "tm"),
        check_vma=False,
    )
```

```python
import functools
import math

import jax
import jax.numpy as jnp
import numpy as np
from jax import lax
from jax.experimental import pallas as pl
from jax.experimental.pallas import tpu as pltpu
from jax.sharding import PartitionSpec as P

HALF_WIN = 512
SMOOTH = 32
EPS_MEAN = 1e-06
EPS_POWER = 1e-06
LANES = 128
SPAN = 2 * HALF_WIN
TILES = SPAN // LANES
HALF_TILES = HALF_WIN // LANES
PAD = 16
BAND_TOP = 137
WIDTH = 2 * LANES
CHUNKS = SPAN // WIDTH
position = lax.axis_index
VMEM_LIMIT = 16 * 1024 * 1024
BF = jnp.bfloat16
F32 = jnp.float32


def up_to(value, step):
    return -(-value // step) * step


def sincos(turns):
    quarter = jnp.round(turns * 4.0)
    rest = turns - quarter * 0.25
    y = rest * (2.0 * math.pi)
    y2 = y * y
    s = y + y * y2 * (-1.0 / 6 + y2 * (1.0 / 120 + y2 * (-1.0 / 5040 + y2 * (1.0 / 362880))))
    c = 1.0 + y2 * (-0.5 + y2 * (1.0 / 24 + y2 * (-1.0 / 720 + y2 * (1.0 / 40320))))
    q = quarter - 4.0 * jnp.floor(quarter * 0.25)
    swap = (q == 1.0) | (q == 3.0)
    sine = jnp.where(swap, c, s)
    cosine = jnp.where(swap, s, c)
    sine = jnp.where(q >= 2.0, -sine, sine)
    cosine = jnp.where((q == 1.0) | (q == 2.0), -cosine, cosine)
    return sine, cosine


def turns_of(product, period):
    whole = jnp.floor(product * (1.0 / period))
    return (product - whole * period) * (1.0 / period)


def split2(value):
    high = value.astype(BF)
    return high, (value - high.astype(F32)).astype(BF)


def iota(shape, axis):
    return lax.broadcasted_iota(jnp.int32, shape, axis)


def iota_f(shape, axis):
    return iota(shape, axis).astype(F32)


def window_tables():
    row, lane = iota((LANES, LANES), 0), iota((LANES, LANES), 1)
    upto = (row <= lane).astype(F32).astype(BF)
    onward = (row >= lane).astype(F32).astype(BF)
    return upto, onward, jnp.ones((LANES, LANES), BF)


def np_split(value):
    high = value.astype(jnp.bfloat16).astype(np.float64)
    return high, (value - high).astype(jnp.bfloat16).astype(np.float64)


class Sizes:
    def __init__(self, stations, length, tm_count, bins):
        self.stations, self.length, self.tm, self.bins = stations, length, tm_count, bins
        self.rows = length // SPAN
        self.half = self.rows // 2 + 1
        self.pad = up_to(self.rows, PAD)
        self.full = self.rows // PAD * PAD
        self.tail = self.rows - self.full
        self.depth = 3 * self.full + PAD
        self.block = min(tm_count, 16)
        self.blocks = tm_count // self.block
        self.folds = (BAND_TOP + bins - 1) // self.rows + 1
        self.lift = up_to(self.half, 2)
        self.spec_rows = up_to(2 * self.lift, 8)
        self.edge_rows = 2 * stations * TILES
        self.sent_rows = self.spec_rows + self.edge_rows
        assert length % SPAN == 0 and tm_count % self.block == 0
        assert stations == 2 and self.folds <= PAD
        assert self.rows >= 2 and 0 < 3 * self.tail <= 8 and self.depth <= LANES

    def parity_tables(self):
        residue = np.arange(self.tm).reshape(-1, 2).T[:, None, :]
        order = (residue + self.tm * np.arange(self.lift)[None, :, None]).reshape(2, -1)
        return self.first_of(order), self.turn_of(order)

    def row_order(self):
        j2 = np.arange(self.tm)[:, None] + self.tm * np.arange(self.half)[None, :]
        return j2.reshape(self.blocks, self.block, self.half).transpose(0, 2, 1).reshape(self.blocks, -1)

    def first_table(self):
        return self.first_of(self.row_order())

    def turn_table(self):
        return self.turn_of(self.row_order())

    def first_of(self, order):
        period = self.tm * self.rows
        angle = 2.0 * np.pi / period * (order[:, :, None] * np.arange(self.rows) % period)
        parts = np.concatenate([np.cos(angle), -np.sin(angle)], axis=1)
        full, rest = parts[..., : self.full], parts[..., self.full :]
        table = np.concatenate([full, full, full, rest, rest, rest], axis=2)
        return np.pad(table, ((0, 0), (0, 0), (0, LANES - table.shape[2]))).astype(np.float32)

    def low_lanes(self, lane):
        at = 3 * self.full
        third = (lane >= 2 * self.full) & (lane < at)
        return third | ((lane >= at + 2 * self.tail) & (lane < at + 3 * self.tail))

    def turn_of(self, order):
        order = order.reshape(order.shape[0], 1, -1, 1)
        time = np.arange(SPAN).reshape(CHUNKS, 1, WIDTH)
        angle = 2.0 * np.pi / (self.tm * self.length) * (order * time)
        return np.stack([np.cos(angle), -np.sin(angle)], axis=2).astype(np.float32)


def unpack(z, x, xs, edges):
    rows, top = z.rows, 8
    for a in range(rows):
        xs[:, top + a, :] = x[:, a * SPAN : (a + 1) * SPAN].astype(F32)
    for s in range(z.stations):
        for side, a in ((0, 0), (1, rows - 1)):
            for c in range(TILES):
                at = (side * z.stations + s) * TILES + c
                edges[at : at + 1, :] = xs[s, top + a : top + a + 1, c * LANES : (c + 1) * LANES]


def window(z, s, xs, sums):
    rows, pad, top = z.rows, z.pad, 8
    short = up_to(rows, 8)
    kernel = jnp.concatenate(window_tables()[:2], axis=1)
    group = 4
    for c0 in range(0, TILES, group):
        parts = [
            jnp.abs(xs[s, top : top + pad, c * LANES : (c + 1) * LANES])
            for c in range(c0, c0 + group)
        ]
        part = jnp.concatenate([part.astype(BF) for part in parts], axis=0)
        got = jnp.dot(part, kernel, preferred_element_type=F32)
        for k in range(group):
            value = got[k * pad : k * pad + short]
            upto, onward = value[:, :LANES], value[:, LANES:]
            sums[s, c0 + k, top : top + short, 0 : 2 * LANES] = value
            sums[s, c0 + k, top : top + short, 2 * LANES :] = upto + (onward - parts[k][:short])
    blank = jnp.zeros((1, HALF_WIN), F32)
    xs[s, top : top + 1, 0:HALF_WIN] = blank
    xs[s, top + rows - 1 : top + rows, HALF_WIN:SPAN] = blank


def level(z, s, tiles, xs, sums, stack):
    rows, top = z.rows, 8
    short = up_to(rows, 8)

    def tile(kind, c):
        turn, cc = divmod(c, TILES)
        lines = slice(top + turn, top + turn + short)
        return sums[s, cc, lines, kind * LANES : (kind + 1) * LANES]

    first = tiles[0] + 1 - HALF_TILES
    single = [tile(2, c) for c in range(first, tiles[-1] + HALF_TILES)]
    twos = [single[c] + single[c + 1] for c in range(len(single) - 1)]
    for k, c in enumerate(tiles):
        inner = (twos[k] + twos[k + 2]) + (twos[k + 4] + single[k + 6])
        total = inner + (tile(1, c - HALF_TILES) + tile(0, c + HALF_TILES))
        value = xs[s, top : top + short, c * LANES : (c + 1) * LANES]
        value = value / (total * (1.0 / (2 * HALF_WIN + 1)) + EPS_MEAN)
        high, low = split2(value[: z.full])
        lanes = slice(c * LANES, (c + 1) * LANES)
        for k2, part in enumerate((high, low, high)):
            stack[s, k2 * z.full : (k2 + 1) * z.full, lanes] = part
        rest = value[z.full :]
        high = rest.astype(BF).astype(F32)
        rest = high + pltpu.roll(rest - high, z.tail, 0) + pltpu.roll(high, 2 * z.tail, 0)
        rest = jnp.concatenate([rest, jnp.zeros((PAD - rest.shape[0], LANES), F32)], axis=0)
        stack[s, 3 * z.full :, lanes] = rest.astype(BF)


def fold_weights(weight):
    lane = iota((PAD, SPAN), 1)
    for kind in range(2):
        turns = jnp.bitwise_and((iota((PAD, SPAN), 0) + kind) * lane, SPAN - 1).astype(F32)
        sine, cosine = sincos(turns * (1.0 / SPAN))
        for h, (s, c) in enumerate(zip(split2(sine), split2(cosine))):
            table = ((c, s), (-s, c)) if kind == 0 else ((c, -s), (-s, -c))
            for part in range(2):
                at = h * 4 * PAD + kind * 2 * PAD + part * PAD
                for side in range(2):
                    for g in range(CHUNKS):
                        to = (2 * g + side) * WIDTH
                        weight[at : at + PAD, to : to + WIDTH] = table[part][side][
                            :, g * WIDTH : (g + 1) * WIDTH
                        ]


def transform_kernel(
    z, flags, x, first, turn, out,
    flags_s, x_v, first_v, turn_v, table, xs, sums, stack, edges, weight, acc, both, spec, sems,
):
    half, block, tm = z.half, z.block, z.tm
    height = half * block
    index = pl.program_id(0)
    top, rows, pad = 8, z.rows, z.pad
    get_first = pltpu.make_async_copy(first.at[index], first_v, sems.at[2])
    get_turn = [
        pltpu.make_async_copy(turn.at[index, g], turn_v.at[g], sems.at[3 + g]) for g in range(CHUNKS)
    ]

    def prologue():
        copies = [
            pltpu.make_async_copy(x, x_v, sems.at[0]),
            pltpu.make_async_copy(flags, flags_s, sems.at[1]),
        ]
        for copy in copies + [get_first] + get_turn:
            copy.start()
        full = rows // 8 * 8
        for s in range(z.stations):
            xs[s, top + full : top + pad, :] = jnp.zeros((pad - full, SPAN), F32)
            for c in range(TILES):
                sums[s, c, 0:top, :] = jnp.zeros((top, 3 * LANES), F32)
                sums[s, c, top + up_to(rows, 8) :, :] = jnp.zeros((8, 3 * LANES), F32)
        spec[:, z.spec_rows - 8 : z.spec_rows, :] = jnp.zeros((tm, 8, LANES), F32)
        fold_weights(weight)
        for copy in copies:
            copy.wait()
        unpack(z, x_v, xs, edges)
        for s in range(z.stations):
            window(z, s, xs, sums)
            if s == 0 or z.blocks > 1:
                level(z, s, range(TILES), xs, sums, stack)

    if z.blocks == 1:
        prologue()
    else:
        pl.when(index == 0)(prologue)

        @pl.when(index > 0)
        def _():
            for copy in [get_first] + get_turn:
                copy.start()

    for copy in [get_first] + get_turn:
        copy.wait()
    residue = index * block + iota((block, LANES), 0)
    sine, cosine = sincos(turns_of((position("tm") * residue).astype(F32), tm))
    f_re = first_v[:height].reshape(half, block, LANES)
    f_im = first_v[height:].reshape(half, block, LANES)
    low = z.low_lanes(iota((height, LANES), 1))
    for k, value in enumerate(
        (f_re * cosine[None] + f_im * sine[None], f_im * cosine[None] - f_re * sine[None])
    ):
        value = value.reshape(height, LANES)
        high = value.astype(BF).astype(F32)
        table[k * height : (k + 1) * height, :] = jnp.where(low, value - high, high).astype(BF)

    def first_stage(s, g):
        return jnp.dot(
            table[:, : z.depth],
            stack[s, :, g * WIDTH : (g + 1) * WIDTH],
            preferred_element_type=F32,
        )

    def second_stage(s, g, parts):
        w = weight[:, 2 * g * WIDTH : 2 * (g + 1) * WIDTH]
        got = lax.dot_general(parts, w, (((1,), (1,)), ((), ())), preferred_element_type=F32)
        value = got[:height] + got[height:]
        acc[s] = value if g == 0 else acc[s] + value

    def settle(s):
        value = acc[s] + pltpu.roll(acc[s], LANES // 2, 1)
        return value * flags_s[s].astype(F32)

    steps = [(s, g) for s in range(z.stations) for g in range(CHUNKS)]
    coming = first_stage(*steps[0])
    waiting = None
    for k, (s, g) in enumerate(steps):
        f_re, f_im = coming[:height], coming[height:]
        t_re, t_im = turn_v[g, 0], turn_v[g, 1]
        re_h, re_l = split2(f_re * t_re - f_im * t_im)
        im_h, im_l = split2(f_re * t_im + f_im * t_re)
        parts = jnp.concatenate(
            [jnp.concatenate([re_h, im_h], axis=1), jnp.concatenate([re_l, im_l], axis=1)], axis=0
        )
        if s == 0 and z.blocks == 1:
            level(z, 1, range(2 * g, 2 * g + 2), xs, sums, stack)
        if k + 1 < len(steps):
            coming = first_stage(*steps[k + 1])
        if waiting is not None:
            second_stage(*steps[k - 1], waiting)
        waiting = parts
    second_stage(*steps[-1], waiting)
    zero, one = settle(0), settle(1)
    lane = iota((height, LANES), 1)
    early = jnp.bitwise_and(lane, LANES // 2 - 1) < LANES // 4
    direct = jnp.where(early, zero, pltpu.roll(one, LANES // 4, 1))
    mirror = jnp.where(early, pltpu.roll(zero, LANES // 4, 1), one)
    for kind, value in enumerate((direct, mirror)):
        high = value.astype(BF).astype(F32)
        both[kind] = jnp.where(lane < LANES // 2, high, value - high)
    for k in range(block):
        here = index * block + k
        there = jnp.where(here == 0, 0, tm - here) if z.blocks > 1 else (tm - k) % tm
        here = here if z.blocks > 1 else k
        lines = pl.ds(k, half, stride=block)
        spec[here, 0:half, :] = both[0, lines, :]
        spec[there, half : 2 * half, :] = both[1, lines, :]

    def finish():
        ends = edges[...].astype(BF)

        def one_row(k, carry):
            out[k, 0 : z.spec_rows, :] = spec[k].astype(BF)
            out[k, z.spec_rows : z.sent_rows, :] = ends
            return carry

        if z.blocks == 1:
            for k in range(tm):
                one_row(k, 0)
        else:
            lax.fori_loop(0, tm, one_row, 0)

    if z.blocks == 1:
        finish()
    else:
        pl.when(index == z.blocks - 1)(finish)


SMEM_SPEC = pl.BlockSpec(memory_space=pltpu.SMEM)
VMEM_SPEC = pl.BlockSpec(memory_space=pltpu.VMEM)
HBM_SPEC = pl.BlockSpec(memory_space=pltpu.HBM)


def params():
    return pltpu.CompilerParams(vmem_limit_bytes=VMEM_LIMIT)


def transform(z, flags, x):
    height = z.half * z.block
    first, turn = z.first_table(), z.turn_table()
    return pl.pallas_call(
        functools.partial(transform_kernel, z),
        grid=(z.blocks,),
        in_specs=[HBM_SPEC] * 4,
        out_specs=VMEM_SPEC,
        out_shape=jax.ShapeDtypeStruct((z.tm, z.sent_rows, LANES), BF),
        scratch_shapes=[
            pltpu.SMEM((z.stations,), jnp.int32),
            pltpu.VMEM(x.shape, BF),
            pltpu.VMEM(first.shape[1:], F32),
            pltpu.VMEM(turn.shape[1:], F32),
            pltpu.VMEM(first.shape[1:], BF),
            pltpu.VMEM((z.stations, 8 + z.pad, SPAN), F32),
            pltpu.VMEM((z.stations, TILES, 16 + up_to(z.rows, 8), 3 * LANES), F32),
            pltpu.VMEM((z.stations, z.depth, SPAN), BF),
            pltpu.VMEM((z.edge_rows, LANES), F32),
            pltpu.VMEM((LANES, 2 * SPAN), BF),
            pltpu.VMEM((z.stations, height, LANES), F32),
            pltpu.VMEM((2, height, LANES), F32),
            pltpu.VMEM((z.tm, z.spec_rows, LANES), F32),
            pltpu.SemaphoreType.DMA((3 + CHUNKS,)),
        ],
        name="transform",
    )(flags, x, jnp.asarray(first), jnp.asarray(turn))


def table_kernel(
    z, offsets, split, band, flags, mask, choose, keep, steps, turns, near, phase, switch, pairs,
    band_s, flags_s, mask_s, sems,
):
    rows, tm, bins, half = z.rows, z.tm, z.bins, z.half
    copies = [
        pltpu.make_async_copy(band, band_s, sems.at[0]),
        pltpu.make_async_copy(flags, flags_s, sems.at[1]),
        pltpu.make_async_copy(mask, mask_s, sems.at[2]),
    ]
    for copy in copies:
        copy.start()
    for copy in copies:
        copy.wait()
    here = position("sta")
    for k, offset in enumerate(offsets):
        pairs[k] = jnp.full((2, LANES), mask_s[here, here ^ offset].astype(F32))
    base, residue = band_s[0, 0], position("tm")
    for s in range(z.stations):
        switch[s] = jnp.full((TILES, LANES), flags_s[s].astype(F32))
    spot = iota_f((1, bins), 1) + base.astype(F32)
    fold = jnp.floor((spot + 0.5) * (1.0 / rows))
    rest = spot - fold * rows
    row = iota_f((z.spec_rows, bins), 0)
    last = (rows - 1 + split + (residue == 0).astype(jnp.int32)).astype(F32)
    mirror = jnp.where((row >= split) & (last - row >= half), last - row, -1.0)
    one = (jnp.where(row < half, row, mirror) == rest).astype(F32).astype(BF)
    for p in range(choose.shape[0]):
        choose[p] = one
    keep[...] = (iota_f((PAD, bins), 0) == fold).astype(F32)
    freq = (residue + tm * (base + iota((1, bins), 1))).astype(F32)
    step = iota_f((TILES, bins), 0) - HALF_TILES
    sine, cosine = sincos(turns_of(step * freq, tm * (z.length // LANES)))
    table = jnp.concatenate(
        [jnp.concatenate([cosine, -sine], axis=1), jnp.concatenate([sine, cosine], axis=1)], axis=0
    )
    high, low = split2(table)
    for k, part in enumerate((high, high, low, low)):
        steps[k * 2 * TILES : (k + 1) * 2 * TILES, :] = part
    sine, cosine = sincos(turns_of(iota_f((LANES, bins), 0) * freq, tm * z.length))
    turns[0] = cosine
    turns[1] = sine
    gap = jnp.abs(iota((bins, bins), 0) - iota((bins, bins), 1))
    near[...] = (gap <= SMOOTH).astype(F32).astype(BF)
    p_sin, p_cos = sincos(turns_of((residue * iota((tm, LANES), 0)).astype(F32), tm))
    phase[0] = p_cos
    phase[1] = -p_sin


def tables(z, offsets, split, copies, band, flags, mask):
    return pl.pallas_call(
        functools.partial(table_kernel, z, offsets, split),
        in_specs=[HBM_SPEC] * 3,
        out_specs=[VMEM_SPEC] * 8,
        scratch_shapes=[
            pltpu.SMEM((1, 1), jnp.int32),
            pltpu.SMEM((z.stations,), jnp.int32),
            pltpu.SMEM(mask.shape, jnp.int32),
            pltpu.SemaphoreType.DMA((3,)),
        ],
        out_shape=[
            jax.ShapeDtypeStruct((copies, z.spec_rows, z.bins), BF),
            jax.ShapeDtypeStruct((PAD, z.bins), F32),
            jax.ShapeDtypeStruct((8 * TILES, 2 * z.bins), BF),
            jax.ShapeDtypeStruct((2, LANES, z.bins), F32),
            jax.ShapeDtypeStruct((z.bins, z.bins), BF),
            jax.ShapeDtypeStruct((2, z.tm, LANES), F32),
            jax.ShapeDtypeStruct((z.stations, TILES, LANES), F32),
            jax.ShapeDtypeStruct((len(offsets), 2, LANES), F32),
        ],
        compiler_params=params(),
        cost_estimate=pl.CostEstimate(flops=4000000, bytes_accessed=2000000, transcendentals=0),
        name="tables",
    )(band.reshape(1, 1), flags, mask)


def sublane_sums(value, row):
    total = value
    for shift in (1, 2, 4):
        total = total + jnp.where(row >= shift, pltpu.roll(total, shift, 0), 0.0)
    return total - value, total


def spectrum_kernel(z, got, choose, keep, steps, turns, near, phase, switch, out):
    tm, bins, at = z.tm, z.bins, z.spec_rows
    parts = got[:, 0:at, :].astype(F32).reshape(tm * at, LANES).astype(BF)
    weights = choose[...].astype(F32).reshape(tm * at, bins).astype(BF)
    placed = lax.dot_general(parts, weights, (((0,), (0,)), ((), ())), preferred_element_type=F32)
    side_rows = z.stations * TILES
    ends = [
        got[:, at + k * side_rows : at + (k + 1) * side_rows, :].astype(F32).reshape(-1, LANES)
        for k in range(2)
    ]
    whiten(z, placed, ends, keep, steps, turns, near, phase, switch, out)


def gathered_kernel(
    z, kept, came, went, choose, keep, steps, turns, near, phase, switch, out, ends
):
    tm = z.tm
    piece = came[0].astype(F32)
    total = kept[0] + (piece + pltpu.roll(piece, LANES // 2, 1))
    placed = lax.dot_general(
        halves(total), choose[0], (((0,), (0,)), ((), ())), preferred_element_type=F32
    )
    here = position("tm")
    for s in range(tm):
        source, slot = (went, s) if s < tm // 2 else (came, s - tm // 2)
        ends[here ^ s] = source[1 + slot, 0 : z.edge_rows, :].astype(F32)
    side_rows = z.stations * TILES
    sides = [ends[:, k * side_rows : (k + 1) * side_rows, :].reshape(-1, LANES) for k in range(2)]
    whiten(z, placed, sides, keep, steps, turns, near, phase, switch, out)


def halves(value):
    high = value.astype(BF).astype(F32)
    return jnp.where(iota(value.shape, 1) < LANES // 2, high, value - high).astype(BF)


def whiten(z, placed, ends, keep, steps, turns, near, phase, switch, out):
    tm, bins = z.tm, z.bins
    mask = keep[...]
    folded = [
        jnp.sum(placed[k * PAD : (k + 1) * PAD] * mask, axis=0, keepdims=True)
        for k in range(4 * z.stations)
    ]
    spec = [folded[k] + folded[k + 2 * z.stations] for k in range(2 * z.stations)]
    upto, onward, ones = window_tables()
    row = iota((TILES, LANES), 0)
    late = row >= HALF_TILES
    sides = []
    for value, table in zip(ends, (upto, onward)):
        sums = jnp.dot(
            jnp.abs(value).astype(BF),
            jnp.concatenate([table, ones], axis=1),
            preferred_element_type=F32,
        )
        sides.append((value, sums))
    mixed = []
    for s in range(z.stations):
        real = jnp.zeros((TILES, LANES), F32)
        imag = jnp.zeros((TILES, LANES), F32)
        flag = switch[s]
        for p in range(tm):
            begin = (p * z.stations + s) * TILES
            before = ((p - 1) % tm * z.stations + s) * TILES
            value_r, sums_r = (v[begin : begin + TILES] for v in sides[0])
            value_l, sums_l = (v[before : before + TILES] for v in sides[1])
            earlier, _ = sublane_sums(sums_r[:, LANES:], row)
            right = sums_r[:, :LANES] + earlier
            tail = sums_l[:, LANES:]
            for shift in (1, 2, 4):
                tail = tail + jnp.where(row < TILES - shift, pltpu.roll(tail, TILES - shift, 0), 0.0)
            left = sums_l[:, :LANES] + jnp.where(
                row < TILES - 1, pltpu.roll(tail, TILES - 1, 0), 0.0
            )
            total = left + right if p else jnp.where(late, right, left)
            sample = pltpu.roll(jnp.where(late, value_l, value_r), HALF_TILES, 0)
            value = flag * sample / (total * (1.0 / (2 * HALF_WIN + 1)) + EPS_MEAN)
            real = real + value * phase[0, p : p + 1, :]
            imag = imag + value * phase[1, p : p + 1, :]
        mixed.append(jnp.concatenate([real, imag], axis=0))
    high, low = split2(jnp.concatenate(mixed, axis=1))
    spread = lax.dot_general(
        jnp.concatenate([high, low, high, low], axis=0),
        steps[...],
        (((0,), (0,)), ((), ())),
        preferred_element_type=F32,
    )
    cosine, sine = turns[0], turns[1]
    pieces = []
    for s in range(z.stations):
        g_re = spread[s * LANES : (s + 1) * LANES, :bins]
        g_im = spread[s * LANES : (s + 1) * LANES, bins:]
        spec[2 * s] += jnp.sum(g_re * cosine + g_im * sine, axis=0, keepdims=True)
        spec[2 * s + 1] += jnp.sum(g_im * cosine - g_re * sine, axis=0, keepdims=True)
        power = spec[2 * s] * spec[2 * s] + spec[2 * s + 1] * spec[2 * s + 1]
        for _ in range(3):
            part = power.astype(BF).astype(F32)
            pieces.append(part)
            power = power - part
    pieces.append(jnp.zeros((8 - len(pieces), bins), F32))
    smooth = jnp.dot(
        jnp.concatenate(pieces, axis=0).astype(BF), near[...], preferred_element_type=F32
    )
    for s in range(z.stations):
        mean = smooth[3 * s : 3 * s + 1] + smooth[3 * s + 1 : 3 * s + 2] + smooth[3 * s + 2 : 3 * s + 3]
        scale = 1.0 / jnp.sqrt(mean * (1.0 / (2 * SMOOTH + 1)) + EPS_POWER)
        out[2 * s : 2 * s + 1, :] = spec[2 * s] * scale
        out[2 * s + 1 : 2 * s + 2, :] = spec[2 * s + 1] * scale


def spectrum(z, got, made):
    return pl.pallas_call(
        functools.partial(spectrum_kernel, z),
        in_specs=[VMEM_SPEC] * 8,
        out_specs=VMEM_SPEC,
        out_shape=jax.ShapeDtypeStruct((2 * z.stations, z.bins), F32),
        compiler_params=params(),
        name="spectrum",
    )(got, *made)


def gathered(z, kept, came, went, made):
    return pl.pallas_call(
        functools.partial(gathered_kernel, z),
        in_specs=[VMEM_SPEC] * 10,
        out_specs=VMEM_SPEC,
        out_shape=jax.ShapeDtypeStruct((2 * z.stations, z.bins), F32),
        scratch_shapes=[pltpu.VMEM((z.tm, z.edge_rows, LANES), F32)],
        compiler_params=params(),
        name="spectrum",
    )(kept, came, went, *made)


def half_transform(z, parity, table, turn, stack, weight, flags, acc, both, spec, before):
    count, lift = z.tm // 2, z.lift
    height = lift * count

    def first_stage(s, g):
        return jnp.dot(
            table[:, : z.depth],
            stack[s, :, g * WIDTH : (g + 1) * WIDTH],
            preferred_element_type=F32,
        )

    def second_stage(s, g, parts):
        w = weight[:, 2 * g * WIDTH : 2 * (g + 1) * WIDTH]
        got = lax.dot_general(parts, w, (((1,), (1,)), ((), ())), preferred_element_type=F32)
        value = got[:height] + got[height:]
        acc[s] = value if g == 0 else acc[s] + value

    def settle(s):
        return (acc[s] + pltpu.roll(acc[s], LANES // 2, 1)) * flags[s, 0:1, :]

    steps = [(s, g) for s in range(z.stations) for g in range(CHUNKS)]
    coming = first_stage(*steps[0])
    waiting = None
    for k, (s, g) in enumerate(steps):
        f_re, f_im = coming[:height], coming[height:]
        t_re, t_im = turn[g, 0], turn[g, 1]
        re_h, re_l = split2(f_re * t_re - f_im * t_im)
        im_h, im_l = split2(f_re * t_im + f_im * t_re)
        parts = jnp.concatenate(
            [jnp.concatenate([re_h, im_h], axis=1), jnp.concatenate([re_l, im_l], axis=1)], axis=0
        )
        if before is not None and s == 0:
            before(g)
        if k + 1 < len(steps):
            coming = first_stage(*steps[k + 1])
        if waiting is not None:
            second_stage(*steps[k - 1], waiting)
        waiting = parts
    second_stage(*steps[-1], waiting)
    zero, one = settle(0), settle(1)
    lane = iota((height, LANES), 1)
    early = jnp.bitwise_and(lane, LANES // 2 - 1) < LANES // 4
    both[0] = jnp.where(early, zero, pltpu.roll(one, LANES // 4, 1))
    both[1] = jnp.where(early, pltpu.roll(zero, LANES // 4, 1), one)
    for j in range(count):
        lines = pl.ds(j, lift, stride=count)
        spec[j, 0:lift, :] = both[0, lines, :]
        spec[lax.rem(2 * count - parity - j, count), lift : 2 * lift, :] = both[1, lines, :]


def away_kernel(
    z, flags, x, first, turn, message, stack, weight, home_table, home_turn, switch,
    flags_s, x_v, first_v, turn_v, table, xs, sums, edges, acc, both, spec, sems,
):
    rows, pad, top = z.rows, z.pad, 8
    count, height = z.tm // 2, z.lift * (z.tm // 2)
    here = position("tm")
    home = jnp.bitwise_and(here, 1)
    away = 1 - home
    copies = [
        pltpu.make_async_copy(x, x_v, sems.at[0]),
        pltpu.make_async_copy(flags, flags_s, sems.at[1]),
        pltpu.make_async_copy(first, first_v, sems.at[2]),
        pltpu.make_async_copy(turn.at[away], turn_v, sems.at[3]),
        pltpu.make_async_copy(turn.at[home], home_turn, sems.at[4]),
    ]
    for copy in copies:
        copy.start()
    full = rows // 8 * 8
    for s in range(z.stations):
        xs[s, top + full : top + pad, :] = jnp.zeros((pad - full, SPAN), F32)
        for c in range(TILES):
            sums[s, c, 0:top, :] = jnp.zeros((top, 3 * LANES), F32)
            sums[s, c, top + up_to(rows, 8) :, :] = jnp.zeros((8, 3 * LANES), F32)
    spec[:, z.spec_rows - 8 : z.spec_rows, :] = jnp.zeros((count, 8, LANES), F32)
    fold_weights(weight)
    copies[0].wait()
    copies[1].wait()
    unpack(z, x_v, xs, edges)
    for s in range(z.stations):
        window(z, s, xs, sums)
        switch[s] = jnp.full((TILES, LANES), flags_s[s].astype(F32))
    level(z, 0, range(TILES), xs, sums, stack)
    for copy in copies[2:]:
        copy.wait()
    low = z.low_lanes(iota((height, LANES), 1))
    for parity, to in ((away, table), (home, home_table)):
        residue = 2 * iota((count, LANES), 0) + parity
        sine, cosine = sincos(turns_of((here * residue).astype(F32), z.tm))
        f_re = first_v[parity, :height].reshape(z.lift, count, LANES)
        f_im = first_v[parity, height:].reshape(z.lift, count, LANES)
        for k, value in enumerate(
            (f_re * cosine[None] + f_im * sine[None], f_im * cosine[None] - f_re * sine[None])
        ):
            value = value.reshape(height, LANES)
            high = value.astype(BF).astype(F32)
            to[k * height : (k + 1) * height, :] = jnp.where(low, value - high, high).astype(BF)
    half_transform(
        z, away, table, turn_v, stack, weight, switch, acc, both, spec,
        lambda g: level(z, 1, range(2 * g, 2 * g + 2), xs, sums, stack),
    )
    for j in range(count):
        message[j] = halves(spec[j])
    message[count, 0 : z.edge_rows, :] = edges[...].astype(BF)
    message[count, z.edge_rows :, :] = jnp.zeros((z.spec_rows - z.edge_rows, LANES), BF)


def home_kernel(z, stack, weight, table, turn, switch, kept, acc, both):
    kept[:, z.spec_rows - 8 : z.spec_rows, :] = jnp.zeros((z.tm // 2, 8, LANES), F32)
    parity = jnp.bitwise_and(position("tm"), 1)
    half_transform(z, parity, table, turn, stack, weight, switch, acc, both, kept, None)


def split_transform(z, flags, x):
    count, height = z.tm // 2, z.lift * (z.tm // 2)
    first, turn = z.parity_tables()
    state = [
        jax.ShapeDtypeStruct((z.stations, z.depth, SPAN), BF),
        jax.ShapeDtypeStruct((LANES, 2 * SPAN), BF),
        jax.ShapeDtypeStruct(first.shape[1:], BF),
        jax.ShapeDtypeStruct(turn.shape[1:], F32),
        jax.ShapeDtypeStruct((z.stations, TILES, LANES), F32),
    ]
    inputs = [flags, x, jnp.asarray(first), jnp.asarray(turn)]
    work = [
        pltpu.VMEM((z.stations, height, LANES), F32),
        pltpu.VMEM((2, height, LANES), F32),
    ]
    message, *state = pl.pallas_call(
        functools.partial(away_kernel, z),
        in_specs=[HBM_SPEC] * 4,
        out_specs=[VMEM_SPEC] * 6,
        out_shape=[jax.ShapeDtypeStruct((count + 1, z.spec_rows, LANES), BF)] + state,
        scratch_shapes=[
            pltpu.SMEM((z.stations,), jnp.int32),
            pltpu.VMEM(x.shape, BF),
            pltpu.VMEM(first.shape, F32),
            pltpu.VMEM(turn.shape[1:], F32),
            pltpu.VMEM(first.shape[1:], BF),
            pltpu.VMEM((z.stations, 8 + z.pad, SPAN), F32),
            pltpu.VMEM((z.stations, TILES, 16 + up_to(z.rows, 8), 3 * LANES), F32),
            pltpu.VMEM((z.edge_rows, LANES), F32),
            *work,
            pltpu.VMEM((count, z.spec_rows, LANES), F32),
            pltpu.SemaphoreType.DMA((5,)),
        ],
        compiler_params=params(),
        name="away",
    )(*(in_hbm(value) for value in inputs))

    def home():
        return pl.pallas_call(
            functools.partial(home_kernel, z),
            in_specs=[VMEM_SPEC] * 5,
            out_specs=VMEM_SPEC,
            out_shape=jax.ShapeDtypeStruct((count, z.spec_rows, LANES), F32),
            scratch_shapes=work,
            compiler_params=params(),
            cost_estimate=pl.CostEstimate(flops=10**9, bytes_accessed=10**6, transcendentals=0),
            name="home",
        )(*state)

    return message, home


def in_hbm(value):
    return pltpu.with_memory_space_constraint(value, pltpu.HBM)


def merge_kernel(z, bit, kept, came, went, message, left):
    slots = kept.shape[0]
    ends = came.shape[0] - slots
    side = jnp.bitwise_and(position("tm") >> bit, 1)
    for i in range(slots // 2):
        pair = []
        for j in (2 * i, 2 * i + 1):
            piece = came[j].astype(F32)
            pair.append(kept[j] + (piece + pltpu.roll(piece, LANES // 2, 1)))
        left[i] = jnp.where(side == 1, pair[1], pair[0])
        message[i] = halves(jnp.where(side == 1, pair[0], pair[1]))
    for s in range(ends):
        message[slots // 2 + s] = went[slots + s]
        message[slots // 2 + ends + s] = came[slots + s]


def merge(z, bit, kept, came, went):
    slots = kept.shape[0]
    ends = came.shape[0] - slots
    return pl.pallas_call(
        functools.partial(merge_kernel, z, bit),
        in_specs=[VMEM_SPEC] * 3,
        out_specs=[VMEM_SPEC] * 2,
        out_shape=[
            jax.ShapeDtypeStruct((slots // 2 + 2 * ends, z.spec_rows, LANES), BF),
            jax.ShapeDtypeStruct((slots // 2, z.spec_rows, LANES), F32),
        ],
        compiler_params=params(),
        name="merge",
    )(kept, came, went)


def cross_kernel(z, offsets, pairs, stacks, *refs):
    pieces, out = refs[:-1], refs[-1]
    here = position("sta")
    mine = pieces[0][...]
    bins = z.bins
    sides = []
    for i in range(z.stations):
        re, im = mine[2 * i : 2 * i + 1], mine[2 * i + 1 : 2 * i + 2]
        sides.append((jnp.concatenate([re, im], axis=0), jnp.concatenate([im, -re], axis=0)))
    for k, (offset, piece) in enumerate(zip(offsets, pieces)):
        on = jnp.concatenate([pairs[k]] * (bins // LANES), axis=1)
        for j in range(z.stations):
            re = jnp.broadcast_to(piece[2 * j : 2 * j + 1, :], (2, bins)) * on
            im = jnp.broadcast_to(piece[2 * j + 1 : 2 * j + 2, :], (2, bins)) * on
            column = (here ^ offset) * z.stations + j
            for i, (p, q) in enumerate(sides):
                out[i, column] = stacks[i, column] + (re * p + im * q)


def cross(z, offsets, pairs, stacks, pieces):
    return pl.pallas_call(
        functools.partial(cross_kernel, z, offsets),
        in_specs=[VMEM_SPEC] * (2 + len(pieces)),
        out_specs=VMEM_SPEC,
        out_shape=jax.ShapeDtypeStruct(stacks.shape, F32),
        compiler_params=params(),
        name="cross",
    )(pairs, stacks, *pieces)


def shards(traces, station_flags, tile_mask, band_block, stacks):
    tm_count, sta_count = lax.axis_size("tm"), lax.axis_size("sta")
    stations, length = traces.shape
    z = Sizes(stations, length, tm_count, stacks.shape[-1])
    assert sta_count & (sta_count - 1) == 0
    offsets = [0]
    bits = [1 << k for k in reversed(range(sta_count.bit_length() - 1))]
    for bit in bits:
        offsets += [offset ^ bit for offset in offsets]
    if tm_count in (4, 8, 16):
        message, home = split_transform(z, station_flags, traces)
        for k in range(tm_count.bit_length() - 1):
            swap = [(i, i ^ (1 << k)) for i in range(tm_count)]
            came, went = lax.ppermute(message, "tm", swap), message
            if k == 0:
                kept = home()
            if 2 << k < tm_count:
                message, kept = merge(z, k + 1, kept, came, went)
        *made, pairs = tables(z, offsets, z.lift, 1, band_block, station_flags, tile_mask)
        white = gathered(z, kept, came, went, made)
    else:
        sent = transform(z, station_flags, traces)
        got = lax.all_to_all(sent, "tm", split_axis=0, concat_axis=0, tiled=True)
        *made, pairs = tables(
            z, offsets, z.half, tm_count, band_block, station_flags, tile_mask
        )
        white = spectrum(z, got, made)
    pieces = [white]
    for bit in bits:
        swap = [(i, i ^ bit) for i in range(sta_count)]
        pieces += [lax.ppermute(piece, "sta", swap) for piece in pieces]
    return cross(z, offsets, pairs, stacks, pieces)


def solution(mesh):
    return jax.shard_map(
        shards,
        mesh=mesh,
        in_specs=(P("sta", "tm"), P("sta"), P(), P(), P("sta", None, None, "tm")),
        out_specs=P("sta", None, None, "tm"),
        check_vma=False,
    )
```

```python
import functools
import math

import jax
import jax.numpy as jnp
import numpy as np
from jax import lax
from jax.experimental import pallas as pl
from jax.experimental.pallas import tpu as pltpu
from jax.sharding import PartitionSpec as P

HALF_WIN = 512
SMOOTH = 32
EPS_MEAN = 1e-06
EPS_POWER = 1e-06
LANES = 128
SPAN = 2 * HALF_WIN
TILES = SPAN // LANES
HALF_TILES = HALF_WIN // LANES
PAD = 16
BAND_TOP = 137
WIDTH = 2 * LANES
CHUNKS = SPAN // WIDTH
position = lax.axis_index
VMEM_LIMIT = 16 * 1024 * 1024
BF = jnp.bfloat16
F32 = jnp.float32


def up_to(value, step):
    return -(-value // step) * step


def sincos(turns):
    quarter = jnp.round(turns * 4.0)
    rest = turns - quarter * 0.25
    y = rest * (2.0 * math.pi)
    y2 = y * y
    s = y + y * y2 * (-1.0 / 6 + y2 * (1.0 / 120 + y2 * (-1.0 / 5040 + y2 * (1.0 / 362880))))
    c = 1.0 + y2 * (-0.5 + y2 * (1.0 / 24 + y2 * (-1.0 / 720 + y2 * (1.0 / 40320))))
    q = quarter - 4.0 * jnp.floor(quarter * 0.25)
    swap = (q == 1.0) | (q == 3.0)
    sine = jnp.where(swap, c, s)
    cosine = jnp.where(swap, s, c)
    sine = jnp.where(q >= 2.0, -sine, sine)
    cosine = jnp.where((q == 1.0) | (q == 2.0), -cosine, cosine)
    return sine, cosine


def turns_of(product, period):
    whole = jnp.floor(product * (1.0 / period))
    return (product - whole * period) * (1.0 / period)


def split2(value):
    high = value.astype(BF)
    return high, (value - high.astype(F32)).astype(BF)


def iota(shape, axis):
    return lax.broadcasted_iota(jnp.int32, shape, axis)


def iota_f(shape, axis):
    return iota(shape, axis).astype(F32)


def window_tables():
    row, lane = iota((LANES, LANES), 0), iota((LANES, LANES), 1)
    upto = (row <= lane).astype(F32).astype(BF)
    onward = (row >= lane).astype(F32).astype(BF)
    return upto, onward, jnp.ones((LANES, LANES), BF)


def np_split(value):
    high = value.astype(jnp.bfloat16).astype(np.float64)
    return high, (value - high).astype(jnp.bfloat16).astype(np.float64)


class Sizes:
    def __init__(self, stations, length, tm_count, bins):
        self.stations, self.length, self.tm, self.bins = stations, length, tm_count, bins
        self.rows = length // SPAN
        self.half = self.rows // 2 + 1
        self.pad = up_to(self.rows, PAD)
        self.full = self.rows // PAD * PAD
        self.tail = self.rows - self.full
        self.depth = 3 * self.full + PAD
        self.block = min(tm_count, 16)
        self.blocks = tm_count // self.block
        self.folds = (BAND_TOP + bins - 1) // self.rows + 1
        self.lift = up_to(self.half, 2)
        self.spec_rows = up_to(2 * self.lift, 8)
        self.edge_rows = 2 * stations * TILES
        self.sent_rows = self.spec_rows + self.edge_rows
        assert length % SPAN == 0 and tm_count % self.block == 0
        assert stations == 2 and self.folds <= PAD
        assert self.rows >= 2 and 0 < 3 * self.tail <= 8 and self.depth <= LANES

    def parity_tables(self):
        residue = np.arange(self.tm).reshape(-1, 2).T[:, None, :]
        order = (residue + self.tm * np.arange(self.lift)[None, :, None]).reshape(2, -1)
        return self.first_of(order), self.turn_of(order)

    def row_order(self):
        j2 = np.arange(self.tm)[:, None] + self.tm * np.arange(self.half)[None, :]
        return j2.reshape(self.blocks, self.block, self.half).transpose(0, 2, 1).reshape(self.blocks, -1)

    def first_table(self):
        return self.first_of(self.row_order())

    def turn_table(self):
        return self.turn_of(self.row_order())

    def first_of(self, order):
        period = self.tm * self.rows
        angle = 2.0 * np.pi / period * (order[:, :, None] * np.arange(self.rows) % period)
        parts = np.concatenate([np.cos(angle), -np.sin(angle)], axis=1)
        full, rest = parts[..., : self.full], parts[..., self.full :]
        table = np.concatenate([full, full, full, rest, rest, rest], axis=2)
        return np.pad(table, ((0, 0), (0, 0), (0, LANES - table.shape[2]))).astype(np.float32)

    def low_lanes(self, lane):
        at = 3 * self.full
        third = (lane >= 2 * self.full) & (lane < at)
        return third | ((lane >= at + 2 * self.tail) & (lane < at + 3 * self.tail))

    def turn_of(self, order):
        order = order.reshape(order.shape[0], 1, -1, 1)
        time = np.arange(SPAN).reshape(CHUNKS, 1, WIDTH)
        angle = 2.0 * np.pi / (self.tm * self.length) * (order * time)
        return np.stack([np.cos(angle), -np.sin(angle)], axis=2).astype(np.float32)


def unpack(z, x, xs, edges):
    rows, top = z.rows, 8
    for a in range(rows):
        xs[:, top + a, :] = x[:, a * SPAN : (a + 1) * SPAN].astype(F32)
    for s in range(z.stations):
        for side, a in ((0, 0), (1, rows - 1)):
            for c in range(TILES):
                at = (side * z.stations + s) * TILES + c
                edges[at : at + 1, :] = xs[s, top + a : top + a + 1, c * LANES : (c + 1) * LANES]


def window(z, s, xs, sums):
    rows, pad, top = z.rows, z.pad, 8
    short = up_to(rows, 8)
    kernel = jnp.concatenate(window_tables()[:2], axis=1)
    group = 4
    for c0 in range(0, TILES, group):
        parts = [
            jnp.abs(xs[s, top : top + pad, c * LANES : (c + 1) * LANES])
            for c in range(c0, c0 + group)
        ]
        part = jnp.concatenate([part.astype(BF) for part in parts], axis=0)
        got = jnp.dot(part, kernel, preferred_element_type=F32)
        for k in range(group):
            value = got[k * pad : k * pad + short]
            upto, onward = value[:, :LANES], value[:, LANES:]
            sums[s, c0 + k, top : top + short, 0 : 2 * LANES] = value
            sums[s, c0 + k, top : top + short, 2 * LANES :] = upto + (onward - parts[k][:short])
    blank = jnp.zeros((1, HALF_WIN), F32)
    xs[s, top : top + 1, 0:HALF_WIN] = blank
    xs[s, top + rows - 1 : top + rows, HALF_WIN:SPAN] = blank


def level(z, s, tiles, xs, sums, stack):
    rows, top = z.rows, 8
    short = up_to(rows, 8)

    def tile(kind, c):
        turn, cc = divmod(c, TILES)
        lines = slice(top + turn, top + turn + short)
        return sums[s, cc, lines, kind * LANES : (kind + 1) * LANES]

    first = tiles[0] + 1 - HALF_TILES
    single = [tile(2, c) for c in range(first, tiles[-1] + HALF_TILES)]
    twos = [single[c] + single[c + 1] for c in range(len(single) - 1)]
    for k, c in enumerate(tiles):
        inner = (twos[k] + twos[k + 2]) + (twos[k + 4] + single[k + 6])
        total = inner + (tile(1, c - HALF_TILES) + tile(0, c + HALF_TILES))
        value = xs[s, top : top + short, c * LANES : (c + 1) * LANES]
        value = value / (total * (1.0 / (2 * HALF_WIN + 1)) + EPS_MEAN)
        high, low = split2(value[: z.full])
        lanes = slice(c * LANES, (c + 1) * LANES)
        for k2, part in enumerate((high, low, high)):
            stack[s, k2 * z.full : (k2 + 1) * z.full, lanes] = part
        rest = value[z.full :]
        high = rest.astype(BF).astype(F32)
        rest = high + pltpu.roll(rest - high, z.tail, 0) + pltpu.roll(high, 2 * z.tail, 0)
        rest = jnp.concatenate([rest, jnp.zeros((PAD - rest.shape[0], LANES), F32)], axis=0)
        stack[s, 3 * z.full :, lanes] = rest.astype(BF)


def fold_weights(weight):
    lane = iota((PAD, SPAN), 1)
    for kind in range(2):
        turns = jnp.bitwise_and((iota((PAD, SPAN), 0) + kind) * lane, SPAN - 1).astype(F32)
        sine, cosine = sincos(turns * (1.0 / SPAN))
        for h, (s, c) in enumerate(zip(split2(sine), split2(cosine))):
            table = ((c, s), (-s, c)) if kind == 0 else ((c, -s), (-s, -c))
            for part in range(2):
                at = h * 4 * PAD + kind * 2 * PAD + part * PAD
                for side in range(2):
                    for g in range(CHUNKS):
                        to = (2 * g + side) * WIDTH
                        weight[at : at + PAD, to : to + WIDTH] = table[part][side][
                            :, g * WIDTH : (g + 1) * WIDTH
                        ]


def transform_kernel(
    z, flags, x, first, turn, out,
    flags_s, x_v, first_v, turn_v, table, xs, sums, stack, edges, weight, acc, both, spec, sems,
):
    half, block, tm = z.half, z.block, z.tm
    height = half * block
    index = pl.program_id(0)
    top, rows, pad = 8, z.rows, z.pad
    get_first = pltpu.make_async_copy(first.at[index], first_v, sems.at[2])
    get_turn = [
        pltpu.make_async_copy(turn.at[index, g], turn_v.at[g], sems.at[3 + g]) for g in range(CHUNKS)
    ]

    def prologue():
        copies = [
            pltpu.make_async_copy(x, x_v, sems.at[0]),
            pltpu.make_async_copy(flags, flags_s, sems.at[1]),
        ]
        for copy in copies + [get_first] + get_turn:
            copy.start()
        full = rows // 8 * 8
        for s in range(z.stations):
            xs[s, top + full : top + pad, :] = jnp.zeros((pad - full, SPAN), F32)
            for c in range(TILES):
                sums[s, c, 0:top, :] = jnp.zeros((top, 3 * LANES), F32)
                sums[s, c, top + up_to(rows, 8) :, :] = jnp.zeros((8, 3 * LANES), F32)
        spec[:, z.spec_rows - 8 : z.spec_rows, :] = jnp.zeros((tm, 8, LANES), F32)
        fold_weights(weight)
        for copy in copies:
            copy.wait()
        unpack(z, x_v, xs, edges)
        for s in range(z.stations):
            window(z, s, xs, sums)
            if s == 0 or z.blocks > 1:
                level(z, s, range(TILES), xs, sums, stack)

    if z.blocks == 1:
        prologue()
    else:
        pl.when(index == 0)(prologue)

        @pl.when(index > 0)
        def _():
            for copy in [get_first] + get_turn:
                copy.start()

    for copy in [get_first] + get_turn:
        copy.wait()
    residue = index * block + iota((block, LANES), 0)
    sine, cosine = sincos(turns_of((position("tm") * residue).astype(F32), tm))
    f_re = first_v[:height].reshape(half, block, LANES)
    f_im = first_v[height:].reshape(half, block, LANES)
    low = z.low_lanes(iota((height, LANES), 1))
    for k, value in enumerate(
        (f_re * cosine[None] + f_im * sine[None], f_im * cosine[None] - f_re * sine[None])
    ):
        value = value.reshape(height, LANES)
        high = value.astype(BF).astype(F32)
        table[k * height : (k + 1) * height, :] = jnp.where(low, value - high, high).astype(BF)

    def first_stage(s, g):
        return jnp.dot(
            table[:, : z.depth],
            stack[s, :, g * WIDTH : (g + 1) * WIDTH],
            preferred_element_type=F32,
        )

    def second_stage(s, g, parts):
        w = weight[:, 2 * g * WIDTH : 2 * (g + 1) * WIDTH]
        got = lax.dot_general(parts, w, (((1,), (1,)), ((), ())), preferred_element_type=F32)
        value = got[:height] + got[height:]
        acc[s] = value if g == 0 else acc[s] + value

    def settle(s):
        value = acc[s] + pltpu.roll(acc[s], LANES // 2, 1)
        return value * flags_s[s].astype(F32)

    steps = [(s, g) for s in range(z.stations) for g in range(CHUNKS)]
    coming = first_stage(*steps[0])
    waiting = None
    for k, (s, g) in enumerate(steps):
        f_re, f_im = coming[:height], coming[height:]
        t_re, t_im = turn_v[g, 0], turn_v[g, 1]
        re_h, re_l = split2(f_re * t_re - f_im * t_im)
        im_h, im_l = split2(f_re * t_im + f_im * t_re)
        parts = jnp.concatenate(
            [jnp.concatenate([re_h, im_h], axis=1), jnp.concatenate([re_l, im_l], axis=1)], axis=0
        )
        if s == 0 and z.blocks == 1:
            level(z, 1, range(2 * g, 2 * g + 2), xs, sums, stack)
        if k + 1 < len(steps):
            coming = first_stage(*steps[k + 1])
        if waiting is not None:
            second_stage(*steps[k - 1], waiting)
        waiting = parts
    second_stage(*steps[-1], waiting)
    zero, one = settle(0), settle(1)
    lane = iota((height, LANES), 1)
    early = jnp.bitwise_and(lane, LANES // 2 - 1) < LANES // 4
    direct = jnp.where(early, zero, pltpu.roll(one, LANES // 4, 1))
    mirror = jnp.where(early, pltpu.roll(zero, LANES // 4, 1), one)
    for kind, value in enumerate((direct, mirror)):
        high = value.astype(BF).astype(F32)
        both[kind] = jnp.where(lane < LANES // 2, high, value - high)
    for k in range(block):
        here = index * block + k
        there = jnp.where(here == 0, 0, tm - here) if z.blocks > 1 else (tm - k) % tm
        here = here if z.blocks > 1 else k
        lines = pl.ds(k, half, stride=block)
        spec[here, 0:half, :] = both[0, lines, :]
        spec[there, half : 2 * half, :] = both[1, lines, :]

    def finish():
        ends = edges[...].astype(BF)

        def one_row(k, carry):
            out[k, 0 : z.spec_rows, :] = spec[k].astype(BF)
            out[k, z.spec_rows : z.sent_rows, :] = ends
            return carry

        if z.blocks == 1:
            for k in range(tm):
                one_row(k, 0)
        else:
            lax.fori_loop(0, tm, one_row, 0)

    if z.blocks == 1:
        finish()
    else:
        pl.when(index == z.blocks - 1)(finish)


SMEM_SPEC = pl.BlockSpec(memory_space=pltpu.SMEM)
VMEM_SPEC = pl.BlockSpec(memory_space=pltpu.VMEM)
HBM_SPEC = pl.BlockSpec(memory_space=pltpu.HBM)


def params():
    return pltpu.CompilerParams(vmem_limit_bytes=VMEM_LIMIT)


def transform(z, flags, x):
    height = z.half * z.block
    first, turn = z.first_table(), z.turn_table()
    return pl.pallas_call(
        functools.partial(transform_kernel, z),
        grid=(z.blocks,),
        in_specs=[HBM_SPEC] * 4,
        out_specs=VMEM_SPEC,
        out_shape=jax.ShapeDtypeStruct((z.tm, z.sent_rows, LANES), BF),
        scratch_shapes=[
            pltpu.SMEM((z.stations,), jnp.int32),
            pltpu.VMEM(x.shape, BF),
            pltpu.VMEM(first.shape[1:], F32),
            pltpu.VMEM(turn.shape[1:], F32),
            pltpu.VMEM(first.shape[1:], BF),
            pltpu.VMEM((z.stations, 8 + z.pad, SPAN), F32),
            pltpu.VMEM((z.stations, TILES, 16 + up_to(z.rows, 8), 3 * LANES), F32),
            pltpu.VMEM((z.stations, z.depth, SPAN), BF),
            pltpu.VMEM((z.edge_rows, LANES), F32),
            pltpu.VMEM((LANES, 2 * SPAN), BF),
            pltpu.VMEM((z.stations, height, LANES), F32),
            pltpu.VMEM((2, height, LANES), F32),
            pltpu.VMEM((z.tm, z.spec_rows, LANES), F32),
            pltpu.SemaphoreType.DMA((3 + CHUNKS,)),
        ],
        name="transform",
    )(flags, x, jnp.asarray(first), jnp.asarray(turn))


def table_kernel(
    z, offsets, split, band, flags, mask, choose, keep, steps, turns, near, phase, switch, pairs,
    band_s, flags_s, mask_s, sems,
):
    rows, tm, bins, half = z.rows, z.tm, z.bins, z.half
    copies = [
        pltpu.make_async_copy(band, band_s, sems.at[0]),
        pltpu.make_async_copy(flags, flags_s, sems.at[1]),
        pltpu.make_async_copy(mask, mask_s, sems.at[2]),
    ]
    for copy in copies:
        copy.start()
    for copy in copies:
        copy.wait()
    here = position("sta")
    for k, offset in enumerate(offsets):
        pairs[k] = jnp.full((2, LANES), mask_s[here, here ^ offset].astype(F32))
    base, residue = band_s[0, 0], position("tm")
    for s in range(z.stations):
        switch[s] = jnp.full((TILES, LANES), flags_s[s].astype(F32))
    spot = iota_f((1, bins), 1) + base.astype(F32)
    fold = jnp.floor((spot + 0.5) * (1.0 / rows))
    rest = spot - fold * rows
    row = iota_f((z.spec_rows, bins), 0)
    last = (rows - 1 + split + (residue == 0).astype(jnp.int32)).astype(F32)
    mirror = jnp.where((row >= split) & (last - row >= half), last - row, -1.0)
    one = (jnp.where(row < half, row, mirror) == rest).astype(F32).astype(BF)
    for p in range(choose.shape[0]):
        choose[p] = one
    keep[...] = (iota_f((PAD, bins), 0) == fold).astype(F32)
    freq = (residue + tm * (base + iota((1, bins), 1))).astype(F32)
    step = iota_f((TILES, bins), 0) - HALF_TILES
    sine, cosine = sincos(turns_of(step * freq, tm * (z.length // LANES)))
    table = jnp.concatenate(
        [jnp.concatenate([cosine, -sine], axis=1), jnp.concatenate([sine, cosine], axis=1)], axis=0
    )
    high, low = split2(table)
    for k, part in enumerate((high, high, low, low)):
        steps[k * 2 * TILES : (k + 1) * 2 * TILES, :] = part
    sine, cosine = sincos(turns_of(iota_f((LANES, bins), 0) * freq, tm * z.length))
    turns[0] = cosine
    turns[1] = sine
    gap = jnp.abs(iota((bins, bins), 0) - iota((bins, bins), 1))
    near[...] = (gap <= SMOOTH).astype(F32).astype(BF)
    p_sin, p_cos = sincos(turns_of((residue * iota((tm, LANES), 0)).astype(F32), tm))
    phase[0] = p_cos
    phase[1] = -p_sin


def tables(z, offsets, split, copies, band, flags, mask):
    return pl.pallas_call(
        functools.partial(table_kernel, z, offsets, split),
        in_specs=[HBM_SPEC] * 3,
        out_specs=[VMEM_SPEC] * 8,
        scratch_shapes=[
            pltpu.SMEM((1, 1), jnp.int32),
            pltpu.SMEM((z.stations,), jnp.int32),
            pltpu.SMEM(mask.shape, jnp.int32),
            pltpu.SemaphoreType.DMA((3,)),
        ],
        out_shape=[
            jax.ShapeDtypeStruct((copies, z.spec_rows, z.bins), BF),
            jax.ShapeDtypeStruct((PAD, z.bins), F32),
            jax.ShapeDtypeStruct((8 * TILES, 2 * z.bins), BF),
            jax.ShapeDtypeStruct((2, LANES, z.bins), F32),
            jax.ShapeDtypeStruct((z.bins, z.bins), BF),
            jax.ShapeDtypeStruct((2, z.tm, LANES), F32),
            jax.ShapeDtypeStruct((z.stations, TILES, LANES), F32),
            jax.ShapeDtypeStruct((len(offsets), 2, LANES), F32),
        ],
        compiler_params=params(),
        cost_estimate=pl.CostEstimate(flops=4000000, bytes_accessed=2000000, transcendentals=0),
        name="tables",
    )(band.reshape(1, 1), flags, mask)


def sublane_sums(value, row):
    total = value
    for shift in (1, 2, 4):
        total = total + jnp.where(row >= shift, pltpu.roll(total, shift, 0), 0.0)
    return total - value, total


def spectrum_kernel(z, got, choose, keep, steps, turns, near, phase, switch, out):
    tm, bins, at = z.tm, z.bins, z.spec_rows
    parts = got[:, 0:at, :].astype(F32).reshape(tm * at, LANES).astype(BF)
    weights = choose[...].astype(F32).reshape(tm * at, bins).astype(BF)
    placed = lax.dot_general(parts, weights, (((0,), (0,)), ((), ())), preferred_element_type=F32)
    side_rows = z.stations * TILES
    ends = [
        got[:, at + k * side_rows : at + (k + 1) * side_rows, :].astype(F32).reshape(-1, LANES)
        for k in range(2)
    ]
    whiten(z, placed, ends, keep, steps, turns, near, phase, switch, out)


def gathered_kernel(
    z, kept, came, went, choose, keep, steps, turns, near, phase, switch, out, ends
):
    tm = z.tm
    piece = came[0].astype(F32)
    total = kept[0] + (piece + pltpu.roll(piece, LANES // 2, 1))
    placed = lax.dot_general(
        halves(total), choose[0], (((0,), (0,)), ((), ())), preferred_element_type=F32
    )
    here = position("tm")
    for s in range(tm):
        source, slot = (went, s) if s < tm // 2 else (came, s - tm // 2)
        ends[here ^ s] = source[1 + slot, 0 : z.edge_rows, :].astype(F32)
    side_rows = z.stations * TILES
    sides = [ends[:, k * side_rows : (k + 1) * side_rows, :].reshape(-1, LANES) for k in range(2)]
    whiten(z, placed, sides, keep, steps, turns, near, phase, switch, out)


def halves(value):
    high = value.astype(BF).astype(F32)
    return jnp.where(iota(value.shape, 1) < LANES // 2, high, value - high).astype(BF)


def whiten(z, placed, ends, keep, steps, turns, near, phase, switch, out):
    tm, bins = z.tm, z.bins
    mask = keep[...]
    folded = [
        jnp.sum(placed[k * PAD : (k + 1) * PAD] * mask, axis=0, keepdims=True)
        for k in range(4 * z.stations)
    ]
    spec = [folded[k] + folded[k + 2 * z.stations] for k in range(2 * z.stations)]
    upto, onward, ones = window_tables()
    row = iota((TILES, LANES), 0)
    late = row >= HALF_TILES
    sides = []
    for value, table in zip(ends, (upto, onward)):
        sums = jnp.dot(
            jnp.abs(value).astype(BF),
            jnp.concatenate([table, ones], axis=1),
            preferred_element_type=F32,
        )
        sides.append((value, sums))
    mixed = []
    for s in range(z.stations):
        real = jnp.zeros((TILES, LANES), F32)
        imag = jnp.zeros((TILES, LANES), F32)
        flag = switch[s]
        for p in range(tm):
            begin = (p * z.stations + s) * TILES
            before = ((p - 1) % tm * z.stations + s) * TILES
            value_r, sums_r = (v[begin : begin + TILES] for v in sides[0])
            value_l, sums_l = (v[before : before + TILES] for v in sides[1])
            earlier, _ = sublane_sums(sums_r[:, LANES:], row)
            right = sums_r[:, :LANES] + earlier
            tail = sums_l[:, LANES:]
            for shift in (1, 2, 4):
                tail = tail + jnp.where(row < TILES - shift, pltpu.roll(tail, TILES - shift, 0), 0.0)
            left = sums_l[:, :LANES] + jnp.where(
                row < TILES - 1, pltpu.roll(tail, TILES - 1, 0), 0.0
            )
            total = left + right if p else jnp.where(late, right, left)
            sample = pltpu.roll(jnp.where(late, value_l, value_r), HALF_TILES, 0)
            value = flag * sample / (total * (1.0 / (2 * HALF_WIN + 1)) + EPS_MEAN)
            real = real + value * phase[0, p : p + 1, :]
            imag = imag + value * phase[1, p : p + 1, :]
        mixed.append(jnp.concatenate([real, imag], axis=0))
    high, low = split2(jnp.concatenate(mixed, axis=1))
    spread = lax.dot_general(
        jnp.concatenate([high, low, high, low], axis=0),
        steps[...],
        (((0,), (0,)), ((), ())),
        preferred_element_type=F32,
    )
    cosine, sine = turns[0], turns[1]
    pieces = []
    for s in range(z.stations):
        g_re = spread[s * LANES : (s + 1) * LANES, :bins]
        g_im = spread[s * LANES : (s + 1) * LANES, bins:]
        spec[2 * s] += jnp.sum(g_re * cosine + g_im * sine, axis=0, keepdims=True)
        spec[2 * s + 1] += jnp.sum(g_im * cosine - g_re * sine, axis=0, keepdims=True)
        power = spec[2 * s] * spec[2 * s] + spec[2 * s + 1] * spec[2 * s + 1]
        for _ in range(3):
            part = power.astype(BF).astype(F32)
            pieces.append(part)
            power = power - part
    pieces.append(jnp.zeros((8 - len(pieces), bins), F32))
    smooth = jnp.dot(
        jnp.concatenate(pieces, axis=0).astype(BF), near[...], preferred_element_type=F32
    )
    for s in range(z.stations):
        mean = smooth[3 * s : 3 * s + 1] + smooth[3 * s + 1 : 3 * s + 2] + smooth[3 * s + 2 : 3 * s + 3]
        scale = 1.0 / jnp.sqrt(mean * (1.0 / (2 * SMOOTH + 1)) + EPS_POWER)
        out[2 * s : 2 * s + 1, :] = spec[2 * s] * scale
        out[2 * s + 1 : 2 * s + 2, :] = spec[2 * s + 1] * scale


def spectrum(z, got, made):
    return pl.pallas_call(
        functools.partial(spectrum_kernel, z),
        in_specs=[VMEM_SPEC] * 8,
        out_specs=VMEM_SPEC,
        out_shape=jax.ShapeDtypeStruct((2 * z.stations, z.bins), F32),
        compiler_params=params(),
        name="spectrum",
    )(got, *made)


def gathered(z, kept, came, went, made):
    return pl.pallas_call(
        functools.partial(gathered_kernel, z),
        in_specs=[VMEM_SPEC] * 10,
        out_specs=VMEM_SPEC,
        out_shape=jax.ShapeDtypeStruct((2 * z.stations, z.bins), F32),
        scratch_shapes=[pltpu.VMEM((z.tm, z.edge_rows, LANES), F32)],
        compiler_params=params(),
        name="spectrum",
    )(kept, came, went, *made)


def half_transform(z, parity, table, turn, stack, weight, flags, acc, both, spec, before):
    count, lift = z.tm // 2, z.lift
    height = lift * count

    def first_stage(s, g):
        return jnp.dot(
            table[:, : z.depth],
            stack[s, :, g * WIDTH : (g + 1) * WIDTH],
            preferred_element_type=F32,
        )

    def second_stage(s, g, parts):
        w = weight[:, 2 * g * WIDTH : 2 * (g + 1) * WIDTH]
        got = lax.dot_general(parts, w, (((1,), (1,)), ((), ())), preferred_element_type=F32)
        value = got[:height] + got[height:]
        acc[s] = value if g == 0 else acc[s] + value

    def settle(s):
        return (acc[s] + pltpu.roll(acc[s], LANES // 2, 1)) * flags[s, 0:1, :]

    steps = [(s, g) for s in range(z.stations) for g in range(CHUNKS)]
    coming = first_stage(*steps[0])
    waiting = None
    for k, (s, g) in enumerate(steps):
        f_re, f_im = coming[:height], coming[height:]
        t_re, t_im = turn[g, 0], turn[g, 1]
        re_h, re_l = split2(f_re * t_re - f_im * t_im)
        im_h, im_l = split2(f_re * t_im + f_im * t_re)
        parts = jnp.concatenate(
            [jnp.concatenate([re_h, im_h], axis=1), jnp.concatenate([re_l, im_l], axis=1)], axis=0
        )
        if before is not None and s == 0:
            before(g)
        if k + 1 < len(steps):
            coming = first_stage(*steps[k + 1])
        if waiting is not None:
            second_stage(*steps[k - 1], waiting)
        waiting = parts
    second_stage(*steps[-1], waiting)
    zero, one = settle(0), settle(1)
    lane = iota((height, LANES), 1)
    early = jnp.bitwise_and(lane, LANES // 2 - 1) < LANES // 4
    both[0] = jnp.where(early, zero, pltpu.roll(one, LANES // 4, 1))
    both[1] = jnp.where(early, pltpu.roll(zero, LANES // 4, 1), one)
    for j in range(count):
        lines = pl.ds(j, lift, stride=count)
        spec[j, 0:lift, :] = both[0, lines, :]
        spec[lax.rem(2 * count - parity - j, count), lift : 2 * lift, :] = both[1, lines, :]


def stretch_table(z, parity, first, table):
    count, height = z.tm // 2, z.lift * (z.tm // 2)
    low = z.low_lanes(iota((height, LANES), 1))
    residue = 2 * iota((count, LANES), 0) + parity
    sine, cosine = sincos(turns_of((position("tm") * residue).astype(F32), z.tm))
    f_re = first[:height].reshape(z.lift, count, LANES)
    f_im = first[height:].reshape(z.lift, count, LANES)
    for k, value in enumerate(
        (f_re * cosine[None] + f_im * sine[None], f_im * cosine[None] - f_re * sine[None])
    ):
        value = value.reshape(height, LANES)
        high = value.astype(BF).astype(F32)
        table[k * height : (k + 1) * height, :] = jnp.where(low, value - high, high).astype(BF)


def away_kernel(
    z, flags, x, first, turn, message, stack, weight, home_first, home_turn, switch,
    flags_s, x_v, first_v, turn_v, table, xs, sums, edges, acc, both, spec, sems,
):
    rows, pad, top = z.rows, z.pad, 8
    count = z.tm // 2
    here = position("tm")
    home = jnp.bitwise_and(here, 1)
    away = 1 - home
    copies = [
        pltpu.make_async_copy(x, x_v, sems.at[0]),
        pltpu.make_async_copy(flags, flags_s, sems.at[1]),
        pltpu.make_async_copy(first.at[away], first_v, sems.at[2]),
        pltpu.make_async_copy(turn.at[away], turn_v, sems.at[3]),
        pltpu.make_async_copy(turn.at[home], home_turn, sems.at[4]),
        pltpu.make_async_copy(first.at[home], home_first, sems.at[5]),
    ]
    for copy in copies:
        copy.start()
    full = rows // 8 * 8
    for s in range(z.stations):
        xs[s, top + full : top + pad, :] = jnp.zeros((pad - full, SPAN), F32)
        for c in range(TILES):
            sums[s, c, 0:top, :] = jnp.zeros((top, 3 * LANES), F32)
            sums[s, c, top + up_to(rows, 8) :, :] = jnp.zeros((8, 3 * LANES), F32)
    spec[:, z.spec_rows - 8 : z.spec_rows, :] = jnp.zeros((count, 8, LANES), F32)
    fold_weights(weight)
    copies[0].wait()
    copies[1].wait()
    unpack(z, x_v, xs, edges)
    for s in range(z.stations):
        window(z, s, xs, sums)
        switch[s] = jnp.full((TILES, LANES), flags_s[s].astype(F32))
    level(z, 0, range(TILES), xs, sums, stack)
    copies[2].wait()
    copies[3].wait()
    stretch_table(z, away, first_v, table)
    half_transform(
        z, away, table, turn_v, stack, weight, switch, acc, both, spec,
        lambda g: level(z, 1, range(2 * g, 2 * g + 2), xs, sums, stack),
    )
    copies[4].wait()
    copies[5].wait()
    for j in range(count):
        message[j] = halves(spec[j])
    message[count, 0 : z.edge_rows, :] = edges[...].astype(BF)
    message[count, z.edge_rows :, :] = jnp.zeros((z.spec_rows - z.edge_rows, LANES), BF)


def home_kernel(z, stack, weight, first, turn, switch, kept, table, acc, both):
    kept[:, z.spec_rows - 8 : z.spec_rows, :] = jnp.zeros((z.tm // 2, 8, LANES), F32)
    parity = jnp.bitwise_and(position("tm"), 1)
    stretch_table(z, parity, first, table)
    half_transform(z, parity, table, turn, stack, weight, switch, acc, both, kept, None)


def split_transform(z, flags, x):
    count, height = z.tm // 2, z.lift * (z.tm // 2)
    first, turn = z.parity_tables()
    state = [
        jax.ShapeDtypeStruct((z.stations, z.depth, SPAN), BF),
        jax.ShapeDtypeStruct((LANES, 2 * SPAN), BF),
        jax.ShapeDtypeStruct(first.shape[1:], F32),
        jax.ShapeDtypeStruct(turn.shape[1:], F32),
        jax.ShapeDtypeStruct((z.stations, TILES, LANES), F32),
    ]
    inputs = [flags, x, jnp.asarray(first), jnp.asarray(turn)]
    work = [
        pltpu.VMEM((z.stations, height, LANES), F32),
        pltpu.VMEM((2, height, LANES), F32),
    ]
    message, *state = pl.pallas_call(
        functools.partial(away_kernel, z),
        in_specs=[HBM_SPEC] * 4,
        out_specs=[VMEM_SPEC] * 6,
        out_shape=[jax.ShapeDtypeStruct((count + 1, z.spec_rows, LANES), BF)] + state,
        scratch_shapes=[
            pltpu.SMEM((z.stations,), jnp.int32),
            pltpu.VMEM(x.shape, BF),
            pltpu.VMEM(first.shape[1:], F32),
            pltpu.VMEM(turn.shape[1:], F32),
            pltpu.VMEM(first.shape[1:], BF),
            pltpu.VMEM((z.stations, 8 + z.pad, SPAN), F32),
            pltpu.VMEM((z.stations, TILES, 16 + up_to(z.rows, 8), 3 * LANES), F32),
            pltpu.VMEM((z.edge_rows, LANES), F32),
            *work,
            pltpu.VMEM((count, z.spec_rows, LANES), F32),
            pltpu.SemaphoreType.DMA((6,)),
        ],
        compiler_params=params(),
        name="away",
    )(*(in_hbm(value) for value in inputs))

    def home():
        return pl.pallas_call(
            functools.partial(home_kernel, z),
            in_specs=[VMEM_SPEC] * 5,
            out_specs=VMEM_SPEC,
            out_shape=jax.ShapeDtypeStruct((count, z.spec_rows, LANES), F32),
            scratch_shapes=[pltpu.VMEM(first.shape[1:], BF), *work],
            compiler_params=params(),
            cost_estimate=pl.CostEstimate(flops=10**9, bytes_accessed=10**6, transcendentals=0),
            name="home",
        )(*state)

    return message, home


def in_hbm(value):
    return pltpu.with_memory_space_constraint(value, pltpu.HBM)


def merge_kernel(z, bit, kept, came, went, message, left):
    slots = kept.shape[0]
    ends = came.shape[0] - slots
    side = jnp.bitwise_and(position("tm") >> bit, 1)
    for i in range(slots // 2):
        pair = []
        for j in (2 * i, 2 * i + 1):
            piece = came[j].astype(F32)
            pair.append(kept[j] + (piece + pltpu.roll(piece, LANES // 2, 1)))
        left[i] = jnp.where(side == 1, pair[1], pair[0])
        message[i] = halves(jnp.where(side == 1, pair[0], pair[1]))
    for s in range(ends):
        message[slots // 2 + s] = went[slots + s]
        message[slots // 2 + ends + s] = came[slots + s]


def merge(z, bit, kept, came, went):
    slots = kept.shape[0]
    ends = came.shape[0] - slots
    return pl.pallas_call(
        functools.partial(merge_kernel, z, bit),
        in_specs=[VMEM_SPEC] * 3,
        out_specs=[VMEM_SPEC] * 2,
        out_shape=[
            jax.ShapeDtypeStruct((slots // 2 + 2 * ends, z.spec_rows, LANES), BF),
            jax.ShapeDtypeStruct((slots // 2, z.spec_rows, LANES), F32),
        ],
        compiler_params=params(),
        name="merge",
    )(kept, came, went)


def cross_kernel(z, offsets, pairs, stacks, *refs):
    pieces, out = refs[:-1], refs[-1]
    here = position("sta")
    mine = pieces[0][...]
    bins = z.bins
    sides = []
    for i in range(z.stations):
        re, im = mine[2 * i : 2 * i + 1], mine[2 * i + 1 : 2 * i + 2]
        sides.append((jnp.concatenate([re, im], axis=0), jnp.concatenate([im, -re], axis=0)))
    for k, (offset, piece) in enumerate(zip(offsets, pieces)):
        on = jnp.concatenate([pairs[k]] * (bins // LANES), axis=1)
        for j in range(z.stations):
            re = jnp.broadcast_to(piece[2 * j : 2 * j + 1, :], (2, bins)) * on
            im = jnp.broadcast_to(piece[2 * j + 1 : 2 * j + 2, :], (2, bins)) * on
            column = (here ^ offset) * z.stations + j
            for i, (p, q) in enumerate(sides):
                out[i, column] = stacks[i, column] + (re * p + im * q)


def cross(z, offsets, pairs, stacks, pieces):
    return pl.pallas_call(
        functools.partial(cross_kernel, z, offsets),
        in_specs=[VMEM_SPEC] * (2 + len(pieces)),
        out_specs=VMEM_SPEC,
        out_shape=jax.ShapeDtypeStruct(stacks.shape, F32),
        compiler_params=params(),
        name="cross",
    )(pairs, stacks, *pieces)


def shards(traces, station_flags, tile_mask, band_block, stacks):
    tm_count, sta_count = lax.axis_size("tm"), lax.axis_size("sta")
    stations, length = traces.shape
    z = Sizes(stations, length, tm_count, stacks.shape[-1])
    assert sta_count & (sta_count - 1) == 0
    offsets = [0]
    bits = [1 << k for k in reversed(range(sta_count.bit_length() - 1))]
    for bit in bits:
        offsets += [offset ^ bit for offset in offsets]
    if tm_count in (4, 8, 16):
        message, home = split_transform(z, station_flags, traces)
        for k in range(tm_count.bit_length() - 1):
            swap = [(i, i ^ (1 << k)) for i in range(tm_count)]
            came, went = lax.ppermute(message, "tm", swap), message
            if k == 0:
                kept = home()
            if 2 << k < tm_count:
                message, kept = merge(z, k + 1, kept, came, went)
        *made, pairs = tables(z, offsets, z.lift, 1, band_block, station_flags, tile_mask)
        white = gathered(z, kept, came, went, made)
    else:
        sent = transform(z, station_flags, traces)
        got = lax.all_to_all(sent, "tm", split_axis=0, concat_axis=0, tiled=True)
        *made, pairs = tables(
            z, offsets, z.half, tm_count, band_block, station_flags, tile_mask
        )
        white = spectrum(z, got, made)
    pieces = [white]
    for bit in bits:
        swap = [(i, i ^ bit) for i in range(sta_count)]
        pieces += [lax.ppermute(piece, "sta", swap) for piece in pieces]
    return cross(z, offsets, pairs, stacks, pieces)


def solution(mesh):
    return jax.shard_map(
        shards,
        mesh=mesh,
        in_specs=(P("sta", "tm"), P("sta"), P(), P(), P("sta", None, None, "tm")),
        out_specs=P("sta", None, None, "tm"),
        check_vma=False,
    )
```

```python
import functools
import math

import jax
import jax.numpy as jnp
import numpy as np
from jax import lax
from jax.experimental import pallas as pl
from jax.experimental.pallas import tpu as pltpu
from jax.sharding import PartitionSpec as P

HALF_WIN = 512
SMOOTH = 32
EPS_MEAN = 1e-06
EPS_POWER = 1e-06
LANES = 128
SPAN = 2 * HALF_WIN
TILES = SPAN // LANES
HALF_TILES = HALF_WIN // LANES
PAD = 16
BAND_TOP = 137
WIDTH = 2 * LANES
CHUNKS = SPAN // WIDTH
position = lax.axis_index
VMEM_LIMIT = 16 * 1024 * 1024
BF = jnp.bfloat16
F32 = jnp.float32


def up_to(value, step):
    return -(-value // step) * step


def sincos(turns):
    quarter = jnp.round(turns * 4.0)
    rest = turns - quarter * 0.25
    y = rest * (2.0 * math.pi)
    y2 = y * y
    s = y + y * y2 * (-1.0 / 6 + y2 * (1.0 / 120 + y2 * (-1.0 / 5040 + y2 * (1.0 / 362880))))
    c = 1.0 + y2 * (-0.5 + y2 * (1.0 / 24 + y2 * (-1.0 / 720 + y2 * (1.0 / 40320))))
    q = quarter - 4.0 * jnp.floor(quarter * 0.25)
    swap = (q == 1.0) | (q == 3.0)
    sine = jnp.where(swap, c, s)
    cosine = jnp.where(swap, s, c)
    sine = jnp.where(q >= 2.0, -sine, sine)
    cosine = jnp.where((q == 1.0) | (q == 2.0), -cosine, cosine)
    return sine, cosine


def turns_of(product, period):
    whole = jnp.floor(product * (1.0 / period))
    return (product - whole * period) * (1.0 / period)


def split2(value):
    high = value.astype(BF)
    return high, (value - high.astype(F32)).astype(BF)


def iota(shape, axis):
    return lax.broadcasted_iota(jnp.int32, shape, axis)


def iota_f(shape, axis):
    return iota(shape, axis).astype(F32)


def window_tables():
    row, lane = iota((LANES, LANES), 0), iota((LANES, LANES), 1)
    upto = (row <= lane).astype(F32).astype(BF)
    onward = (row >= lane).astype(F32).astype(BF)
    return upto, onward, jnp.ones((LANES, LANES), BF)


def np_split(value):
    high = value.astype(jnp.bfloat16).astype(np.float64)
    return high, (value - high).astype(jnp.bfloat16).astype(np.float64)


class Sizes:
    def __init__(self, stations, length, tm_count, bins):
        self.stations, self.length, self.tm, self.bins = stations, length, tm_count, bins
        self.rows = length // SPAN
        self.half = self.rows // 2 + 1
        self.pad = up_to(self.rows, PAD)
        self.full = self.rows // PAD * PAD
        self.tail = self.rows - self.full
        self.depth = 3 * self.full + PAD
        self.block = min(tm_count, 16)
        self.blocks = tm_count // self.block
        self.folds = (BAND_TOP + bins - 1) // self.rows + 1
        self.lift = up_to(self.half, 2)
        self.spec_rows = up_to(2 * self.lift, 8)
        self.edge_rows = 2 * stations * TILES
        self.sent_rows = self.spec_rows + self.edge_rows
        assert length % SPAN == 0 and tm_count % self.block == 0
        assert stations == 2 and self.folds <= PAD
        assert self.rows >= 2 and 0 < 3 * self.tail <= 8 and self.depth <= LANES

    def parity_tables(self):
        residue = np.arange(self.tm).reshape(-1, 2).T[:, None, :]
        order = (residue + self.tm * np.arange(self.lift)[None, :, None]).reshape(2, -1)
        return self.first_of(order), self.turn_of(order)

    def row_order(self):
        j2 = np.arange(self.tm)[:, None] + self.tm * np.arange(self.half)[None, :]
        return j2.reshape(self.blocks, self.block, self.half).transpose(0, 2, 1).reshape(self.blocks, -1)

    def first_table(self):
        return self.first_of(self.row_order())

    def turn_table(self):
        return self.turn_of(self.row_order())

    def first_of(self, order):
        period = self.tm * self.rows
        angle = 2.0 * np.pi / period * (order[:, :, None] * np.arange(self.rows) % period)
        parts = np.concatenate([np.cos(angle), -np.sin(angle)], axis=1)
        full, rest = parts[..., : self.full], parts[..., self.full :]
        table = np.concatenate([full, full, full, rest, rest, rest], axis=2)
        return np.pad(table, ((0, 0), (0, 0), (0, LANES - table.shape[2]))).astype(np.float32)

    def low_lanes(self, lane):
        at = 3 * self.full
        third = (lane >= 2 * self.full) & (lane < at)
        return third | ((lane >= at + 2 * self.tail) & (lane < at + 3 * self.tail))

    def turn_of(self, order):
        order = order.reshape(order.shape[0], 1, -1, 1)
        time = np.arange(SPAN).reshape(CHUNKS, 1, WIDTH)
        angle = 2.0 * np.pi / (self.tm * self.length) * (order * time)
        return np.stack([np.cos(angle), -np.sin(angle)], axis=2).astype(np.float32)


def unpack(z, x, xs, edges):
    rows, top = z.rows, 8
    for a in range(rows):
        xs[:, top + a, :] = x[:, a * SPAN : (a + 1) * SPAN].astype(F32)
    for s in range(z.stations):
        for side, a in ((0, 0), (1, rows - 1)):
            for c in range(TILES):
                at = (side * z.stations + s) * TILES + c
                edges[at : at + 1, :] = xs[s, top + a : top + a + 1, c * LANES : (c + 1) * LANES]


def window(z, s, xs, sums):
    rows, pad, top = z.rows, z.pad, 8
    short = up_to(rows, 8)
    kernel = jnp.concatenate(window_tables()[:2], axis=1)
    group = 4
    for c0 in range(0, TILES, group):
        parts = [
            jnp.abs(xs[s, top : top + pad, c * LANES : (c + 1) * LANES])
            for c in range(c0, c0 + group)
        ]
        part = jnp.concatenate([part.astype(BF) for part in parts], axis=0)
        got = jnp.dot(part, kernel, preferred_element_type=F32)
        for k in range(group):
            value = got[k * pad : k * pad + short]
            upto, onward = value[:, :LANES], value[:, LANES:]
            sums[s, c0 + k, top : top + short, 0 : 2 * LANES] = value
            sums[s, c0 + k, top : top + short, 2 * LANES :] = upto + (onward - parts[k][:short])
    blank = jnp.zeros((1, HALF_WIN), F32)
    xs[s, top : top + 1, 0:HALF_WIN] = blank
    xs[s, top + rows - 1 : top + rows, HALF_WIN:SPAN] = blank


def level(z, s, tiles, xs, sums, stack):
    rows, top = z.rows, 8
    short = up_to(rows, 8)

    def tile(kind, c):
        turn, cc = divmod(c, TILES)
        lines = slice(top + turn, top + turn + short)
        return sums[s, cc, lines, kind * LANES : (kind + 1) * LANES]

    first = tiles[0] + 1 - HALF_TILES
    single = [tile(2, c) for c in range(first, tiles[-1] + HALF_TILES)]
    twos = [single[c] + single[c + 1] for c in range(len(single) - 1)]
    for k, c in enumerate(tiles):
        inner = (twos[k] + twos[k + 2]) + (twos[k + 4] + single[k + 6])
        total = inner + (tile(1, c - HALF_TILES) + tile(0, c + HALF_TILES))
        value = xs[s, top : top + short, c * LANES : (c + 1) * LANES]
        value = value / (total * (1.0 / (2 * HALF_WIN + 1)) + EPS_MEAN)
        high, low = split2(value[: z.full])
        lanes = slice(c * LANES, (c + 1) * LANES)
        for k2, part in enumerate((high, low, high)):
            stack[s, k2 * z.full : (k2 + 1) * z.full, lanes] = part
        rest = value[z.full :]
        high = rest.astype(BF).astype(F32)
        rest = high + pltpu.roll(rest - high, z.tail, 0) + pltpu.roll(high, 2 * z.tail, 0)
        rest = jnp.concatenate([rest, jnp.zeros((PAD - rest.shape[0], LANES), F32)], axis=0)
        stack[s, 3 * z.full :, lanes] = rest.astype(BF)


def fold_weights(weight):
    lane = iota((PAD, SPAN), 1)
    for kind in range(2):
        turns = jnp.bitwise_and((iota((PAD, SPAN), 0) + kind) * lane, SPAN - 1).astype(F32)
        sine, cosine = sincos(turns * (1.0 / SPAN))
        for h, (s, c) in enumerate(zip(split2(sine), split2(cosine))):
            table = ((c, s), (-s, c)) if kind == 0 else ((c, -s), (-s, -c))
            for part in range(2):
                at = h * 4 * PAD + kind * 2 * PAD + part * PAD
                for side in range(2):
                    for g in range(CHUNKS):
                        to = (2 * g + side) * WIDTH
                        weight[at : at + PAD, to : to + WIDTH] = table[part][side][
                            :, g * WIDTH : (g + 1) * WIDTH
                        ]


def transform_kernel(
    z, flags, x, first, turn, out,
    flags_s, x_v, first_v, turn_v, table, xs, sums, stack, edges, weight, acc, both, spec, sems,
):
    half, block, tm = z.half, z.block, z.tm
    height = half * block
    index = pl.program_id(0)
    top, rows, pad = 8, z.rows, z.pad
    get_first = pltpu.make_async_copy(first.at[index], first_v, sems.at[2])
    get_turn = [
        pltpu.make_async_copy(turn.at[index, g], turn_v.at[g], sems.at[3 + g]) for g in range(CHUNKS)
    ]

    def prologue():
        copies = [
            pltpu.make_async_copy(x, x_v, sems.at[0]),
            pltpu.make_async_copy(flags, flags_s, sems.at[1]),
        ]
        for copy in copies + [get_first] + get_turn:
            copy.start()
        full = rows // 8 * 8
        for s in range(z.stations):
            xs[s, top + full : top + pad, :] = jnp.zeros((pad - full, SPAN), F32)
            for c in range(TILES):
                sums[s, c, 0:top, :] = jnp.zeros((top, 3 * LANES), F32)
                sums[s, c, top + up_to(rows, 8) :, :] = jnp.zeros((8, 3 * LANES), F32)
        spec[:, z.spec_rows - 8 : z.spec_rows, :] = jnp.zeros((tm, 8, LANES), F32)
        fold_weights(weight)
        for copy in copies:
            copy.wait()
        unpack(z, x_v, xs, edges)
        for s in range(z.stations):
            window(z, s, xs, sums)
            if s == 0 or z.blocks > 1:
                level(z, s, range(TILES), xs, sums, stack)

    if z.blocks == 1:
        prologue()
    else:
        pl.when(index == 0)(prologue)

        @pl.when(index > 0)
        def _():
            for copy in [get_first] + get_turn:
                copy.start()

    for copy in [get_first] + get_turn:
        copy.wait()
    residue = index * block + iota((block, LANES), 0)
    sine, cosine = sincos(turns_of((position("tm") * residue).astype(F32), tm))
    f_re = first_v[:height].reshape(half, block, LANES)
    f_im = first_v[height:].reshape(half, block, LANES)
    low = z.low_lanes(iota((height, LANES), 1))
    for k, value in enumerate(
        (f_re * cosine[None] + f_im * sine[None], f_im * cosine[None] - f_re * sine[None])
    ):
        value = value.reshape(height, LANES)
        high = value.astype(BF).astype(F32)
        table[k * height : (k + 1) * height, :] = jnp.where(low, value - high, high).astype(BF)

    def first_stage(s, g):
        return jnp.dot(
            table[:, : z.depth],
            stack[s, :, g * WIDTH : (g + 1) * WIDTH],
            preferred_element_type=F32,
        )

    def second_stage(s, g, parts):
        w = weight[:, 2 * g * WIDTH : 2 * (g + 1) * WIDTH]
        got = lax.dot_general(parts, w, (((1,), (1,)), ((), ())), preferred_element_type=F32)
        value = got[:height] + got[height:]
        acc[s] = value if g == 0 else acc[s] + value

    def settle(s):
        value = acc[s] + pltpu.roll(acc[s], LANES // 2, 1)
        return value * flags_s[s].astype(F32)

    steps = [(s, g) for s in range(z.stations) for g in range(CHUNKS)]
    coming = first_stage(*steps[0])
    waiting = None
    for k, (s, g) in enumerate(steps):
        f_re, f_im = coming[:height], coming[height:]
        t_re, t_im = turn_v[g, 0], turn_v[g, 1]
        re_h, re_l = split2(f_re * t_re - f_im * t_im)
        im_h, im_l = split2(f_re * t_im + f_im * t_re)
        parts = jnp.concatenate(
            [jnp.concatenate([re_h, im_h], axis=1), jnp.concatenate([re_l, im_l], axis=1)], axis=0
        )
        if s == 0 and z.blocks == 1:
            level(z, 1, range(2 * g, 2 * g + 2), xs, sums, stack)
        if k + 1 < len(steps):
            coming = first_stage(*steps[k + 1])
        if waiting is not None:
            second_stage(*steps[k - 1], waiting)
        waiting = parts
    second_stage(*steps[-1], waiting)
    zero, one = settle(0), settle(1)
    lane = iota((height, LANES), 1)
    early = jnp.bitwise_and(lane, LANES // 2 - 1) < LANES // 4
    direct = jnp.where(early, zero, pltpu.roll(one, LANES // 4, 1))
    mirror = jnp.where(early, pltpu.roll(zero, LANES // 4, 1), one)
    for kind, value in enumerate((direct, mirror)):
        high = value.astype(BF).astype(F32)
        both[kind] = jnp.where(lane < LANES // 2, high, value - high)
    for k in range(block):
        here = index * block + k
        there = jnp.where(here == 0, 0, tm - here) if z.blocks > 1 else (tm - k) % tm
        here = here if z.blocks > 1 else k
        lines = pl.ds(k, half, stride=block)
        spec[here, 0:half, :] = both[0, lines, :]
        spec[there, half : 2 * half, :] = both[1, lines, :]

    def finish():
        ends = edges[...].astype(BF)

        def one_row(k, carry):
            out[k, 0 : z.spec_rows, :] = spec[k].astype(BF)
            out[k, z.spec_rows : z.sent_rows, :] = ends
            return carry

        if z.blocks == 1:
            for k in range(tm):
                one_row(k, 0)
        else:
            lax.fori_loop(0, tm, one_row, 0)

    if z.blocks == 1:
        finish()
    else:
        pl.when(index == z.blocks - 1)(finish)


SMEM_SPEC = pl.BlockSpec(memory_space=pltpu.SMEM)
VMEM_SPEC = pl.BlockSpec(memory_space=pltpu.VMEM)
HBM_SPEC = pl.BlockSpec(memory_space=pltpu.HBM)


def params():
    return pltpu.CompilerParams(vmem_limit_bytes=VMEM_LIMIT)


def transform(z, flags, x):
    height = z.half * z.block
    first, turn = z.first_table(), z.turn_table()
    return pl.pallas_call(
        functools.partial(transform_kernel, z),
        grid=(z.blocks,),
        in_specs=[HBM_SPEC] * 4,
        out_specs=VMEM_SPEC,
        out_shape=jax.ShapeDtypeStruct((z.tm, z.sent_rows, LANES), BF),
        scratch_shapes=[
            pltpu.SMEM((z.stations,), jnp.int32),
            pltpu.VMEM(x.shape, BF),
            pltpu.VMEM(first.shape[1:], F32),
            pltpu.VMEM(turn.shape[1:], F32),
            pltpu.VMEM(first.shape[1:], BF),
            pltpu.VMEM((z.stations, 8 + z.pad, SPAN), F32),
            pltpu.VMEM((z.stations, TILES, 16 + up_to(z.rows, 8), 3 * LANES), F32),
            pltpu.VMEM((z.stations, z.depth, SPAN), BF),
            pltpu.VMEM((z.edge_rows, LANES), F32),
            pltpu.VMEM((LANES, 2 * SPAN), BF),
            pltpu.VMEM((z.stations, height, LANES), F32),
            pltpu.VMEM((2, height, LANES), F32),
            pltpu.VMEM((z.tm, z.spec_rows, LANES), F32),
            pltpu.SemaphoreType.DMA((3 + CHUNKS,)),
        ],
        name="transform",
    )(flags, x, jnp.asarray(first), jnp.asarray(turn))


def table_kernel(
    z, offsets, split, band, flags, mask, choose, keep, steps, turns, near, phase, switch, pairs,
    band_s, flags_s, mask_s, sems,
):
    rows, tm, bins, half = z.rows, z.tm, z.bins, z.half
    copies = [
        pltpu.make_async_copy(band, band_s, sems.at[0]),
        pltpu.make_async_copy(flags, flags_s, sems.at[1]),
        pltpu.make_async_copy(mask, mask_s, sems.at[2]),
    ]
    for copy in copies:
        copy.start()
    for copy in copies:
        copy.wait()
    here = position("sta")
    for k, offset in enumerate(offsets):
        pairs[k] = jnp.full((2, LANES), mask_s[here, here ^ offset].astype(F32))
    base, residue = band_s[0, 0], position("tm")
    for s in range(z.stations):
        switch[s] = jnp.full((TILES, LANES), flags_s[s].astype(F32))
    spot = iota_f((1, bins), 1) + base.astype(F32)
    fold = jnp.floor((spot + 0.5) * (1.0 / rows))
    rest = spot - fold * rows
    row = iota_f((z.spec_rows, bins), 0)
    last = (rows - 1 + split + (residue == 0).astype(jnp.int32)).astype(F32)
    mirror = jnp.where((row >= split) & (last - row >= half), last - row, -1.0)
    one = (jnp.where(row < half, row, mirror) == rest).astype(F32).astype(BF)
    for p in range(choose.shape[0]):
        choose[p] = one
    keep[...] = (iota_f((PAD, bins), 0) == fold).astype(F32)
    freq = (residue + tm * (base + iota((1, bins), 1))).astype(F32)
    step = iota_f((TILES, bins), 0) - HALF_TILES
    sine, cosine = sincos(turns_of(step * freq, tm * (z.length // LANES)))
    table = jnp.concatenate(
        [jnp.concatenate([cosine, -sine], axis=1), jnp.concatenate([sine, cosine], axis=1)], axis=0
    )
    high, low = split2(table)
    for k, part in enumerate((high, high, low, low)):
        steps[k * 2 * TILES : (k + 1) * 2 * TILES, :] = part
    sine, cosine = sincos(turns_of(iota_f((LANES, bins), 0) * freq, tm * z.length))
    turns[0] = cosine
    turns[1] = sine
    gap = jnp.abs(iota((bins, bins), 0) - iota((bins, bins), 1))
    near[...] = (gap <= SMOOTH).astype(F32).astype(BF)
    p_sin, p_cos = sincos(turns_of((residue * iota((tm, LANES), 0)).astype(F32), tm))
    phase[0] = p_cos
    phase[1] = -p_sin


def tables(z, offsets, split, copies, band, flags, mask):
    return pl.pallas_call(
        functools.partial(table_kernel, z, offsets, split),
        in_specs=[HBM_SPEC] * 3,
        out_specs=[VMEM_SPEC] * 8,
        scratch_shapes=[
            pltpu.SMEM((1, 1), jnp.int32),
            pltpu.SMEM((z.stations,), jnp.int32),
            pltpu.SMEM(mask.shape, jnp.int32),
            pltpu.SemaphoreType.DMA((3,)),
        ],
        out_shape=[
            jax.ShapeDtypeStruct((copies, z.spec_rows, z.bins), BF),
            jax.ShapeDtypeStruct((PAD, z.bins), F32),
            jax.ShapeDtypeStruct((8 * TILES, 2 * z.bins), BF),
            jax.ShapeDtypeStruct((2, LANES, z.bins), F32),
            jax.ShapeDtypeStruct((z.bins, z.bins), BF),
            jax.ShapeDtypeStruct((2, z.tm, LANES), F32),
            jax.ShapeDtypeStruct((z.stations, TILES, LANES), F32),
            jax.ShapeDtypeStruct((len(offsets), 2, LANES), F32),
        ],
        compiler_params=params(),
        cost_estimate=pl.CostEstimate(flops=4000000, bytes_accessed=2000000, transcendentals=0),
        name="tables",
    )(band.reshape(1, 1), flags, mask)


def sublane_sums(value, row):
    total = value
    for shift in (1, 2, 4):
        total = total + jnp.where(row >= shift, pltpu.roll(total, shift, 0), 0.0)
    return total - value, total


def spectrum_kernel(z, got, choose, keep, steps, turns, near, phase, switch, out):
    tm, bins, at = z.tm, z.bins, z.spec_rows
    parts = got[:, 0:at, :].astype(F32).reshape(tm * at, LANES).astype(BF)
    weights = choose[...].astype(F32).reshape(tm * at, bins).astype(BF)
    placed = lax.dot_general(parts, weights, (((0,), (0,)), ((), ())), preferred_element_type=F32)
    side_rows = z.stations * TILES
    ends = [
        got[:, at + k * side_rows : at + (k + 1) * side_rows, :].astype(F32).reshape(-1, LANES)
        for k in range(2)
    ]
    whiten(z, placed, ends, keep, steps, turns, near, phase, switch, out)


def gathered_kernel(
    z, kept, came, went, choose, keep, steps, turns, near, phase, switch, out, ends
):
    tm = z.tm
    piece = came[0 : z.spec_rows, :].astype(F32)
    total = kept[0] + (piece + pltpu.roll(piece, LANES // 2, 1))
    placed = lax.dot_general(
        halves(total), choose[0], (((0,), (0,)), ((), ())), preferred_element_type=F32
    )
    here = position("tm")
    for s in range(tm):
        source, slot = (went, s) if s < tm // 2 else (came, s - tm // 2)
        at = z.spec_rows + slot * z.edge_rows
        ends[here ^ s] = source[at : at + z.edge_rows, :].astype(F32)
    side_rows = z.stations * TILES
    sides = [ends[:, k * side_rows : (k + 1) * side_rows, :].reshape(-1, LANES) for k in range(2)]
    whiten(z, placed, sides, keep, steps, turns, near, phase, switch, out)


def halves(value):
    high = value.astype(BF).astype(F32)
    return jnp.where(iota(value.shape, 1) < LANES // 2, high, value - high).astype(BF)


def whiten(z, placed, ends, keep, steps, turns, near, phase, switch, out):
    tm, bins = z.tm, z.bins
    mask = keep[...]
    folded = [
        jnp.sum(placed[k * PAD : (k + 1) * PAD] * mask, axis=0, keepdims=True)
        for k in range(4 * z.stations)
    ]
    spec = [folded[k] + folded[k + 2 * z.stations] for k in range(2 * z.stations)]
    upto, onward, ones = window_tables()
    row = iota((TILES, LANES), 0)
    late = row >= HALF_TILES
    sides = []
    for value, table in zip(ends, (upto, onward)):
        sums = jnp.dot(
            jnp.abs(value).astype(BF),
            jnp.concatenate([table, ones], axis=1),
            preferred_element_type=F32,
        )
        sides.append((value, sums))
    mixed = []
    for s in range(z.stations):
        real = jnp.zeros((TILES, LANES), F32)
        imag = jnp.zeros((TILES, LANES), F32)
        flag = switch[s]
        for p in range(tm):
            begin = (p * z.stations + s) * TILES
            before = ((p - 1) % tm * z.stations + s) * TILES
            value_r, sums_r = (v[begin : begin + TILES] for v in sides[0])
            value_l, sums_l = (v[before : before + TILES] for v in sides[1])
            earlier, _ = sublane_sums(sums_r[:, LANES:], row)
            right = sums_r[:, :LANES] + earlier
            tail = sums_l[:, LANES:]
            for shift in (1, 2, 4):
                tail = tail + jnp.where(row < TILES - shift, pltpu.roll(tail, TILES - shift, 0), 0.0)
            left = sums_l[:, :LANES] + jnp.where(
                row < TILES - 1, pltpu.roll(tail, TILES - 1, 0), 0.0
            )
            total = left + right if p else jnp.where(late, right, left)
            sample = pltpu.roll(jnp.where(late, value_l, value_r), HALF_TILES, 0)
            value = flag * sample / (total * (1.0 / (2 * HALF_WIN + 1)) + EPS_MEAN)
            real = real + value * phase[0, p : p + 1, :]
            imag = imag + value * phase[1, p : p + 1, :]
        mixed.append(jnp.concatenate([real, imag], axis=0))
    high, low = split2(jnp.concatenate(mixed, axis=1))
    spread = lax.dot_general(
        jnp.concatenate([high, low, high, low], axis=0),
        steps[...],
        (((0,), (0,)), ((), ())),
        preferred_element_type=F32,
    )
    cosine, sine = turns[0], turns[1]
    pieces = []
    for s in range(z.stations):
        g_re = spread[s * LANES : (s + 1) * LANES, :bins]
        g_im = spread[s * LANES : (s + 1) * LANES, bins:]
        spec[2 * s] += jnp.sum(g_re * cosine + g_im * sine, axis=0, keepdims=True)
        spec[2 * s + 1] += jnp.sum(g_im * cosine - g_re * sine, axis=0, keepdims=True)
        power = spec[2 * s] * spec[2 * s] + spec[2 * s + 1] * spec[2 * s + 1]
        for _ in range(3):
            part = power.astype(BF).astype(F32)
            pieces.append(part)
            power = power - part
    pieces.append(jnp.zeros((8 - len(pieces), bins), F32))
    smooth = jnp.dot(
        jnp.concatenate(pieces, axis=0).astype(BF), near[...], preferred_element_type=F32
    )
    for s in range(z.stations):
        mean = smooth[3 * s : 3 * s + 1] + smooth[3 * s + 1 : 3 * s + 2] + smooth[3 * s + 2 : 3 * s + 3]
        scale = 1.0 / jnp.sqrt(mean * (1.0 / (2 * SMOOTH + 1)) + EPS_POWER)
        out[2 * s : 2 * s + 1, :] = spec[2 * s] * scale
        out[2 * s + 1 : 2 * s + 2, :] = spec[2 * s + 1] * scale


def spectrum(z, got, made):
    return pl.pallas_call(
        functools.partial(spectrum_kernel, z),
        in_specs=[VMEM_SPEC] * 8,
        out_specs=VMEM_SPEC,
        out_shape=jax.ShapeDtypeStruct((2 * z.stations, z.bins), F32),
        compiler_params=params(),
        name="spectrum",
    )(got, *made)


def gathered(z, kept, came, went, made):
    return pl.pallas_call(
        functools.partial(gathered_kernel, z),
        in_specs=[VMEM_SPEC] * 10,
        out_specs=VMEM_SPEC,
        out_shape=jax.ShapeDtypeStruct((2 * z.stations, z.bins), F32),
        scratch_shapes=[pltpu.VMEM((z.tm, z.edge_rows, LANES), F32)],
        compiler_params=params(),
        name="spectrum",
    )(kept, came, went, *made)


def half_transform(z, parity, table, turn, stack, weight, flags, acc, both, spec, before):
    count, lift = z.tm // 2, z.lift
    height = lift * count

    def first_stage(s, g):
        return jnp.dot(
            table[:, : z.depth],
            stack[s, :, g * WIDTH : (g + 1) * WIDTH],
            preferred_element_type=F32,
        )

    def second_stage(s, g, parts):
        w = weight[:, 2 * g * WIDTH : 2 * (g + 1) * WIDTH]
        got = lax.dot_general(parts, w, (((1,), (1,)), ((), ())), preferred_element_type=F32)
        value = got[:height] + got[height:]
        acc[s] = value if g == 0 else acc[s] + value

    def settle(s):
        return (acc[s] + pltpu.roll(acc[s], LANES // 2, 1)) * flags[s, 0:1, :]

    steps = [(s, g) for s in range(z.stations) for g in range(CHUNKS)]
    coming = first_stage(*steps[0])
    waiting = None
    for k, (s, g) in enumerate(steps):
        f_re, f_im = coming[:height], coming[height:]
        t_re, t_im = turn[g, 0], turn[g, 1]
        re_h, re_l = split2(f_re * t_re - f_im * t_im)
        im_h, im_l = split2(f_re * t_im + f_im * t_re)
        parts = jnp.concatenate(
            [jnp.concatenate([re_h, im_h], axis=1), jnp.concatenate([re_l, im_l], axis=1)], axis=0
        )
        if before is not None and s == 0:
            before(g)
        if k + 1 < len(steps):
            coming = first_stage(*steps[k + 1])
        if waiting is not None:
            second_stage(*steps[k - 1], waiting)
        waiting = parts
    second_stage(*steps[-1], waiting)
    zero, one = settle(0), settle(1)
    lane = iota((height, LANES), 1)
    early = jnp.bitwise_and(lane, LANES // 2 - 1) < LANES // 4
    both[0] = jnp.where(early, zero, pltpu.roll(one, LANES // 4, 1))
    both[1] = jnp.where(early, pltpu.roll(zero, LANES // 4, 1), one)
    for j in range(count):
        lines = pl.ds(j, lift, stride=count)
        spec[j, 0:lift, :] = both[0, lines, :]
        spec[lax.rem(2 * count - parity - j, count), lift : 2 * lift, :] = both[1, lines, :]


def stretch_table(z, parity, first, table):
    count, height = z.tm // 2, z.lift * (z.tm // 2)
    low = z.low_lanes(iota((height, LANES), 1))
    residue = 2 * iota((count, LANES), 0) + parity
    sine, cosine = sincos(turns_of((position("tm") * residue).astype(F32), z.tm))
    f_re = first[:height].reshape(z.lift, count, LANES)
    f_im = first[height:].reshape(z.lift, count, LANES)
    for k, value in enumerate(
        (f_re * cosine[None] + f_im * sine[None], f_im * cosine[None] - f_re * sine[None])
    ):
        value = value.reshape(height, LANES)
        high = value.astype(BF).astype(F32)
        table[k * height : (k + 1) * height, :] = jnp.where(low, value - high, high).astype(BF)


def away_kernel(
    z, flags, x, first, turn, message, stack, weight, home_first, home_turn, switch,
    flags_s, x_v, first_v, turn_v, table, xs, sums, edges, acc, both, spec, sems,
):
    rows, pad, top = z.rows, z.pad, 8
    count = z.tm // 2
    here = position("tm")
    home = jnp.bitwise_and(here, 1)
    away = 1 - home
    copies = [
        pltpu.make_async_copy(x, x_v, sems.at[0]),
        pltpu.make_async_copy(flags, flags_s, sems.at[1]),
        pltpu.make_async_copy(first.at[away], first_v, sems.at[2]),
        pltpu.make_async_copy(turn.at[away], turn_v, sems.at[3]),
        pltpu.make_async_copy(turn.at[home], home_turn, sems.at[4]),
        pltpu.make_async_copy(first.at[home], home_first, sems.at[5]),
    ]
    for copy in copies:
        copy.start()
    full = rows // 8 * 8
    for s in range(z.stations):
        xs[s, top + full : top + pad, :] = jnp.zeros((pad - full, SPAN), F32)
        for c in range(TILES):
            sums[s, c, 0:top, :] = jnp.zeros((top, 3 * LANES), F32)
            sums[s, c, top + up_to(rows, 8) :, :] = jnp.zeros((8, 3 * LANES), F32)
    spec[:, z.spec_rows - 8 : z.spec_rows, :] = jnp.zeros((count, 8, LANES), F32)
    fold_weights(weight)
    copies[0].wait()
    copies[1].wait()
    unpack(z, x_v, xs, edges)
    for s in range(z.stations):
        window(z, s, xs, sums)
        switch[s] = jnp.full((TILES, LANES), flags_s[s].astype(F32))
    level(z, 0, range(TILES), xs, sums, stack)
    copies[2].wait()
    copies[3].wait()
    stretch_table(z, away, first_v, table)
    half_transform(
        z, away, table, turn_v, stack, weight, switch, acc, both, spec,
        lambda g: level(z, 1, range(2 * g, 2 * g + 2), xs, sums, stack),
    )
    copies[4].wait()
    copies[5].wait()
    for j in range(count):
        message[j * z.spec_rows : (j + 1) * z.spec_rows, :] = halves(spec[j])
    message[count * z.spec_rows :, :] = edges[...].astype(BF)


def home_kernel(z, stack, weight, first, turn, switch, kept, table, acc, both):
    kept[:, z.spec_rows - 8 : z.spec_rows, :] = jnp.zeros((z.tm // 2, 8, LANES), F32)
    parity = jnp.bitwise_and(position("tm"), 1)
    stretch_table(z, parity, first, table)
    half_transform(z, parity, table, turn, stack, weight, switch, acc, both, kept, None)


def split_transform(z, flags, x):
    count, height = z.tm // 2, z.lift * (z.tm // 2)
    first, turn = z.parity_tables()
    state = [
        jax.ShapeDtypeStruct((z.stations, z.depth, SPAN), BF),
        jax.ShapeDtypeStruct((LANES, 2 * SPAN), BF),
        jax.ShapeDtypeStruct(first.shape[1:], F32),
        jax.ShapeDtypeStruct(turn.shape[1:], F32),
        jax.ShapeDtypeStruct((z.stations, TILES, LANES), F32),
    ]
    inputs = [flags, x, jnp.asarray(first), jnp.asarray(turn)]
    work = [
        pltpu.VMEM((z.stations, height, LANES), F32),
        pltpu.VMEM((2, height, LANES), F32),
    ]
    message, *state = pl.pallas_call(
        functools.partial(away_kernel, z),
        in_specs=[HBM_SPEC] * 4,
        out_specs=[VMEM_SPEC] * 6,
        out_shape=[jax.ShapeDtypeStruct((count * z.spec_rows + z.edge_rows, LANES), BF)] + state,
        scratch_shapes=[
            pltpu.SMEM((z.stations,), jnp.int32),
            pltpu.VMEM(x.shape, BF),
            pltpu.VMEM(first.shape[1:], F32),
            pltpu.VMEM(turn.shape[1:], F32),
            pltpu.VMEM(first.shape[1:], BF),
            pltpu.VMEM((z.stations, 8 + z.pad, SPAN), F32),
            pltpu.VMEM((z.stations, TILES, 16 + up_to(z.rows, 8), 3 * LANES), F32),
            pltpu.VMEM((z.edge_rows, LANES), F32),
            *work,
            pltpu.VMEM((count, z.spec_rows, LANES), F32),
            pltpu.SemaphoreType.DMA((6,)),
        ],
        compiler_params=params(),
        name="away",
    )(*(in_hbm(value) for value in inputs))

    def home():
        return pl.pallas_call(
            functools.partial(home_kernel, z),
            in_specs=[VMEM_SPEC] * 5,
            out_specs=VMEM_SPEC,
            out_shape=jax.ShapeDtypeStruct((count, z.spec_rows, LANES), F32),
            scratch_shapes=[pltpu.VMEM(first.shape[1:], BF), *work],
            compiler_params=params(),
            cost_estimate=pl.CostEstimate(flops=10**9, bytes_accessed=10**6, transcendentals=0),
            name="home",
        )(*state)

    return message, home


def in_hbm(value):
    return pltpu.with_memory_space_constraint(value, pltpu.HBM)


def merge_kernel(z, bit, kept, came, went, message, left):
    slots = kept.shape[0]
    at, to = slots * z.spec_rows, slots // 2 * z.spec_rows
    ends = came.shape[0] - at
    side = jnp.bitwise_and(position("tm") >> bit, 1)
    for i in range(slots // 2):
        pair = []
        for j in (2 * i, 2 * i + 1):
            piece = came[j * z.spec_rows : (j + 1) * z.spec_rows, :].astype(F32)
            pair.append(kept[j] + (piece + pltpu.roll(piece, LANES // 2, 1)))
        left[i] = jnp.where(side == 1, pair[1], pair[0])
        lines = slice(i * z.spec_rows, (i + 1) * z.spec_rows)
        message[lines, :] = halves(jnp.where(side == 1, pair[0], pair[1]))
    message[to : to + ends, :] = went[at:, :]
    message[to + ends :, :] = came[at:, :]


def merge(z, bit, kept, came, went):
    slots = kept.shape[0]
    ends = came.shape[0] - slots * z.spec_rows
    return pl.pallas_call(
        functools.partial(merge_kernel, z, bit),
        in_specs=[VMEM_SPEC] * 3,
        out_specs=[VMEM_SPEC] * 2,
        out_shape=[
            jax.ShapeDtypeStruct((slots // 2 * z.spec_rows + 2 * ends, LANES), BF),
            jax.ShapeDtypeStruct((slots // 2, z.spec_rows, LANES), F32),
        ],
        compiler_params=params(),
        name="merge",
    )(kept, came, went)


def cross_kernel(z, offsets, pairs, stacks, *refs):
    pieces, out = refs[:-1], refs[-1]
    here = position("sta")
    mine = pieces[0][...]
    bins = z.bins
    sides = []
    for i in range(z.stations):
        re, im = mine[2 * i : 2 * i + 1], mine[2 * i + 1 : 2 * i + 2]
        sides.append((jnp.concatenate([re, im], axis=0), jnp.concatenate([im, -re], axis=0)))
    for k, (offset, piece) in enumerate(zip(offsets, pieces)):
        on = jnp.concatenate([pairs[k]] * (bins // LANES), axis=1)
        for j in range(z.stations):
            re = jnp.broadcast_to(piece[2 * j : 2 * j + 1, :], (2, bins)) * on
            im = jnp.broadcast_to(piece[2 * j + 1 : 2 * j + 2, :], (2, bins)) * on
            column = (here ^ offset) * z.stations + j
            for i, (p, q) in enumerate(sides):
                out[i, column] = stacks[i, column] + (re * p + im * q)


def cross(z, offsets, pairs, stacks, pieces):
    return pl.pallas_call(
        functools.partial(cross_kernel, z, offsets),
        in_specs=[VMEM_SPEC] * (2 + len(pieces)),
        out_specs=VMEM_SPEC,
        out_shape=jax.ShapeDtypeStruct(stacks.shape, F32),
        compiler_params=params(),
        name="cross",
    )(pairs, stacks, *pieces)


def shards(traces, station_flags, tile_mask, band_block, stacks):
    tm_count, sta_count = lax.axis_size("tm"), lax.axis_size("sta")
    stations, length = traces.shape
    z = Sizes(stations, length, tm_count, stacks.shape[-1])
    assert sta_count & (sta_count - 1) == 0
    offsets = [0]
    bits = [1 << k for k in reversed(range(sta_count.bit_length() - 1))]
    for bit in bits:
        offsets += [offset ^ bit for offset in offsets]
    if tm_count in (4, 8, 16):
        message, home = split_transform(z, station_flags, traces)
        for k in range(tm_count.bit_length() - 1):
            swap = [(i, i ^ (1 << k)) for i in range(tm_count)]
            came, went = lax.ppermute(message, "tm", swap), message
            if k == 0:
                kept = home()
            if 2 << k < tm_count:
                message, kept = merge(z, k + 1, kept, came, went)
        *made, pairs = tables(z, offsets, z.lift, 1, band_block, station_flags, tile_mask)
        white = gathered(z, kept, came, went, made)
    else:
        sent = transform(z, station_flags, traces)
        got = lax.all_to_all(sent, "tm", split_axis=0, concat_axis=0, tiled=True)
        *made, pairs = tables(
            z, offsets, z.half, tm_count, band_block, station_flags, tile_mask
        )
        white = spectrum(z, got, made)
    pieces = [white]
    for bit in bits:
        swap = [(i, i ^ bit) for i in range(sta_count)]
        pieces += [lax.ppermute(piece, "sta", swap) for piece in pieces]
    return cross(z, offsets, pairs, stacks, pieces)


def solution(mesh):
    return jax.shard_map(
        shards,
        mesh=mesh,
        in_specs=(P("sta", "tm"), P("sta"), P(), P(), P("sta", None, None, "tm")),
        out_specs=P("sta", None, None, "tm"),
        check_vma=False,
    )
```

```python
import functools
import math

import jax
import jax.numpy as jnp
import numpy as np
from jax import lax
from jax.experimental import pallas as pl
from jax.experimental.pallas import tpu as pltpu
from jax.sharding import PartitionSpec as P

HALF_WIN = 512
SMOOTH = 32
EPS_MEAN = 1e-06
EPS_POWER = 1e-06
LANES = 128
SPAN = 2 * HALF_WIN
TILES = SPAN // LANES
HALF_TILES = HALF_WIN // LANES
PAD = 16
BAND_TOP = 137
WIDTH = 2 * LANES
CHUNKS = SPAN // WIDTH
position = lax.axis_index
VMEM_LIMIT = 16 * 1024 * 1024
BF = jnp.bfloat16
F32 = jnp.float32


def up_to(value, step):
    return -(-value // step) * step


def sincos(turns):
    quarter = jnp.round(turns * 4.0)
    rest = turns - quarter * 0.25
    y = rest * (2.0 * math.pi)
    y2 = y * y
    s = y + y * y2 * (-1.0 / 6 + y2 * (1.0 / 120 + y2 * (-1.0 / 5040 + y2 * (1.0 / 362880))))
    c = 1.0 + y2 * (-0.5 + y2 * (1.0 / 24 + y2 * (-1.0 / 720 + y2 * (1.0 / 40320))))
    q = quarter - 4.0 * jnp.floor(quarter * 0.25)
    swap = (q == 1.0) | (q == 3.0)
    sine = jnp.where(swap, c, s)
    cosine = jnp.where(swap, s, c)
    sine = jnp.where(q >= 2.0, -sine, sine)
    cosine = jnp.where((q == 1.0) | (q == 2.0), -cosine, cosine)
    return sine, cosine


def turns_of(product, period):
    whole = jnp.floor(product * (1.0 / period))
    return (product - whole * period) * (1.0 / period)


def split2(value):
    high = value.astype(BF)
    return high, (value - high.astype(F32)).astype(BF)


def iota(shape, axis):
    return lax.broadcasted_iota(jnp.int32, shape, axis)


def iota_f(shape, axis):
    return iota(shape, axis).astype(F32)


def window_tables():
    row, lane = iota((LANES, LANES), 0), iota((LANES, LANES), 1)
    upto = (row <= lane).astype(F32).astype(BF)
    onward = (row >= lane).astype(F32).astype(BF)
    return upto, onward, jnp.ones((LANES, LANES), BF)


def np_split(value):
    high = value.astype(jnp.bfloat16).astype(np.float64)
    return high, (value - high).astype(jnp.bfloat16).astype(np.float64)


class Sizes:
    def __init__(self, stations, length, tm_count, bins):
        self.stations, self.length, self.tm, self.bins = stations, length, tm_count, bins
        self.rows = length // SPAN
        self.half = self.rows // 2 + 1
        self.pad = up_to(self.rows, PAD)
        self.full = self.rows // PAD * PAD
        self.tail = self.rows - self.full
        self.depth = 3 * self.full + PAD
        self.block = min(tm_count, 16)
        self.blocks = tm_count // self.block
        self.folds = (BAND_TOP + bins - 1) // self.rows + 1
        self.lift = up_to(self.half, 2)
        self.spec_rows = up_to(2 * self.lift, 8)
        self.edge_rows = 2 * stations * TILES
        self.sent_rows = self.spec_rows + self.edge_rows
        assert length % SPAN == 0 and tm_count % self.block == 0
        assert stations == 2 and self.folds <= PAD
        assert self.rows >= 2 and 0 < 3 * self.tail <= 8 and self.depth <= LANES

    def parity_tables(self):
        residue = np.arange(self.tm).reshape(-1, 2).T[:, None, :]
        order = (residue + self.tm * np.arange(self.lift)[None, :, None]).reshape(2, -1)
        return self.first_of(order), self.turn_of(order)

    def row_order(self):
        j2 = np.arange(self.tm)[:, None] + self.tm * np.arange(self.half)[None, :]
        return j2.reshape(self.blocks, self.block, self.half).transpose(0, 2, 1).reshape(self.blocks, -1)

    def first_table(self):
        return self.first_of(self.row_order())

    def turn_table(self):
        return self.turn_of(self.row_order())

    def first_of(self, order):
        period = self.tm * self.rows
        angle = 2.0 * np.pi / period * (order[:, :, None] * np.arange(self.rows) % period)
        parts = np.concatenate([np.cos(angle), -np.sin(angle)], axis=1)
        full, rest = parts[..., : self.full], parts[..., self.full :]
        table = np.concatenate([full, full, full, rest, rest, rest], axis=2)
        return np.pad(table, ((0, 0), (0, 0), (0, LANES - table.shape[2]))).astype(np.float32)

    def low_lanes(self, lane):
        at = 3 * self.full
        third = (lane >= 2 * self.full) & (lane < at)
        return third | ((lane >= at + 2 * self.tail) & (lane < at + 3 * self.tail))

    def turn_of(self, order):
        order = order.reshape(order.shape[0], 1, -1, 1)
        time = np.arange(SPAN).reshape(CHUNKS, 1, WIDTH)
        angle = 2.0 * np.pi / (self.tm * self.length) * (order * time)
        return np.stack([np.cos(angle), -np.sin(angle)], axis=2).astype(np.float32)


def unpack(z, x, xs, edges):
    rows, top = z.rows, 8
    for a in range(rows):
        xs[:, top + a, :] = x[:, a * SPAN : (a + 1) * SPAN].astype(F32)
    for s in range(z.stations):
        for side, a in ((0, 0), (1, rows - 1)):
            for c in range(TILES):
                at = (side * z.stations + s) * TILES + c
                edges[at : at + 1, :] = xs[s, top + a : top + a + 1, c * LANES : (c + 1) * LANES]


def window(z, s, xs, sums):
    rows, pad, top = z.rows, z.pad, 8
    short = up_to(rows, 8)
    kernel = jnp.concatenate(window_tables()[:2], axis=1)
    group = 4
    for c0 in range(0, TILES, group):
        parts = [
            jnp.abs(xs[s, top : top + pad, c * LANES : (c + 1) * LANES])
            for c in range(c0, c0 + group)
        ]
        part = jnp.concatenate([part.astype(BF) for part in parts], axis=0)
        got = jnp.dot(part, kernel, preferred_element_type=F32)
        for k in range(group):
            value = got[k * pad : k * pad + short]
            upto, onward = value[:, :LANES], value[:, LANES:]
            sums[s, c0 + k, top : top + short, 0 : 2 * LANES] = value
            sums[s, c0 + k, top : top + short, 2 * LANES :] = upto + (onward - parts[k][:short])
    blank = jnp.zeros((1, HALF_WIN), F32)
    xs[s, top : top + 1, 0:HALF_WIN] = blank
    xs[s, top + rows - 1 : top + rows, HALF_WIN:SPAN] = blank


def level(z, s, tiles, xs, sums, stack):
    rows, top = z.rows, 8
    skip = z.tail == 1 and tiles[0] >= HALF_TILES
    short = z.full if skip else up_to(rows, 8)

    def tile(kind, c):
        turn, cc = divmod(c, TILES)
        lines = slice(top + turn, top + turn + short)
        return sums[s, cc, lines, kind * LANES : (kind + 1) * LANES]

    first = tiles[0] + 1 - HALF_TILES
    single = [tile(2, c) for c in range(first, tiles[-1] + HALF_TILES)]
    twos = [single[c] + single[c + 1] for c in range(len(single) - 1)]
    for k, c in enumerate(tiles):
        inner = (twos[k] + twos[k + 2]) + (twos[k + 4] + single[k + 6])
        total = inner + (tile(1, c - HALF_TILES) + tile(0, c + HALF_TILES))
        value = xs[s, top : top + short, c * LANES : (c + 1) * LANES]
        value = value / (total * (1.0 / (2 * HALF_WIN + 1)) + EPS_MEAN)
        high, low = split2(value[: z.full])
        lanes = slice(c * LANES, (c + 1) * LANES)
        for k2, part in enumerate((high, low, high)):
            stack[s, k2 * z.full : (k2 + 1) * z.full, lanes] = part
        if skip:
            stack[s, 3 * z.full :, lanes] = jnp.zeros((PAD, LANES), BF)
            continue
        rest = value[z.full :]
        high = rest.astype(BF).astype(F32)
        rest = high + pltpu.roll(rest - high, z.tail, 0) + pltpu.roll(high, 2 * z.tail, 0)
        rest = jnp.concatenate([rest, jnp.zeros((PAD - rest.shape[0], LANES), F32)], axis=0)
        stack[s, 3 * z.full :, lanes] = rest.astype(BF)


def fold_weights(weight):
    lane = iota((PAD, SPAN), 1)
    for kind in range(2):
        turns = jnp.bitwise_and((iota((PAD, SPAN), 0) + kind) * lane, SPAN - 1).astype(F32)
        sine, cosine = sincos(turns * (1.0 / SPAN))
        for h, (s, c) in enumerate(zip(split2(sine), split2(cosine))):
            table = ((c, s), (-s, c)) if kind == 0 else ((c, -s), (-s, -c))
            for part in range(2):
                at = h * 4 * PAD + kind * 2 * PAD + part * PAD
                for side in range(2):
                    for g in range(CHUNKS):
                        to = (2 * g + side) * WIDTH
                        weight[at : at + PAD, to : to + WIDTH] = table[part][side][
                            :, g * WIDTH : (g + 1) * WIDTH
                        ]


def transform_kernel(
    z, flags, x, first, turn, out,
    flags_s, x_v, first_v, turn_v, table, xs, sums, stack, edges, weight, acc, both, spec, sems,
):
    half, block, tm = z.half, z.block, z.tm
    height = half * block
    index = pl.program_id(0)
    top, rows, pad = 8, z.rows, z.pad
    get_first = pltpu.make_async_copy(first.at[index], first_v, sems.at[2])
    get_turn = [
        pltpu.make_async_copy(turn.at[index, g], turn_v.at[g], sems.at[3 + g]) for g in range(CHUNKS)
    ]

    def prologue():
        copies = [
            pltpu.make_async_copy(x, x_v, sems.at[0]),
            pltpu.make_async_copy(flags, flags_s, sems.at[1]),
        ]
        for copy in copies + [get_first] + get_turn:
            copy.start()
        full = rows // 8 * 8
        for s in range(z.stations):
            xs[s, top + full : top + pad, :] = jnp.zeros((pad - full, SPAN), F32)
            for c in range(TILES):
                sums[s, c, 0:top, :] = jnp.zeros((top, 3 * LANES), F32)
                sums[s, c, top + up_to(rows, 8) :, :] = jnp.zeros((8, 3 * LANES), F32)
        spec[:, z.spec_rows - 8 : z.spec_rows, :] = jnp.zeros((tm, 8, LANES), F32)
        fold_weights(weight)
        for copy in copies:
            copy.wait()
        unpack(z, x_v, xs, edges)
        for s in range(z.stations):
            window(z, s, xs, sums)
            if s == 0 or z.blocks > 1:
                level(z, s, range(TILES), xs, sums, stack)

    if z.blocks == 1:
        prologue()
    else:
        pl.when(index == 0)(prologue)

        @pl.when(index > 0)
        def _():
            for copy in [get_first] + get_turn:
                copy.start()

    for copy in [get_first] + get_turn:
        copy.wait()
    residue = index * block + iota((block, LANES), 0)
    sine, cosine = sincos(turns_of((position("tm") * residue).astype(F32), tm))
    f_re = first_v[:height].reshape(half, block, LANES)
    f_im = first_v[height:].reshape(half, block, LANES)
    low = z.low_lanes(iota((height, LANES), 1))
    for k, value in enumerate(
        (f_re * cosine[None] + f_im * sine[None], f_im * cosine[None] - f_re * sine[None])
    ):
        value = value.reshape(height, LANES)
        high = value.astype(BF).astype(F32)
        table[k * height : (k + 1) * height, :] = jnp.where(low, value - high, high).astype(BF)

    def first_stage(s, g):
        return jnp.dot(
            table[:, : z.depth],
            stack[s, :, g * WIDTH : (g + 1) * WIDTH],
            preferred_element_type=F32,
        )

    def second_stage(s, g, parts):
        w = weight[:, 2 * g * WIDTH : 2 * (g + 1) * WIDTH]
        got = lax.dot_general(parts, w, (((1,), (1,)), ((), ())), preferred_element_type=F32)
        value = got[:height] + got[height:]
        acc[s] = value if g == 0 else acc[s] + value

    def settle(s):
        value = acc[s] + pltpu.roll(acc[s], LANES // 2, 1)
        return value * flags_s[s].astype(F32)

    steps = [(s, g) for s in range(z.stations) for g in range(CHUNKS)]
    coming = first_stage(*steps[0])
    waiting = None
    for k, (s, g) in enumerate(steps):
        f_re, f_im = coming[:height], coming[height:]
        t_re, t_im = turn_v[g, 0], turn_v[g, 1]
        re_h, re_l = split2(f_re * t_re - f_im * t_im)
        im_h, im_l = split2(f_re * t_im + f_im * t_re)
        parts = jnp.concatenate(
            [jnp.concatenate([re_h, im_h], axis=1), jnp.concatenate([re_l, im_l], axis=1)], axis=0
        )
        if s == 0 and z.blocks == 1:
            level(z, 1, range(2 * g, 2 * g + 2), xs, sums, stack)
        if k + 1 < len(steps):
            coming = first_stage(*steps[k + 1])
        if waiting is not None:
            second_stage(*steps[k - 1], waiting)
        waiting = parts
    second_stage(*steps[-1], waiting)
    zero, one = settle(0), settle(1)
    lane = iota((height, LANES), 1)
    early = jnp.bitwise_and(lane, LANES // 2 - 1) < LANES // 4
    direct = jnp.where(early, zero, pltpu.roll(one, LANES // 4, 1))
    mirror = jnp.where(early, pltpu.roll(zero, LANES // 4, 1), one)
    for kind, value in enumerate((direct, mirror)):
        high = value.astype(BF).astype(F32)
        both[kind] = jnp.where(lane < LANES // 2, high, value - high)
    for k in range(block):
        here = index * block + k
        there = jnp.where(here == 0, 0, tm - here) if z.blocks > 1 else (tm - k) % tm
        here = here if z.blocks > 1 else k
        lines = pl.ds(k, half, stride=block)
        spec[here, 0:half, :] = both[0, lines, :]
        spec[there, half : 2 * half, :] = both[1, lines, :]

    def finish():
        ends = edges[...].astype(BF)

        def one_row(k, carry):
            out[k, 0 : z.spec_rows, :] = spec[k].astype(BF)
            out[k, z.spec_rows : z.sent_rows, :] = ends
            return carry

        if z.blocks == 1:
            for k in range(tm):
                one_row(k, 0)
        else:
            lax.fori_loop(0, tm, one_row, 0)

    if z.blocks == 1:
        finish()
    else:
        pl.when(index == z.blocks - 1)(finish)


SMEM_SPEC = pl.BlockSpec(memory_space=pltpu.SMEM)
VMEM_SPEC = pl.BlockSpec(memory_space=pltpu.VMEM)
HBM_SPEC = pl.BlockSpec(memory_space=pltpu.HBM)


def params():
    return pltpu.CompilerParams(vmem_limit_bytes=VMEM_LIMIT)


def transform(z, flags, x):
    height = z.half * z.block
    first, turn = z.first_table(), z.turn_table()
    return pl.pallas_call(
        functools.partial(transform_kernel, z),
        grid=(z.blocks,),
        in_specs=[HBM_SPEC] * 4,
        out_specs=VMEM_SPEC,
        out_shape=jax.ShapeDtypeStruct((z.tm, z.sent_rows, LANES), BF),
        scratch_shapes=[
            pltpu.SMEM((z.stations,), jnp.int32),
            pltpu.VMEM(x.shape, BF),
            pltpu.VMEM(first.shape[1:], F32),
            pltpu.VMEM(turn.shape[1:], F32),
            pltpu.VMEM(first.shape[1:], BF),
            pltpu.VMEM((z.stations, 8 + z.pad, SPAN), F32),
            pltpu.VMEM((z.stations, TILES, 16 + up_to(z.rows, 8), 3 * LANES), F32),
            pltpu.VMEM((z.stations, z.depth, SPAN), BF),
            pltpu.VMEM((z.edge_rows, LANES), F32),
            pltpu.VMEM((LANES, 2 * SPAN), BF),
            pltpu.VMEM((z.stations, height, LANES), F32),
            pltpu.VMEM((2, height, LANES), F32),
            pltpu.VMEM((z.tm, z.spec_rows, LANES), F32),
            pltpu.SemaphoreType.DMA((3 + CHUNKS,)),
        ],
        name="transform",
    )(flags, x, jnp.asarray(first), jnp.asarray(turn))


def table_kernel(
    z, offsets, split, band, flags, mask, choose, keep, steps, turns, near, phase, switch, pairs,
    band_s, flags_s, mask_s, sems,
):
    rows, tm, bins, half = z.rows, z.tm, z.bins, z.half
    copies = [
        pltpu.make_async_copy(band, band_s, sems.at[0]),
        pltpu.make_async_copy(flags, flags_s, sems.at[1]),
        pltpu.make_async_copy(mask, mask_s, sems.at[2]),
    ]
    for copy in copies:
        copy.start()
    for copy in copies:
        copy.wait()
    here = position("sta")
    for k, offset in enumerate(offsets):
        pairs[k] = jnp.full((2, LANES), mask_s[here, here ^ offset].astype(F32))
    base, residue = band_s[0, 0], position("tm")
    for s in range(z.stations):
        switch[s] = jnp.full((TILES, LANES), flags_s[s].astype(F32))
    spot = iota_f((1, bins), 1) + base.astype(F32)
    fold = jnp.floor((spot + 0.5) * (1.0 / rows))
    rest = spot - fold * rows
    row = iota_f((z.spec_rows, bins), 0)
    last = (rows - 1 + split + (residue == 0).astype(jnp.int32)).astype(F32)
    mirror = jnp.where((row >= split) & (last - row >= half), last - row, -1.0)
    one = (jnp.where(row < half, row, mirror) == rest).astype(F32).astype(BF)
    for p in range(choose.shape[0]):
        choose[p] = one
    keep[...] = (iota_f((PAD, bins), 0) == fold).astype(F32)
    freq = (residue + tm * (base + iota((1, bins), 1))).astype(F32)
    step = iota_f((TILES, bins), 0) - HALF_TILES
    sine, cosine = sincos(turns_of(step * freq, tm * (z.length // LANES)))
    table = jnp.concatenate(
        [jnp.concatenate([cosine, -sine], axis=1), jnp.concatenate([sine, cosine], axis=1)], axis=0
    )
    high, low = split2(table)
    for k, part in enumerate((high, high, low, low)):
        steps[k * 2 * TILES : (k + 1) * 2 * TILES, :] = part
    sine, cosine = sincos(turns_of(iota_f((LANES, bins), 0) * freq, tm * z.length))
    turns[0] = cosine
    turns[1] = sine
    gap = jnp.abs(iota((bins, bins), 0) - iota((bins, bins), 1))
    near[...] = (gap <= SMOOTH).astype(F32).astype(BF)
    p_sin, p_cos = sincos(turns_of((residue * iota((tm, LANES), 0)).astype(F32), tm))
    phase[0] = p_cos
    phase[1] = -p_sin


def tables(z, offsets, split, copies, band, flags, mask):
    return pl.pallas_call(
        functools.partial(table_kernel, z, offsets, split),
        in_specs=[HBM_SPEC] * 3,
        out_specs=[VMEM_SPEC] * 8,
        scratch_shapes=[
            pltpu.SMEM((1, 1), jnp.int32),
            pltpu.SMEM((z.stations,), jnp.int32),
            pltpu.SMEM(mask.shape, jnp.int32),
            pltpu.SemaphoreType.DMA((3,)),
        ],
        out_shape=[
            jax.ShapeDtypeStruct((copies, z.spec_rows, z.bins), BF),
            jax.ShapeDtypeStruct((PAD, z.bins), F32),
            jax.ShapeDtypeStruct((8 * TILES, 2 * z.bins), BF),
            jax.ShapeDtypeStruct((2, LANES, z.bins), F32),
            jax.ShapeDtypeStruct((z.bins, z.bins), BF),
            jax.ShapeDtypeStruct((2, z.tm, LANES), F32),
            jax.ShapeDtypeStruct((z.stations, TILES, LANES), F32),
            jax.ShapeDtypeStruct((len(offsets), 2, LANES), F32),
        ],
        compiler_params=params(),
        cost_estimate=pl.CostEstimate(flops=4000000, bytes_accessed=2000000, transcendentals=0),
        name="tables",
    )(band.reshape(1, 1), flags, mask)


def sublane_sums(value, row):
    total = value
    for shift in (1, 2, 4):
        total = total + jnp.where(row >= shift, pltpu.roll(total, shift, 0), 0.0)
    return total - value, total


def spectrum_kernel(z, got, choose, keep, steps, turns, near, phase, switch, out):
    tm, bins, at = z.tm, z.bins, z.spec_rows
    parts = got[:, 0:at, :].astype(F32).reshape(tm * at, LANES).astype(BF)
    weights = choose[...].astype(F32).reshape(tm * at, bins).astype(BF)
    placed = lax.dot_general(parts, weights, (((0,), (0,)), ((), ())), preferred_element_type=F32)
    side_rows = z.stations * TILES
    ends = [
        got[:, at + k * side_rows : at + (k + 1) * side_rows, :].astype(F32).reshape(-1, LANES)
        for k in range(2)
    ]
    whiten(z, placed, ends, keep, steps, turns, near, phase, switch, out)


def gathered_kernel(
    z, kept, came, went, choose, keep, steps, turns, near, phase, switch, out, ends
):
    tm = z.tm
    piece = came[0 : z.spec_rows, :].astype(F32)
    total = kept[0] + (piece + pltpu.roll(piece, LANES // 2, 1))
    placed = lax.dot_general(
        halves(total), choose[0], (((0,), (0,)), ((), ())), preferred_element_type=F32
    )
    here = position("tm")
    for s in range(tm):
        source, slot = (went, s) if s < tm // 2 else (came, s - tm // 2)
        at = z.spec_rows + slot * z.edge_rows
        ends[here ^ s] = source[at : at + z.edge_rows, :].astype(F32)
    side_rows = z.stations * TILES
    sides = [ends[:, k * side_rows : (k + 1) * side_rows, :].reshape(-1, LANES) for k in range(2)]
    whiten(z, placed, sides, keep, steps, turns, near, phase, switch, out)


def halves(value):
    high = value.astype(BF).astype(F32)
    return jnp.where(iota(value.shape, 1) < LANES // 2, high, value - high).astype(BF)


def whiten(z, placed, ends, keep, steps, turns, near, phase, switch, out):
    tm, bins = z.tm, z.bins
    mask = keep[...]
    folded = [
        jnp.sum(placed[k * PAD : (k + 1) * PAD] * mask, axis=0, keepdims=True)
        for k in range(4 * z.stations)
    ]
    spec = [folded[k] + folded[k + 2 * z.stations] for k in range(2 * z.stations)]
    upto, onward, ones = window_tables()
    row = iota((TILES, LANES), 0)
    late = row >= HALF_TILES
    sides = []
    for value, table in zip(ends, (upto, onward)):
        sums = jnp.dot(
            jnp.abs(value).astype(BF),
            jnp.concatenate([table, ones], axis=1),
            preferred_element_type=F32,
        )
        sides.append((value, sums))
    mixed = []
    for s in range(z.stations):
        real = jnp.zeros((TILES, LANES), F32)
        imag = jnp.zeros((TILES, LANES), F32)
        flag = switch[s]
        for p in range(tm):
            begin = (p * z.stations + s) * TILES
            before = ((p - 1) % tm * z.stations + s) * TILES
            value_r, sums_r = (v[begin : begin + TILES] for v in sides[0])
            value_l, sums_l = (v[before : before + TILES] for v in sides[1])
            earlier, _ = sublane_sums(sums_r[:, LANES:], row)
            right = sums_r[:, :LANES] + earlier
            tail = sums_l[:, LANES:]
            for shift in (1, 2, 4):
                tail = tail + jnp.where(row < TILES - shift, pltpu.roll(tail, TILES - shift, 0), 0.0)
            left = sums_l[:, :LANES] + jnp.where(
                row < TILES - 1, pltpu.roll(tail, TILES - 1, 0), 0.0
            )
            total = left + right if p else jnp.where(late, right, left)
            sample = pltpu.roll(jnp.where(late, value_l, value_r), HALF_TILES, 0)
            value = flag * sample / (total * (1.0 / (2 * HALF_WIN + 1)) + EPS_MEAN)
            real = real + value * phase[0, p : p + 1, :]
            imag = imag + value * phase[1, p : p + 1, :]
        mixed.append(jnp.concatenate([real, imag], axis=0))
    high, low = split2(jnp.concatenate(mixed, axis=1))
    spread = lax.dot_general(
        jnp.concatenate([high, low, high, low], axis=0),
        steps[...],
        (((0,), (0,)), ((), ())),
        preferred_element_type=F32,
    )
    cosine, sine = turns[0], turns[1]
    pieces = []
    for s in range(z.stations):
        g_re = spread[s * LANES : (s + 1) * LANES, :bins]
        g_im = spread[s * LANES : (s + 1) * LANES, bins:]
        spec[2 * s] += jnp.sum(g_re * cosine + g_im * sine, axis=0, keepdims=True)
        spec[2 * s + 1] += jnp.sum(g_im * cosine - g_re * sine, axis=0, keepdims=True)
        power = spec[2 * s] * spec[2 * s] + spec[2 * s + 1] * spec[2 * s + 1]
        for _ in range(3):
            part = power.astype(BF).astype(F32)
            pieces.append(part)
            power = power - part
    pieces.append(jnp.zeros((8 - len(pieces), bins), F32))
    smooth = jnp.dot(
        jnp.concatenate(pieces, axis=0).astype(BF), near[...], preferred_element_type=F32
    )
    for s in range(z.stations):
        mean = smooth[3 * s : 3 * s + 1] + smooth[3 * s + 1 : 3 * s + 2] + smooth[3 * s + 2 : 3 * s + 3]
        scale = lax.rsqrt(mean * (1.0 / (2 * SMOOTH + 1)) + EPS_POWER)
        out[2 * s : 2 * s + 1, :] = spec[2 * s] * scale
        out[2 * s + 1 : 2 * s + 2, :] = spec[2 * s + 1] * scale


def spectrum(z, got, made):
    return pl.pallas_call(
        functools.partial(spectrum_kernel, z),
        in_specs=[VMEM_SPEC] * 8,
        out_specs=VMEM_SPEC,
        out_shape=jax.ShapeDtypeStruct((2 * z.stations, z.bins), F32),
        compiler_params=params(),
        name="spectrum",
    )(got, *made)


def gathered(z, kept, came, went, made):
    return pl.pallas_call(
        functools.partial(gathered_kernel, z),
        in_specs=[VMEM_SPEC] * 10,
        out_specs=VMEM_SPEC,
        out_shape=jax.ShapeDtypeStruct((2 * z.stations, z.bins), F32),
        scratch_shapes=[pltpu.VMEM((z.tm, z.edge_rows, LANES), F32)],
        compiler_params=params(),
        name="spectrum",
    )(kept, came, went, *made)


def half_transform(z, parity, table, turn, stack, weight, flags, acc, both, spec, before):
    count, lift = z.tm // 2, z.lift
    height = lift * count

    def first_stage(s, g):
        return jnp.dot(
            table[:, : z.depth],
            stack[s, :, g * WIDTH : (g + 1) * WIDTH],
            preferred_element_type=F32,
        )

    def second_stage(s, g, parts):
        w = weight[:, 2 * g * WIDTH : 2 * (g + 1) * WIDTH]
        got = lax.dot_general(parts, w, (((1,), (1,)), ((), ())), preferred_element_type=F32)
        value = got[:height] + got[height:]
        acc[s] = value if g == 0 else acc[s] + value

    def settle(s):
        return (acc[s] + pltpu.roll(acc[s], LANES // 2, 1)) * flags[s, 0:1, :]

    steps = [(s, g) for s in range(z.stations) for g in range(CHUNKS)]
    coming = first_stage(*steps[0])
    waiting = None
    for k, (s, g) in enumerate(steps):
        f_re, f_im = coming[:height], coming[height:]
        t_re, t_im = turn[g, 0], turn[g, 1]
        re_h, re_l = split2(f_re * t_re - f_im * t_im)
        im_h, im_l = split2(f_re * t_im + f_im * t_re)
        parts = jnp.concatenate(
            [jnp.concatenate([re_h, im_h], axis=1), jnp.concatenate([re_l, im_l], axis=1)], axis=0
        )
        if before is not None and s == 0:
            before(g)
        if k + 1 < len(steps):
            coming = first_stage(*steps[k + 1])
        if waiting is not None:
            second_stage(*steps[k - 1], waiting)
        waiting = parts
    second_stage(*steps[-1], waiting)
    zero, one = settle(0), settle(1)
    lane = iota((height, LANES), 1)
    early = jnp.bitwise_and(lane, LANES // 2 - 1) < LANES // 4
    both[0] = jnp.where(early, zero, pltpu.roll(one, LANES // 4, 1))
    both[1] = jnp.where(early, pltpu.roll(zero, LANES // 4, 1), one)
    for j in range(count):
        lines = pl.ds(j, lift, stride=count)
        spec[j, 0:lift, :] = both[0, lines, :]
        spec[lax.rem(2 * count - parity - j, count), lift : 2 * lift, :] = both[1, lines, :]


def stretch_table(z, parity, first, table):
    count, height = z.tm // 2, z.lift * (z.tm // 2)
    low = z.low_lanes(iota((height, LANES), 1))
    residue = 2 * iota((count, LANES), 0) + parity
    sine, cosine = sincos(turns_of((position("tm") * residue).astype(F32), z.tm))
    f_re = first[:height].reshape(z.lift, count, LANES)
    f_im = first[height:].reshape(z.lift, count, LANES)
    for k, value in enumerate(
        (f_re * cosine[None] + f_im * sine[None], f_im * cosine[None] - f_re * sine[None])
    ):
        value = value.reshape(height, LANES)
        high = value.astype(BF).astype(F32)
        table[k * height : (k + 1) * height, :] = jnp.where(low, value - high, high).astype(BF)


def away_kernel(
    z, flags, x, first, turn, message, stack, weight, home_first, home_turn, switch,
    flags_s, x_v, first_v, turn_v, table, xs, sums, edges, acc, both, spec, sems,
):
    rows, pad, top = z.rows, z.pad, 8
    count = z.tm // 2
    here = position("tm")
    home = jnp.bitwise_and(here, 1)
    away = 1 - home
    copies = [
        pltpu.make_async_copy(x, x_v, sems.at[0]),
        pltpu.make_async_copy(flags, flags_s, sems.at[1]),
        pltpu.make_async_copy(first.at[away], first_v, sems.at[2]),
        pltpu.make_async_copy(turn.at[away], turn_v, sems.at[3]),
        pltpu.make_async_copy(turn.at[home], home_turn, sems.at[4]),
        pltpu.make_async_copy(first.at[home], home_first, sems.at[5]),
    ]
    for copy in copies:
        copy.start()
    full = rows // 8 * 8
    for s in range(z.stations):
        xs[s, top + full : top + pad, :] = jnp.zeros((pad - full, SPAN), F32)
        for c in range(TILES):
            sums[s, c, 0:top, :] = jnp.zeros((top, 3 * LANES), F32)
            sums[s, c, top + up_to(rows, 8) :, :] = jnp.zeros((8, 3 * LANES), F32)
    spec[:, z.spec_rows - 8 : z.spec_rows, :] = jnp.zeros((count, 8, LANES), F32)
    fold_weights(weight)
    copies[0].wait()
    copies[1].wait()
    unpack(z, x_v, xs, edges)
    for s in range(z.stations):
        window(z, s, xs, sums)
        switch[s] = jnp.full((TILES, LANES), flags_s[s].astype(F32))
    for g in range(0, TILES, HALF_TILES):
        level(z, 0, range(g, g + HALF_TILES), xs, sums, stack)
    copies[2].wait()
    copies[3].wait()
    stretch_table(z, away, first_v, table)
    half_transform(
        z, away, table, turn_v, stack, weight, switch, acc, both, spec,
        lambda g: level(z, 1, range(2 * g, 2 * g + 2), xs, sums, stack),
    )
    copies[4].wait()
    copies[5].wait()
    for j in range(count):
        message[j * z.spec_rows : (j + 1) * z.spec_rows, :] = halves(spec[j])
    message[count * z.spec_rows :, :] = edges[...].astype(BF)


def home_kernel(z, stack, weight, first, turn, switch, kept, table, acc, both):
    kept[:, z.spec_rows - 8 : z.spec_rows, :] = jnp.zeros((z.tm // 2, 8, LANES), F32)
    parity = jnp.bitwise_and(position("tm"), 1)
    stretch_table(z, parity, first, table)
    half_transform(z, parity, table, turn, stack, weight, switch, acc, both, kept, None)


def split_transform(z, flags, x):
    count, height = z.tm // 2, z.lift * (z.tm // 2)
    first, turn = z.parity_tables()
    state = [
        jax.ShapeDtypeStruct((z.stations, z.depth, SPAN), BF),
        jax.ShapeDtypeStruct((LANES, 2 * SPAN), BF),
        jax.ShapeDtypeStruct(first.shape[1:], F32),
        jax.ShapeDtypeStruct(turn.shape[1:], F32),
        jax.ShapeDtypeStruct((z.stations, TILES, LANES), F32),
    ]
    inputs = [flags, x, jnp.asarray(first), jnp.asarray(turn)]
    work = [
        pltpu.VMEM((z.stations, height, LANES), F32),
        pltpu.VMEM((2, height, LANES), F32),
    ]
    message, *state = pl.pallas_call(
        functools.partial(away_kernel, z),
        in_specs=[HBM_SPEC] * 4,
        out_specs=[VMEM_SPEC] * 6,
        out_shape=[jax.ShapeDtypeStruct((count * z.spec_rows + z.edge_rows, LANES), BF)] + state,
        scratch_shapes=[
            pltpu.SMEM((z.stations,), jnp.int32),
            pltpu.VMEM(x.shape, BF),
            pltpu.VMEM(first.shape[1:], F32),
            pltpu.VMEM(turn.shape[1:], F32),
            pltpu.VMEM(first.shape[1:], BF),
            pltpu.VMEM((z.stations, 8 + z.pad, SPAN), F32),
            pltpu.VMEM((z.stations, TILES, 16 + up_to(z.rows, 8), 3 * LANES), F32),
            pltpu.VMEM((z.edge_rows, LANES), F32),
            *work,
            pltpu.VMEM((count, z.spec_rows, LANES), F32),
            pltpu.SemaphoreType.DMA((6,)),
        ],
        compiler_params=params(),
        name="away",
    )(*(in_hbm(value) for value in inputs))

    def home():
        return pl.pallas_call(
            functools.partial(home_kernel, z),
            in_specs=[VMEM_SPEC] * 5,
            out_specs=VMEM_SPEC,
            out_shape=jax.ShapeDtypeStruct((count, z.spec_rows, LANES), F32),
            scratch_shapes=[pltpu.VMEM(first.shape[1:], BF), *work],
            compiler_params=params(),
            cost_estimate=pl.CostEstimate(flops=10**9, bytes_accessed=10**6, transcendentals=0),
            name="home",
        )(*state)

    return message, home


def in_hbm(value):
    return pltpu.with_memory_space_constraint(value, pltpu.HBM)


def merge_kernel(z, bit, kept, came, went, message, left):
    slots = kept.shape[0]
    at, to = slots * z.spec_rows, slots // 2 * z.spec_rows
    ends = came.shape[0] - at
    side = jnp.bitwise_and(position("tm") >> bit, 1)
    for i in range(slots // 2):
        pair = []
        for j in (2 * i, 2 * i + 1):
            piece = came[j * z.spec_rows : (j + 1) * z.spec_rows, :].astype(F32)
            pair.append(kept[j] + (piece + pltpu.roll(piece, LANES // 2, 1)))
        left[i] = jnp.where(side == 1, pair[1], pair[0])
        lines = slice(i * z.spec_rows, (i + 1) * z.spec_rows)
        message[lines, :] = halves(jnp.where(side == 1, pair[0], pair[1]))
    message[to : to + ends, :] = went[at:, :]
    message[to + ends :, :] = came[at:, :]


def merge(z, bit, kept, came, went):
    slots = kept.shape[0]
    ends = came.shape[0] - slots * z.spec_rows
    return pl.pallas_call(
        functools.partial(merge_kernel, z, bit),
        in_specs=[VMEM_SPEC] * 3,
        out_specs=[VMEM_SPEC] * 2,
        out_shape=[
            jax.ShapeDtypeStruct((slots // 2 * z.spec_rows + 2 * ends, LANES), BF),
            jax.ShapeDtypeStruct((slots // 2, z.spec_rows, LANES), F32),
        ],
        compiler_params=params(),
        name="merge",
    )(kept, came, went)


def cross_kernel(z, offsets, pairs, stacks, *refs):
    pieces, out = refs[:-1], refs[-1]
    here = position("sta")
    mine = pieces[0][...]
    bins = z.bins
    sides = []
    for i in range(z.stations):
        re, im = mine[2 * i : 2 * i + 1], mine[2 * i + 1 : 2 * i + 2]
        sides.append((jnp.concatenate([re, im], axis=0), jnp.concatenate([im, -re], axis=0)))
    for k, (offset, piece) in enumerate(zip(offsets, pieces)):
        on = jnp.concatenate([pairs[k]] * (bins // LANES), axis=1)
        for j in range(z.stations):
            re = jnp.broadcast_to(piece[2 * j : 2 * j + 1, :], (2, bins)) * on
            im = jnp.broadcast_to(piece[2 * j + 1 : 2 * j + 2, :], (2, bins)) * on
            column = (here ^ offset) * z.stations + j
            for i, (p, q) in enumerate(sides):
                out[i, column] = stacks[i, column] + (re * p + im * q)


def cross(z, offsets, pairs, stacks, pieces):
    return pl.pallas_call(
        functools.partial(cross_kernel, z, offsets),
        in_specs=[VMEM_SPEC] * (2 + len(pieces)),
        out_specs=VMEM_SPEC,
        out_shape=jax.ShapeDtypeStruct(stacks.shape, F32),
        compiler_params=params(),
        name="cross",
    )(pairs, stacks, *pieces)


def shards(traces, station_flags, tile_mask, band_block, stacks):
    tm_count, sta_count = lax.axis_size("tm"), lax.axis_size("sta")
    stations, length = traces.shape
    z = Sizes(stations, length, tm_count, stacks.shape[-1])
    assert sta_count & (sta_count - 1) == 0
    offsets = [0]
    bits = [1 << k for k in reversed(range(sta_count.bit_length() - 1))]
    for bit in bits:
        offsets += [offset ^ bit for offset in offsets]
    if tm_count in (4, 8, 16):
        message, home = split_transform(z, station_flags, traces)
        for k in range(tm_count.bit_length() - 1):
            swap = [(i, i ^ (1 << k)) for i in range(tm_count)]
            came, went = lax.ppermute(message, "tm", swap), message
            if k == 0:
                kept = home()
            if 2 << k < tm_count:
                message, kept = merge(z, k + 1, kept, came, went)
        *made, pairs = tables(z, offsets, z.lift, 1, band_block, station_flags, tile_mask)
        white = gathered(z, kept, came, went, made)
    else:
        sent = transform(z, station_flags, traces)
        got = lax.all_to_all(sent, "tm", split_axis=0, concat_axis=0, tiled=True)
        *made, pairs = tables(
            z, offsets, z.half, tm_count, band_block, station_flags, tile_mask
        )
        white = spectrum(z, got, made)
    pieces = [white]
    for bit in bits:
        swap = [(i, i ^ bit) for i in range(sta_count)]
        pieces += [lax.ppermute(piece, "sta", swap) for piece in pieces]
    return cross(z, offsets, pairs, stacks, pieces)


def solution(mesh):
    return jax.shard_map(
        shards,
        mesh=mesh,
        in_specs=(P("sta", "tm"), P("sta"), P(), P(), P("sta", None, None, "tm")),
        out_specs=P("sta", None, None, "tm"),
        check_vma=False,
    )
```
